256 devices in a mesh: leaf: 128 (over x, y, z), vec: 2 (over core).
Axes of the slice: x: 4, y: 4, z: 8, core: 2. Of those that a mesh axis runs over, the one named last changes fastest.
Arguments:
- points: bfloat16 [3, 1048576], P(None, 'leaf'), may hold values from -4 to 4
- vectors: bfloat16 [16, 1048576], P('vec', 'leaf'), may hold values from -6 to 6
- leaf_order: int32 [128, 8192], P('leaf'), may hold values from 0 to 8191, each once within a row
- leaf_bases: bfloat16 [2048, 64, 512], P('leaf'), may hold values from -0.25 to 0.25
- transfers: bfloat16 [3840, 64, 64], P('leaf'), may hold values from -0.5 to 0.5
- coupling_blocks: bfloat16 [32768, 64, 64], P('leaf'), may hold values from -0.75 to 0.75
- block_source: int32 [32768], P('leaf'), may hold values from 0 to 30, as said below
- block_owner: int32 [32768, 1], P('leaf'), may hold values from 0 to 127; in each aligned block of 256 rows (0 to 255, 256 to 511, ...) at most 4 rows name the same one
- block_target: int32 [32768], P('leaf'), may hold values from 0 to 30, as said below
- up_transfer: bfloat16 [254, 64, 64], replicated, may hold values from -0.5 to 0.5
- up_coupling: bfloat16 [254, 64, 64], replicated, as said below
Outputs:
- product: bfloat16 [16, 1048576], P('vec', 'leaf')
The draws below stay inside these ranges and needn't reach their ends.
Inputs may be any that keep to these rules, and one draw needn't show every extreme that they name: `leaf_order`: within each row, each point of the device once. `block_source`: A cluster of the subtree of the device that stores the block, numbered leaves first and level by level up to the root. `block_target`: A cluster of the subtree of the device block_owner names, in the same numbering, on the same level as the block's source cluster. `block_owner`: of the 256 blocks stored on one device, at most 4 name the same device, and exactly 4 name some device; every device is named by some block. `up_coupling`: coupling matrices of sibling clusters of the upper tree, finite.
All inputs are finite; a program needn't handle non-finite values.
Results may differ from the reference program's by a relative error of at most 0.0065.
Values may be sent and summed in bfloat16 or wider, within the bound.
No kernel may reach another device: no remote copies, remote signals or barrier semaphores. Data moves between devices by JAX's collectives and lax.ppermute only.
A program may use at most 128 MiB of HBM per device.

```python
import math
import jax
import jax.numpy as jnp
import numpy as np
from jax import lax

K = 64
LEAF = 512
NV = 16
NEAR = 2
LEAF_DEV = 16
LEAVES = 2048
NPTS = 1048576
NCL = 31
NTR = 30
NBLK = 256
CAP = 4
UP_NODES = 254
N_LEAF = 128


def level_pairs(key):
    count = N_LEAF * NBLK
    depth = LEAF_DEV.bit_length() - 1
    level = jax.random.randint(jax.random.fold_in(key, 11), (count,), 0, depth + 1, jnp.int32)
    level_width = jnp.right_shift(jnp.int32(LEAF_DEV), level)
    level_start = 2 * LEAF_DEV - 2 * level_width
    source_pick = jax.random.randint(jax.random.fold_in(key, 12), (count,), 0, LEAF_DEV, jnp.int32)
    target_pick = jax.random.randint(jax.random.fold_in(key, 13), (count,), 0, LEAF_DEV, jnp.int32)
    sources = level_start + source_pick % level_width
    targets = level_start + target_pick % level_width
    return (sources.astype(jnp.int32), targets.astype(jnp.int32))


def draw_block_source(key, part):
    return level_pairs(key)[0]


def draw_block_target(key, part):
    return level_pairs(key)[1]


def draw_up_coupling(key, part):
    node_ids = jnp.arange(UP_NODES, dtype=jnp.int32)
    whole_count = UP_NODES + 2
    tier = jnp.zeros((UP_NODES,), jnp.float32)
    for shift_no in range(1, 24):
        tier = tier + (node_ids >= whole_count - (whole_count >> shift_no)).astype(jnp.float32)
    local_levels = LEAF_DEV.bit_length() - 1
    scales = jnp.power(2.0, (tier + local_levels) / 2.0) / math.sqrt(K)
    base_draw = jnp.clip(jax.random.normal(key, (UP_NODES, K, K), jnp.float32), -4.0, 4.0)
    return (base_draw * scales[:, None, None]).astype(jnp.bfloat16)


def level_of(key, dims, shards, smallest, largest):
    factor_of = 1.0
    for position, blocks in shards:
        heights = jax.random.uniform(jax.random.fold_in(jax.random.fold_in(key, 6), position), (blocks,), jnp.float32, smallest / len(shards), largest / len(shards))
        factor_of = factor_of * jnp.repeat(jnp.exp(heights), dims[position] // blocks).reshape((-1,) + (1,) * (len(dims) - 1 - position))
    return factor_of


def assign_block(stream_key, own, number, rows, amount, top, most, skew):
    ranking = jax.random.permutation(stream_key, amount)
    packed, usual = shares(amount, rows * top, most, skew, True), shares(amount, rows * top, most, skew, False)
    places = jnp.arange(amount)

    def named(lengths, turn):
        used = int((lengths > 0).sum())
        fixed = max(1, used // 4)
        shifted = fixed + (places - fixed + turn * (used - fixed)) % max(1, amount - fixed)
        return jnp.zeros((amount,), jnp.int32).at[ranking[jnp.where(places < fixed, places, shifted)]].set(jnp.asarray(lengths, jnp.int32))

    lengths = jnp.where(number % 4 == 0, named(packed, number // 4), named(usual, number - number // 4 - 1))
    mixed = jax.random.permutation(jax.random.fold_in(own, 3), amount)
    source_of, sink = mixed[0:amount // 2 * 2:2], mixed[1:amount // 2 * 2:2]
    margin = jnp.minimum(lengths[source_of] - 1, most - lengths[sink]) // 2
    margin = jnp.where((source_of == ranking[0]) | (sink == ranking[0]) | (lengths[sink] == 0), 0, jnp.maximum(margin, 0))
    shifted = jax.random.randint(jax.random.fold_in(own, 4), (amount // 2,), 0, 1 << 20) % (margin + 1)
    lengths = lengths.at[source_of].add(-shifted).at[sink].add(shifted)
    members = jnp.searchsorted(jnp.cumsum(lengths), jnp.arange(rows * top), side="right").astype(jnp.int32)
    listing = members.reshape(top, rows).T
    listing = listing[jax.random.permutation(jax.random.fold_in(own, 1), rows)]
    turn = jax.random.randint(jax.random.fold_in(own, 2), (rows, 1), 0, top)
    return jnp.take_along_axis(listing, (jnp.arange(top)[None, :] + turn) % top, axis=1)


def shares(number_of, total, bound, slope, full):
    loads = [(1 << 20) // math.isqrt(rank ** slope) + 1 for rank in range(1, number_of + 1)]
    largest = bound if full else min(bound, max(-(-total // number_of), total * loads[0] // sum(loads)))
    least = 1 if total - largest >= number_of - 1 else 0
    holding, rest = [largest] + [least] * (number_of - 1), total - largest - least * (number_of - 1)
    while rest > 0:
        movable = [i for i in range(1, number_of) if holding[i] < largest] or [i for i in range(1, number_of) if holding[i] < bound]
        pool, remaining = sum([loads[i] for i in movable]), rest
        for i in movable:
            more = min(bound - holding[i], max(1, remaining * loads[i] // pool), rest)
            holding[i] = holding[i] + more
            rest = rest - more
    return np.array(holding)


def bell_draw(own_key, shape, deviation, limit, shards=(), kind=jnp.bfloat16):
    result = deviation * jax.random.normal(own_key, shape, jnp.float32)
    if shards:
        result = result * level_of(own_key, shape, shards, -0.22, 0.18)
    return jnp.clip(result, -limit, limit).astype(kind)


def setup_inputs(seed: int = 0) -> dict:
    seeds = jax.random.split(jax.random.key(seed), 12)
    points = bell_draw(seeds[0], (3, NPTS), 1.0, 4.0, ((1, 128),))
    vectors = bell_draw(seeds[1], (NV, NPTS), 1.0, 6.0, ((0, 2), (1, 128)))
    leaf_order = jax.vmap(lambda own: jax.random.permutation(own, LEAF_DEV * LEAF))(jax.random.split(seeds[2], N_LEAF)).reshape((N_LEAF, LEAF_DEV * LEAF)).astype(jnp.int32)
    leaf_bases = bell_draw(seeds[3], (LEAVES, K, LEAF), LEAF ** -0.5, 0.25, ((0, 128),))
    transfers = bell_draw(seeds[4], (N_LEAF * NTR, K, K), (2 * K) ** -0.5, 0.5, ((0, 128),))
    coupling_blocks = bell_draw(seeds[5], (N_LEAF * NBLK, K, K), K ** -0.5, 0.75, ((0, 128),))
    block_source = draw_block_source(jax.random.fold_in(seeds[11], 71), 0)
    block_owner_keys = jax.random.split(jax.random.fold_in(seeds[7], 1), (N_LEAF * NBLK) // NBLK)
    block_owner_turns = jax.random.permutation(jax.random.fold_in(seeds[7], 3), (N_LEAF * NBLK) // NBLK)
    block_owner = jax.vmap(lambda own, number: assign_block(jax.random.fold_in(seeds[7], 2), own, number, NBLK, N_LEAF, 1, CAP, 2))(block_owner_keys, block_owner_turns).reshape((N_LEAF * NBLK, 1))
    block_target = draw_block_target(jax.random.fold_in(seeds[11], 71), 0)
    up_transfer = bell_draw(seeds[9], (UP_NODES, K, K), (2 * K) ** -0.5, 0.5)
    up_coupling = draw_up_coupling(jax.random.fold_in(seeds[11], 71), 0)
    return {"points": points, "vectors": vectors, "leaf_order": leaf_order, "leaf_bases": leaf_bases, "transfers": transfers, "coupling_blocks": coupling_blocks, "block_source": block_source, "block_owner": block_owner, "block_target": block_target, "up_transfer": up_transfer, "up_coupling": up_coupling}


near_scale = 8.0
smooth_sq = 0.0025
highest = lax.Precision.HIGHEST

def kernel_block(sources, targets):
    source_f = sources.astype(jnp.float32)
    target_f = targets.astype(jnp.float32)
    distance = (source_f[0][:, None] - target_f[0][None, :]) ** 2
    distance = distance + (source_f[1][:, None] - target_f[1][None, :]) ** 2
    distance = distance + (source_f[2][:, None] - target_f[2][None, :]) ** 2
    return lax.rsqrt(distance + smooth_sq).astype(jnp.bfloat16)

def near_block(padded, first_leaf, number, leaf_len):
    reach = NEAR * leaf_len
    window_len = (2 * NEAR + 1) * leaf_len

    def one_leaf(leaf_no):
        start_col = (first_leaf + leaf_no) * leaf_len
        targets = lax.dynamic_slice_in_dim(padded, start_col + reach, leaf_len, 1)
        window = lax.dynamic_slice_in_dim(padded, start_col, window_len, 1)
        kernel = kernel_block(window[:3], targets[:3])
        return jnp.dot(window[3:], kernel, preferred_element_type=jnp.float32) * (near_scale / leaf_len)
    per_leaf = lax.map(one_leaf, jnp.arange(number, dtype=jnp.int32))
    return jnp.transpose(per_leaf, (1, 0, 2)).reshape(per_leaf.shape[1], number * leaf_len)

def climb(children, matrices):
    moved_rows = jnp.einsum('...jvk,...jkp->...jvp', children, matrices.astype(jnp.float32), precision=highest)
    return moved_rows[..., 0::2, :, :] + moved_rows[..., 1::2, :, :]

def descend(parent, matrices):
    spread = jnp.repeat(parent, 2, axis=-3)
    return jnp.einsum('...jvp,...jkp->...jvk', spread, matrices.astype(jnp.float32), precision=highest)

def upper_tree(roots, up_transfer, up_coupling):
    current = roots
    gain_list = []
    offset = 0
    number = roots.shape[0]
    while number > 1:
        matrices = up_transfer[offset:offset + number].astype(jnp.float32)
        partner = current.reshape(number // 2, 2, current.shape[1], current.shape[2])[:, ::-1].reshape(current.shape)
        gain_term = jnp.einsum('jvk,jkp->jvp', partner, up_coupling[offset:offset + number].astype(jnp.float32), precision=highest)
        gain_list.append((matrices, gain_term))
        current = climb(current, matrices)
        offset += number
        number //= 2
    top_down = jnp.zeros_like(current)
    for matrices, gain_term in reversed(gain_list):
        top_down = descend(top_down, matrices) + gain_term
    return top_down

def reorder(array, permute):
    per_dev = LEAF_DEV * LEAF
    row_count = array.shape[0]
    blocked = array.reshape(row_count, N_LEAF, per_dev)
    picks = jnp.broadcast_to(permute[None], (row_count, N_LEAF, per_dev))
    return jnp.take_along_axis(blocked, picks, axis=2).reshape(row_count, NPTS)

def reference(points, vectors, leaf_order, leaf_bases, transfers, coupling_blocks, block_source, block_owner, block_target, up_transfer, up_coupling):
    per_dev = LEAF_DEV * LEAF
    points_tree = reorder(points, leaf_order)
    vectors_tree = reorder(vectors, leaf_order)
    reach = NEAR * LEAF
    joined = jnp.concatenate([points_tree, vectors_tree], axis=0)
    padded = jnp.pad(joined, ((0, 0), (reach, reach)))
    near_part = near_block(padded, 0, LEAVES, LEAF)
    shaped = vectors_tree.reshape(NV, LEAVES, LEAF).astype(jnp.float32)
    leaf_coeff = jnp.einsum('vlp,lkp->lvk', shaped, leaf_bases.astype(jnp.float32), precision=highest)
    leaf_coeff = leaf_coeff.reshape(N_LEAF, LEAF_DEV, NV, K)
    trans_all = transfers.reshape(N_LEAF, NTR, K, K)
    levels = [leaf_coeff]
    offset = 0
    number = LEAF_DEV
    while number > 1:
        levels.append(climb(levels[-1], trans_all[:, offset:offset + number]))
        offset += number
        number //= 2
    all_coeff = jnp.concatenate(levels, axis=1)
    top_down = upper_tree(all_coeff[:, NCL - 1], up_transfer, up_coupling)
    coeff_bf = all_coeff.astype(jnp.bfloat16)
    owner_dev = jnp.arange(N_LEAF * NBLK, dtype=jnp.int32) // NBLK
    picked = coeff_bf[owner_dev, block_source].astype(jnp.float32)
    products = jnp.einsum('bvk,bkp->bvp', picked, coupling_blocks.astype(jnp.float32), precision=highest)
    flat_target = block_owner[:, 0] * NCL + block_target
    coupled = jax.ops.segment_sum(products, flat_target, num_segments=N_LEAF * NCL).reshape(N_LEAF, NCL, NV, K)
    current = (top_down + coupled[:, NCL - 1])[:, None]
    number = 1
    while number < LEAF_DEV:
        number *= 2
        offset = 2 * LEAF_DEV - 2 * number
        current = descend(current, trans_all[:, offset:offset + number]) + coupled[:, offset:offset + number]
    down_leaf = lax.optimization_barrier(current.astype(jnp.bfloat16)).astype(jnp.float32)
    bases_f = leaf_bases.reshape(N_LEAF, LEAF_DEV, K, LEAF).astype(jnp.float32)
    far_part = jnp.einsum('nlvk,nlkp->vnlp', down_leaf, bases_f, precision=highest).reshape(NV, NPTS)
    tree_out = (far_part + near_part).astype(jnp.bfloat16)
    row_ids = jnp.arange(N_LEAF, dtype=jnp.int32)[:, None]
    positions = jnp.broadcast_to(jnp.arange(per_dev, dtype=jnp.int32)[None], (N_LEAF, per_dev))
    inverse = jnp.zeros((N_LEAF, per_dev), jnp.int32).at[row_ids, leaf_order].set(positions)
    return reorder(tree_out, inverse)
```

```python
import jax
import jax.numpy as jnp
import ml_dtypes
from jax import lax
from jax.experimental import pallas as pl
from jax.experimental.pallas import tpu as pltpu
from jax.sharding import PartitionSpec as P

f32 = jnp.float32
bf16 = jnp.bfloat16
i32 = jnp.int32

LEAF = 512
COLS = 8192
HALO = 1024
LOCAL = 5120
HALF = 4096
NT = (((1,), (1,)), ((), ()))
TN = (((0,), (0,)), ((), ()))
SMOOTH_HI = float(ml_dtypes.bfloat16(0.0025))
SMOOTH_LO = float(ml_dtypes.bfloat16(0.0025 - SMOOTH_HI))
VM = pl.BlockSpec(memory_space=pltpu.VMEM)


def dot(a, b, dims=(((1,), (0,)), ((), ()))):
    return lax.dot_general(a, b, dims, preferred_element_type=f32)


def iota(shape, dim):
    return lax.broadcasted_iota(i32, shape, dim)


def hot(mask):
    return jnp.where(mask, 1.0, 0.0).astype(bf16)


def halves(x):
    hi = x.astype(bf16)
    lo = (x - hi.astype(f32)).astype(bf16)
    return jnp.concatenate([hi, lo], axis=0)


def wide(x):
    return jnp.concatenate([x, jnp.zeros_like(x)], axis=1)


def dot_pair(x, w, dims=(((1,), (0,)), ((), ()))):
    y = dot(halves(x), w, dims)
    n = x.shape[0]
    return y[:n] + y[n:]


def call(kernel, outs, scratch, args, flops, nbytes, vmem=48):
    return pl.pallas_call(
        kernel,
        out_shape=[jax.ShapeDtypeStruct(s, d) for s, d in outs],
        in_specs=[VM] * len(args),
        out_specs=[VM] * len(outs),
        scratch_shapes=scratch,
        compiler_params=pltpu.CompilerParams(vmem_limit_bytes=vmem << 20),
        cost_estimate=pl.CostEstimate(flops=flops, bytes_accessed=nbytes, transcendentals=0),
    )(*args)


def gather_kernel(pts, vec, perm, vt, pt, send_a, send_b, send_c, dv, dp):
    core = lax.axis_index("vec")
    for m in range(16):
        a, b = 512 * m, 512 * m + 256
        dv[16 * m : 16 * m + 16, :] = jnp.concatenate(
            [vec[:, a : a + 256], vec[:, b : b + 256]], axis=0
        )
        three = pts[:, a : a + 512].astype(f32)
        four = jnp.concatenate([three, jnp.zeros((1, 512), f32)], axis=0)
        dp[8 * m : 8 * m + 8, :] = jnp.concatenate([four[:, :256], four[:, 256:]], axis=0)
    data_v = dv[...]
    data_p = dp[...].astype(bf16)
    width = 512
    for n in range(COLS // width):
        cols = slice(n * width, (n + 1) * width)
        index = perm[:, cols]
        low = index & 255
        high = jnp.broadcast_to(lax.shift_right_logical(index, 8), (8, width))
        select = hot(iota((256, width), 0) == low)
        got = dot(data_v, select)
        out = got[:8]
        for q in range(1, 32):
            out = jnp.where(high == q, got[8 * q : 8 * q + 8], out)
        vt[:, cols] = out.astype(bf16)
        got = dot(data_p, select)
        pair = high - iota((8, width), 0) // 4
        out = jnp.zeros((8, width), f32)
        for m in range(16):
            out = jnp.where(pair == 2 * m, got[8 * m : 8 * m + 8], out)
        out = out[:4] + out[4:]
        pt[:, cols] = jnp.concatenate([out, jnp.zeros((4, width), f32)], axis=0).astype(bf16)
    first, last = slice(0, HALO), slice(COLS - HALO, COLS)

    @pl.when(core == 0)
    def _():
        send_a[0:8, :] = vt[:, first]
        send_a[8:16, :] = pt[:, first]
        send_b[...] = vt[:, last]
        send_c[...] = vt[:, COLS - LOCAL :]

    @pl.when(core == 1)
    def _():
        send_a[0:8, :] = vt[:, last]
        send_a[8:16, :] = pt[:, last]
        send_b[...] = vt[:, first]
        send_c[...] = vt[:, :LOCAL]


def coeff_kernel(vt, bases, tr, cp, bsrc, bown, btgt, send, cf, pick, prod):
    cf[248:256, :] = jnp.zeros((8, 128), f32)
    for leaf in range(16):
        cf[8 * leaf : 8 * leaf + 8, :64] = dot(
            vt[:, LEAF * leaf : LEAF * leaf + LEAF], bases[leaf], NT
        )
    off, n = 0, 16
    while n > 1:
        for m in range(n // 2):
            r = 8 * (off + 2 * m)
            pair = jnp.concatenate([cf[r : r + 8, :64], cf[r + 8 : r + 16, :64]], axis=1)
            w = tr[off + 2 * m : off + 2 * m + 2].reshape(128, 64)
            t = 8 * (off + n + m)
            cf[t : t + 8, :64] = dot_pair(pair, w)
        off += n
        n //= 2
    source = hot(iota((32, 256), 0) == bsrc[...])
    for v in range(8):
        mine = cf[pl.ds(v, 32, stride=8), :][:, :64].astype(bf16)
        chosen = dot(mine, source, TN)
        pick[pl.ds(v, 64, stride=8), :] = chosen[:, :128]
        pick[pl.ds(512 + v, 64, stride=8), :] = chosen[:, 128:]
    for half in range(2):
        lanes = slice(128 * half, 128 * half + 128)
        for pb in range(4):
            rows = slice(16 * pb, 16 * pb + 16)

            def step(k, acc):
                block = cp[k, rows, lanes].astype(f32)
                picked = pick[pl.ds(pl.multiple_of(512 * half + 8 * k, 8), 8), :]
                return tuple(acc[v] + picked[v : v + 1] * block for v in range(8))

            acc = lax.fori_loop(0, 64, step, (jnp.zeros((16, 128), f32),) * 8, unroll=8)
            for v in range(8):
                top = 64 * (v % 4) + 16 * pb
                left = 256 * (v // 4) + 128 * half
                prod[top : top + 16, left : left + 128] = acc[v].astype(bf16)
    prod[256:384, 0:256] = jnp.zeros((128, 256), bf16)
    prod[256:384, 256:512] = jnp.broadcast_to((btgt[...] + 1).astype(f32), (128, 256)).astype(bf16)
    owner = bown[...]
    owner_f = owner.astype(f32)
    column = jnp.transpose(jnp.broadcast_to(owner_f, (128, 256)))
    ranks = []
    for half in range(2):
        row = owner_f[:, 128 * half : 128 * half + 128]
        before = iota((256, 128), 0) < iota((256, 128), 1) + 128 * half
        same = jnp.where((column == row) & before, 1.0, 0.0)
        ranks.append(jnp.sum(same, axis=0, keepdims=True))
    place = owner * 8 + jnp.concatenate(ranks, axis=1).astype(i32)
    place = jnp.concatenate([place, place + 4], axis=1)
    even = cf[pl.ds(240, 4, stride=2), :][:, :64]
    odd = cf[pl.ds(241, 4, stride=2), :][:, :64]
    root = jnp.concatenate([even, odd], axis=1)
    root = jnp.concatenate([root, jnp.zeros((4, 128), f32)], axis=0)
    payload = prod[...]
    for part in range(4):
        rows = slice(256 * part, 256 * part + 256)
        slots = hot(iota((256, 512), 0) + 256 * part == place)
        out = dot(slots, payload, NT)
        send[rows, 0:256] = out[:, :256].astype(bf16)
        extra = out[:, 256:].reshape(32, 8, 128) + root[None]
        send[rows, 256:384] = extra.reshape(256, 128).astype(bf16)


def split3(x):
    a = x.astype(bf16).astype(f32)
    b = (x - a).astype(bf16).astype(f32)
    return a, b, x - a - b


def near_kernel(vt, pt, rec_a, rec_b, rec_c, mine, other, vw, pw, fs, ft, acc):
    core = lax.axis_index("vec")

    @pl.when(core == 0)
    def _():
        vw[0:8, HALO:] = vt[:, :LOCAL]
        vw[8:16, HALO:] = rec_c[...]
        vw[0:8, :HALO] = rec_b[...]
        vw[8:16, :HALO] = rec_a[0:8, :]
        pw[:, HALO:] = pt[:, :LOCAL].astype(f32)
        pw[:, :HALO] = rec_a[8:16, :].astype(f32)

    @pl.when(core == 1)
    def _():
        vw[0:8, :LOCAL] = vt[:, COLS - LOCAL :]
        vw[8:16, :LOCAL] = rec_c[...]
        vw[0:8, LOCAL:] = rec_b[...]
        vw[8:16, LOCAL:] = rec_a[0:8, :]
        pw[:, :LOCAL] = pt[:, COLS - LOCAL :].astype(f32)
        pw[:, LOCAL:] = rec_a[8:16, :].astype(f32)

    for leaf in range(12):
        cols = slice(LEAF * leaf, LEAF * leaf + LEAF)
        p = pw[0:3, cols]
        norm = p[0:1] * p[0:1] + p[1:2] * p[1:2] + p[2:3] * p[2:3]
        parts = jnp.concatenate(split3(norm), axis=0)
        one = jnp.ones((3, LEAF), f32)
        two = jnp.ones((2, LEAF), f32)
        pad = jnp.zeros((5, LEAF), f32)
        source = jnp.concatenate([p, parts, one, two, pad], axis=0)
        smooth = jnp.where(iota((2, LEAF), 0) == 0, SMOOTH_HI, SMOOTH_LO)
        target = jnp.concatenate([-2.0 * p, one, parts, smooth, pad], axis=0)
        fs[cols, :] = jnp.transpose(source).astype(bf16)
        ft[:, cols] = target.astype(bf16)
    acc[...] = jnp.zeros_like(acc)
    for t in range(2, 10):
        tc = slice(LEAF * t, LEAF * t + LEAF)
        to = slice(LEAF * (t - 2), LEAF * (t - 1))
        total = jnp.zeros((16, LEAF), f32)
        for s in range(t - 2, t + 3):
            if 2 <= s < t:
                continue
            sc = slice(LEAF * s, LEAF * s + LEAF)
            kernel = lax.rsqrt(dot(fs[sc, :], ft[:, tc])).astype(bf16)
            total = total + dot(vw[:, sc], kernel)
            if t < s < 10:
                so = slice(LEAF * (s - 2), LEAF * (s - 1))
                acc[:, so] += dot(vw[:, tc], kernel, NT)
        acc[:, to] += total
    mine[...] = acc[0:8, :] * (8.0 / LEAF)
    other[...] = acc[8:16, :] * (8.0 / LEAF)


LEVEL_START = [256 - (256 >> u) for u in range(7)]


def matrices_kernel(ut, uc, et, eu):
    device = lax.axis_index("leaf")
    row, lane = iota((80, 254), 0), iota((80, 254), 1)
    own = jnp.zeros((80, 254), i32) - 1
    for u in range(7):
        own = jnp.where(row == 64 + u, LEVEL_START[u] + lax.shift_right_logical(device, u), own)
    pick_t = hot(((row < 62) & (lane == row + 192)) | (lane == own))
    pick_c = pick_t[64:80]

    def step(k, carry):
        et[pl.ds(pl.multiple_of(80 * k, 8), 80), :64] = dot(pick_t, ut[k], NT)
        eu[pl.ds(pl.multiple_of(16 * k, 8), 16), :64] = dot(pick_c, uc[k], NT)
        return carry

    lax.fori_loop(0, 64, step, 0, unroll=8)


def final_kernel(
    recv, near_mine, near_other, ut, et, eu, tr, bases, perm, out,
    ext, xt, y0, y1, xs, gain, cpl, dn, tree,
):
    device = lax.axis_index("leaf")
    core = lax.axis_index("vec")
    ext[...] = recv[:, 256:384].astype(f32)

    for s in range(4):
        turned = jnp.transpose(ext[pl.ds(s, 128, stride=8), :])
        xt[pl.ds(2 * s, 64, stride=8), :] = turned[:64]
        xt[pl.ds(2 * s + 1, 64, stride=8), :] = turned[64:]

    def climb_lanes(left, width, dest):
        for pb in range(4):
            rows = slice(16 * pb, 16 * pb + 16)

            def step(k, acc):
                block = ut[k, rows, left : left + width].astype(f32)
                values = xt[pl.ds(pl.multiple_of(8 * k, 8), 8), 0:width]
                return tuple(acc[v] + values[v : v + 1] * block for v in range(8))

            acc = lax.fori_loop(0, 64, step, (jnp.zeros((16, width), f32),) * 8, unroll=8)
            for v in range(8):
                dest[64 * v + 16 * pb : 64 * v + 16 * pb + 16, :] = acc[v]

    def to_rows(values, count, base):
        for v in range(8):
            xs[pl.ds(base * 8 + v, count, stride=8), :] = wide(values[:count, 64 * v : 64 * v + 64])

    sibling0 = lax.bitwise_xor(device, 1)
    lines = ext[pl.ds(pl.multiple_of(sibling0 * 8, 8), 8), :]
    for s in range(4):
        line = lines[s : s + 1]
        xs[2 * s : 2 * s + 1, :64] = line[:, :64]
        xs[2 * s + 1 : 2 * s + 2, :64] = line[:, 64:]
    climb_lanes(0, 128, y0)
    hi = y0[...].astype(bf16)
    lo = (y0[...] - hi.astype(f32)).astype(bf16)
    join = hot(iota((128, 128), 0) // 2 == iota((128, 128), 1))
    joined = dot(hi, join) + dot(lo, join)
    for v in range(8):
        xt[pl.ds(v, 64, stride=8), :] = joined[64 * v : 64 * v + 64]
    sibling1 = lax.bitwise_xor(lax.shift_right_logical(device, 1), 1)
    pick = hot((iota((8, 128), 1) // 2 == sibling1) & (iota((8, 128), 0) == 0))
    to_rows(dot(pick, hi, NT) + dot(pick, lo, NT), 1, 1)
    climb_lanes(128, 64, y1)
    hi = y1[...].astype(bf16)
    lo = (y1[...] - hi.astype(f32)).astype(bf16)
    join = hot(iota((32, 64), 1) // 2 == iota((32, 64), 0))
    to_rows(dot(join, hi, NT) + dot(join, lo, NT), 32, 2)
    first, n = 2, 32
    firsts = {2: 2}
    for u in range(2, 6):
        for m in range(n // 2):
            r = 8 * (first + 2 * m)
            e = LEVEL_START[u] - 192 + 2 * m
            pair = jnp.concatenate([xs[r : r + 8, :64], xs[r + 8 : r + 16, :64]], axis=1)
            w = jnp.concatenate(
                [et[pl.ds(e, 64, stride=80), :], et[pl.ds(e + 1, 64, stride=80), :]], axis=0
            )[:, :64].astype(bf16)
            t = 8 * (first + n + m)
            xs[t : t + 8, :64] = dot_pair(pair, w)
        first += n
        n //= 2
        firsts[u + 1] = first

    for u in range(7):
        if u < 2:
            partner = xs[8 * u : 8 * u + 8, :64]
        else:
            sib = lax.bitwise_xor(lax.shift_right_logical(device, u), 1)
            partner = xs[pl.ds(pl.multiple_of((firsts[u] + sib) * 8, 8), 8), :64]
        gain[8 * u : 8 * u + 8, :] = dot_pair(
            partner, eu[pl.ds(u, 64, stride=16), :][:, :64].astype(bf16)
        )
    down = gain[48:56, :]
    for u in range(5, -1, -1):
        w = et[pl.ds(64 + u, 64, stride=80), :][:, :64].astype(bf16)
        down = dot_pair(down, w, NT) + gain[8 * u : 8 * u + 8, :]

    late = (iota((128, 8, 128), 1) >= 4)
    lab = ext[...].reshape(128, 8, 128)
    early_lab = jnp.where(late, 0.0, pltpu.roll(lab, 4, 1)).reshape(1024, 128)
    late_lab = jnp.where(late, lab, 0.0).reshape(1024, 128)
    name = (iota((1024, 128), 1) + 1).astype(f32)
    for h, label in enumerate((early_lab, late_lab)):
        sums = dot(hot(label == name), recv[:, 0:256], TN)
        for v in range(4):
            cpl[pl.ds(4 * h + v, 32, stride=8), :] = wide(sums[:32, 64 * v : 64 * v + 64])

    dn[240:248, :] = down + cpl[240:248, :64]
    n = 1
    while n < 16:
        off_parent = 32 - 2 * n
        n *= 2
        off = 32 - 2 * n
        for m in range(n // 2):
            r = 8 * (off_parent + m)
            w = tr[off + 2 * m : off + 2 * m + 2].reshape(128, 64)
            both = dot_pair(dn[r : r + 8, :], w, NT)
            t = 8 * (off + 2 * m)
            dn[t : t + 8, :] = both[:, :64] + cpl[t : t + 8, :64]
            dn[t + 8 : t + 16, :] = both[:, 64:] + cpl[t + 8 : t + 16, :64]
    for leaf in range(16):
        tree[:, LEAF * leaf : LEAF * leaf + LEAF] = dot(
            dn[8 * leaf : 8 * leaf + 8, :].astype(bf16), bases[leaf]
        )

    @pl.when(core == 0)
    def _():
        tree[:, :HALF] += near_mine[...]
        tree[:, HALF:] += near_other[...]

    @pl.when(core == 1)
    def _():
        tree[:, :HALF] += near_other[...]
        tree[:, HALF:] += near_mine[...]

    width = 512
    total = jnp.zeros((256, 256), f32)
    for b in range(COLS // width):
        cols = slice(b * width, (b + 1) * width)
        index = perm[:, cols]
        select = hot(iota((256, width), 0) == (index & 255))
        high = jnp.broadcast_to(lax.shift_right_logical(index, 8), (8, width))
        values = tree[:, cols]
        spread = jnp.concatenate(
            [jnp.where(high == q, values, 0.0) for q in range(32)], axis=0
        ).astype(bf16)
        total = total + dot(spread, select, NT)
    for q in range(32):
        out[:, 256 * q : 256 * q + 256] = total[8 * q : 8 * q + 8].astype(bf16)


def shards(
    points, vectors, leaf_order, leaf_bases, transfers, coupling_blocks,
    block_source, block_owner, block_target, up_transfer, up_coupling,
):
    peers = lax.axis_size("leaf")
    axes = ("leaf", "vec")
    vt, pt, send_a, send_b, send_c = call(
        gather_kernel,
        [((8, COLS), bf16), ((8, COLS), bf16), ((16, HALO), bf16), ((8, HALO), bf16), ((8, LOCAL), bf16)],
        [pltpu.VMEM((256, 256), bf16), pltpu.VMEM((128, 256), f32)],
        (points, vectors, leaf_order),
        2 * 384 * 256 * COLS, 1 << 20,
    )
    pairs_a, pairs_b, pairs_c = [], [], []
    for d in range(peers):
        pairs_c += [(2 * d, 2 * d + 1), (2 * d + 1, 2 * d)]
        if d + 1 < peers:
            pairs_a += [(2 * d + 1, 2 * d + 2), (2 * d + 2, 2 * d + 1)]
            pairs_b += [(2 * d, 2 * d + 2), (2 * d + 3, 2 * d + 1)]
    rec_c = lax.ppermute(send_c, axes, pairs_c)
    rec_a = lax.ppermute(send_a, axes, pairs_a)
    rec_b = lax.ppermute(send_b, axes, pairs_b)
    (send,) = call(
        coeff_kernel,
        [((1024, 384), bf16)],
        [pltpu.VMEM((256, 128), f32), pltpu.VMEM((1024, 128), f32), pltpu.VMEM((384, 512), bf16)],
        (
            vt, leaf_bases, transfers, jnp.transpose(coupling_blocks, (1, 2, 0)),
            block_source.reshape(1, -1), block_owner.reshape(1, -1), block_target.reshape(1, -1),
        ),
        2 * 1024 * 512 * 384, 4 << 20,
    )
    recv = lax.all_to_all(send, "leaf", split_axis=0, concat_axis=0, tiled=True)
    near_mine, near_send = call(
        near_kernel,
        [((8, HALF), f32), ((8, HALF), f32)],
        [
            pltpu.VMEM((16, 6144), bf16), pltpu.VMEM((8, 6144), f32), pltpu.VMEM((6144, 16), bf16),
            pltpu.VMEM((16, 6144), bf16), pltpu.VMEM((16, HALF), f32),
        ],
        (vt, pt, rec_a, rec_b, rec_c),
        2 * 67 * 512 * 512 * 256, 1 << 20,
    )
    near_other = lax.ppermute(near_send, axes, pairs_c)
    ut = jnp.transpose(up_transfer, (1, 2, 0))
    uc = jnp.transpose(up_coupling, (1, 2, 0))
    et, eu = call(
        matrices_kernel,
        [((64 * 80, 128), f32), ((64 * 16, 128), f32)],
        [],
        (ut, uc),
        2 * 8192 * 256 * 96, 8 << 20,
    )
    (out,) = call(
        final_kernel,
        [((8, COLS), bf16)],
        [
            pltpu.VMEM((1024, 128), f32), pltpu.VMEM((512, 128), f32), pltpu.VMEM((512, 128), f32),
            pltpu.VMEM((512, 64), f32), pltpu.VMEM((576, 128), f32), pltpu.VMEM((56, 64), f32),
            pltpu.VMEM((256, 128), f32), pltpu.VMEM((248, 64), f32), pltpu.VMEM((8, COLS), f32),
        ],
        (recv, near_mine, near_other, ut, et, eu, transfers, leaf_bases, leaf_order),
        2 * 256 * 256 * COLS, 8 << 20,
    )
    return out


def solution(mesh):
    return jax.shard_map(
        shards,
        mesh=mesh,
        in_specs=(
            P(None, "leaf"),
            P("vec", "leaf"),
            P("leaf", None),
            P("leaf", None, None),
            P("leaf", None, None),
            P("leaf", None, None),
            P("leaf"),
            P("leaf", None),
            P("leaf"),
            P(),
            P(),
        ),
        out_specs=P("vec", "leaf"),
        check_vma=False,
    )
```

```python
import jax
import jax.numpy as jnp
import ml_dtypes
from jax import lax
from jax.experimental import pallas as pl
from jax.experimental.pallas import tpu as pltpu
from jax.sharding import PartitionSpec as P

f32 = jnp.float32
bf16 = jnp.bfloat16
i32 = jnp.int32

LEAF = 512
COLS = 8192
HALO = 1024
LOCAL = 5120
HALF = 4096
NT = (((1,), (1,)), ((), ()))
TN = (((0,), (0,)), ((), ()))
SMOOTH_HI = float(ml_dtypes.bfloat16(0.0025))
SMOOTH_LO = float(ml_dtypes.bfloat16(0.0025 - SMOOTH_HI))
VM = pl.BlockSpec(memory_space=pltpu.VMEM)


def dot(a, b, dims=(((1,), (0,)), ((), ()))):
    return lax.dot_general(a, b, dims, preferred_element_type=f32)


def iota(shape, dim):
    return lax.broadcasted_iota(i32, shape, dim)


def hot(mask):
    return jnp.where(mask, 1.0, 0.0).astype(bf16)


def halves(x):
    hi = x.astype(bf16)
    lo = (x - hi.astype(f32)).astype(bf16)
    return jnp.concatenate([hi, lo], axis=0)


def wide(x):
    return jnp.concatenate([x, jnp.zeros_like(x)], axis=1)


def dot_pair(x, w, dims=(((1,), (0,)), ((), ()))):
    y = dot(halves(x), w, dims)
    n = x.shape[0]
    return y[:n] + y[n:]


def call(kernel, outs, scratch, args, flops, nbytes, vmem=16, anywhere=0):
    return pl.pallas_call(
        kernel,
        out_shape=[jax.ShapeDtypeStruct(s, d) for s, d in outs],
        in_specs=[VM] * (len(args) - anywhere) + [pl.BlockSpec(memory_space=pl.ANY)] * anywhere,
        out_specs=[VM] * len(outs),
        scratch_shapes=scratch,
        compiler_params=pltpu.CompilerParams(vmem_limit_bytes=vmem << 20),
        cost_estimate=pl.CostEstimate(flops=flops, bytes_accessed=nbytes, transcendentals=0),
    )(*args)


def gather_kernel(pts, vec, perm, vt, pt, send_a, send_b, send_c, dv, dp):
    core = lax.axis_index("vec")
    for m in range(16):
        a, b = 512 * m, 512 * m + 256
        dv[16 * m : 16 * m + 16, :] = jnp.concatenate(
            [vec[:, a : a + 256], vec[:, b : b + 256]], axis=0
        )
        three = pts[:, a : a + 512].astype(f32)
        four = jnp.concatenate([three, jnp.zeros((1, 512), f32)], axis=0)
        dp[8 * m : 8 * m + 8, :] = jnp.concatenate([four[:, :256], four[:, 256:]], axis=0)
    data_v = dv[...]
    data_p = dp[...].astype(bf16)
    width = 512
    for n in range(COLS // width):
        cols = slice(n * width, (n + 1) * width)
        index = perm[:, cols]
        low = index & 255
        high = jnp.broadcast_to(lax.shift_right_logical(index, 8), (8, width))
        select = hot(iota((256, width), 0) == low)
        got = dot(data_v, select)
        out = got[:8]
        for q in range(1, 32):
            out = jnp.where(high == q, got[8 * q : 8 * q + 8], out)
        vt[:, cols] = out.astype(bf16)
        got = dot(data_p, select)
        pair = high - iota((8, width), 0) // 4
        out = jnp.zeros((8, width), f32)
        for m in range(16):
            out = jnp.where(pair == 2 * m, got[8 * m : 8 * m + 8], out)
        out = out[:4] + out[4:]
        pt[:, cols] = jnp.concatenate([out, jnp.zeros((4, width), f32)], axis=0).astype(bf16)
    first, last = slice(0, HALO), slice(COLS - HALO, COLS)

    @pl.when(core == 0)
    def _():
        send_a[0:8, :] = vt[:, first]
        send_a[8:16, :] = pt[:, first]
        send_b[...] = vt[:, last]
        send_c[...] = vt[:, COLS - LOCAL :]

    @pl.when(core == 1)
    def _():
        send_a[0:8, :] = vt[:, last]
        send_a[8:16, :] = pt[:, last]
        send_b[...] = vt[:, first]
        send_c[...] = vt[:, :LOCAL]


def coeff_kernel(vt, bases, tr, et, cf, path):
    cf[248:256, :] = jnp.zeros((8, 128), f32)
    for leaf in range(16):
        cf[8 * leaf : 8 * leaf + 8, :64] = dot(
            vt[:, LEAF * leaf : LEAF * leaf + LEAF], bases[leaf], NT
        )
    off, n = 0, 16
    while n > 1:
        for m in range(n // 2):
            r = 8 * (off + 2 * m)
            pair = jnp.concatenate([cf[r : r + 8, :64], cf[r + 8 : r + 16, :64]], axis=1)
            w = tr[off + 2 * m : off + 2 * m + 2].reshape(128, 64)
            t = 8 * (off + n + m)
            cf[t : t + 8, :64] = dot_pair(pair, w)
        off += n
        n //= 2
    value = cf[240:248, :64]
    for u in range(3):
        path[8 * u : 8 * u + 8, :] = value
        value = dot_pair(value, own_matrix(et, OWN + u, T_ROWS))
    path[24:32, :] = value


def own_matrix(ref, row, rows):
    return ref[pl.ds(row, 64, stride=rows), :][:, :64].astype(bf16)


def product_kernel(cf, path, cp, bsrc, bown, btgt, seen_a, seen_b, seen_c, send, pick, prod):
    source = hot(iota((32, 256), 0) == bsrc[...])
    for v in range(8):
        mine = cf[pl.ds(v, 32, stride=8), :][:, :64].astype(bf16)
        chosen = dot(mine, source, TN)
        pick[pl.ds(v, 64, stride=8), :] = chosen[:, :128]
        pick[pl.ds(512 + v, 64, stride=8), :] = chosen[:, 128:]
    for half in range(2):
        lanes = slice(128 * half, 128 * half + 128)
        for pb in range(4):
            rows = slice(16 * pb, 16 * pb + 16)

            def step(k, acc):
                block = cp[k, rows, lanes].astype(f32)
                picked = pick[pl.ds(pl.multiple_of(512 * half + 8 * k, 8), 8), :]
                return tuple(acc[v] + picked[v : v + 1] * block for v in range(8))

            acc = lax.fori_loop(0, 64, step, (jnp.zeros((16, 128), f32),) * 8, unroll=8)
            for v in range(8):
                top = 64 * v + 16 * pb
                prod[top : top + 16, lanes] = acc[v].astype(bf16)
    prod[512:576, :] = jnp.zeros((64, 256), bf16)
    prod[576:640, :] = jnp.broadcast_to((btgt[...] + 1).astype(f32), (64, 256)).astype(bf16)
    owner = bown[...]
    owner_f = owner.astype(f32)
    column = jnp.transpose(jnp.broadcast_to(owner_f, (128, 256)))
    ranks = []
    for half in range(2):
        row = owner_f[:, 128 * half : 128 * half + 128]
        before = iota((256, 128), 0) < iota((256, 128), 1) + 128 * half
        same = jnp.where((column == row) & before, 1.0, 0.0)
        ranks.append(jnp.sum(same, axis=0, keepdims=True))
    place = owner * 4 + jnp.concatenate(ranks, axis=1).astype(i32)
    top = path[24:32, :]
    high = top.astype(bf16).astype(f32)
    extra = jnp.concatenate([high, top - high, jnp.zeros((16, 64), f32)], axis=0)
    extra = wide(extra)
    payload = prod[...]
    for part in range(2):
        rows = slice(256 * part, 256 * part + 256)
        slots = hot(iota((256, 256), 0) + 256 * part == place)
        out = dot(slots, payload, NT)
        send[rows, 0:512] = out[:, :512].astype(bf16)
        tail = out[:, 512:].reshape(8, 32, 128) + extra[None]
        send[rows, 512:640] = tail.reshape(256, 128).astype(bf16)


def split3(x):
    a = x.astype(bf16).astype(f32)
    b = (x - a).astype(bf16).astype(f32)
    return a, b, x - a - b


def near_setup_kernel(vt, pt, rec_a, rec_b, rec_c, vw, fs, ft, acc, pw):
    core = lax.axis_index("vec")

    @pl.when(core == 0)
    def _():
        vw[0:8, HALO:] = vt[:, :LOCAL]
        vw[8:16, HALO:] = rec_c[...]
        vw[0:8, :HALO] = rec_b[...]
        vw[8:16, :HALO] = rec_a[0:8, :]
        pw[:, HALO:] = pt[:, :LOCAL].astype(f32)
        pw[:, :HALO] = rec_a[8:16, :].astype(f32)

    @pl.when(core == 1)
    def _():
        vw[0:8, :LOCAL] = vt[:, COLS - LOCAL :]
        vw[8:16, :LOCAL] = rec_c[...]
        vw[0:8, LOCAL:] = rec_b[...]
        vw[8:16, LOCAL:] = rec_a[0:8, :]
        pw[:, :LOCAL] = pt[:, COLS - LOCAL :].astype(f32)
        pw[:, LOCAL:] = rec_a[8:16, :].astype(f32)

    for leaf in range(12):
        cols = slice(LEAF * leaf, LEAF * leaf + LEAF)
        p = pw[0:3, cols]
        norm = p[0:1] * p[0:1] + p[1:2] * p[1:2] + p[2:3] * p[2:3]
        parts = jnp.concatenate(split3(norm), axis=0)
        one = jnp.ones((3, LEAF), f32)
        two = jnp.ones((2, LEAF), f32)
        pad = jnp.zeros((5, LEAF), f32)
        source = jnp.concatenate([p, parts, one, two, pad], axis=0)
        smooth = jnp.where(iota((2, LEAF), 0) == 0, SMOOTH_HI, SMOOTH_LO)
        target = jnp.concatenate([-2.0 * p, one, parts, smooth, pad], axis=0)
        fs[cols, :] = jnp.transpose(source).astype(bf16)
        ft[:, cols] = target.astype(bf16)
    acc[...] = jnp.zeros_like(acc)
    near_blocks(range(2, 6), vw, fs, ft, acc)


def near_blocks(targets, vw, fs, ft, acc):
    for t in targets:
        tc = slice(LEAF * t, LEAF * t + LEAF)
        to = slice(LEAF * (t - 2), LEAF * (t - 1))
        total = jnp.zeros((16, LEAF), f32)
        for s in range(t - 2, t + 3):
            if 2 <= s < t:
                continue
            sc = slice(LEAF * s, LEAF * s + LEAF)
            kernel = lax.rsqrt(dot(fs[sc, :], ft[:, tc])).astype(bf16)
            total = total + dot(vw[:, sc], kernel)
            if t < s < 10:
                so = slice(LEAF * (s - 2), LEAF * (s - 1))
                acc[:, so] += dot(vw[:, tc], kernel, NT)
        acc[:, to] += total


def near_rest_kernel(vw, fs, ft, begun, mine, other, acc):
    acc[...] = begun[...]
    near_blocks(range(6, 10), vw, fs, ft, acc)
    mine[...] = acc[0:8, :] * (8.0 / LEAF)
    other[...] = acc[8:16, :] * (8.0 / LEAF)


LEVEL_START = [256 - (256 >> u) for u in range(7)]
UPPER = 224
OWN = 30
SIBLING = 33
OWN_UPPER = 36
T_ROWS = 40
C_ROWS = 8


def matrices_kernel(ut, uc, et, eu):
    device = lax.axis_index("leaf")

    def node(u, other=False):
        n = lax.shift_right_logical(device, u)
        return LEVEL_START[u] + (lax.bitwise_xor(n, 1) if other else n)

    row, lane = iota((T_ROWS, 254), 0), iota((T_ROWS, 254), 1)
    want = jnp.where(row < 30, row + UPPER, -1)
    for u in range(3):
        want = jnp.where(row == OWN + u, node(u), want)
        want = jnp.where(row == SIBLING + u, node(u, True), want)
        want = jnp.where(row == OWN_UPPER + u, node(u + 3), want)
    pick_t = hot(lane == want)
    row, lane = iota((C_ROWS, 254), 0), iota((C_ROWS, 254), 1)
    want = jnp.zeros((C_ROWS, 254), i32) - 1
    for u in range(7):
        want = jnp.where(row == u, node(u, u < 3), want)
    pick_c = hot(lane == want)

    def step(g, carry):
        for ref, pick, dest, rows in ((ut, pick_t, et, T_ROWS), (uc, pick_c, eu, C_ROWS)):
            block = ref[pl.ds(4 * g, 4)].reshape(256, 254)
            out = dot(pick, block, NT)
            for j in range(4):
                at = pl.multiple_of((4 * g + j) * rows, 8)
                dest[pl.ds(at, rows), :64] = out[:, 64 * j : 64 * j + 64]
        return carry

    lax.fori_loop(0, 16, step, 0, unroll=4)


def middle_kernel(recv, path, et, eu, send, ext, xs, gain):
    device = lax.axis_index("leaf")
    ext[...] = recv[:, 512:640].astype(f32)

    labels = jnp.concatenate(
        [jnp.transpose(ext[128 * i : 128 * i + 128, :])[64:65, :] for i in range(4)], axis=1
    )
    row, lane = iota((256, 512), 0), iota((256, 512), 1)
    wanted = ((row & 31) + 1).astype(f32)
    fits = lax.shift_right_logical(row, 5) == (lax.shift_right_logical(lane, 2) & 7)
    sums = dot(hot((labels == wanted) & fits), recv[:, 0:512])

    for g in range(16):
        rows = ext[32 * g : 32 * g + 16, :64]
        xs[8 * g : 8 * g + 8, :] = rows[:8] + rows[8:]
    first, n = 0, 16
    firsts = {3: 0}
    for u in range(3, 6):
        for m in range(n // 2):
            r = 8 * (first + 2 * m)
            e = LEVEL_START[u] - UPPER + 2 * m
            pair = jnp.concatenate([xs[r : r + 8, :], xs[r + 8 : r + 16, :]], axis=1)
            w = jnp.concatenate([own_matrix(et, e, T_ROWS), own_matrix(et, e + 1, T_ROWS)], axis=0)
            t = 8 * (first + n + m)
            xs[t : t + 8, :] = dot_pair(pair, w)
        first += n
        n //= 2
        firsts[u + 1] = first
    for u in range(7):
        if u < 3:
            partner = path[8 * u : 8 * u + 8, :]
        else:
            sib = lax.bitwise_xor(lax.shift_right_logical(device, u), 1)
            partner = xs[pl.ds(pl.multiple_of((firsts[u] + sib) * 8, 8), 8), :]
        gain[8 * u : 8 * u + 8, :] = dot_pair(partner, own_matrix(eu, u, C_ROWS))
    down = gain[48:56, :]
    for u in (5, 4, 3):
        w = own_matrix(et, OWN_UPPER + u - 3, T_ROWS)
        down = dot_pair(down, w, NT) + gain[8 * u : 8 * u + 8, :]
    lines = {}
    for u in (2, 1, 0):
        both = jnp.concatenate(
            [own_matrix(et, OWN + u, T_ROWS), own_matrix(et, SIBLING + u, T_ROWS)], axis=0
        )
        spread = dot_pair(down, both, NT)
        lines[u] = flat(spread[:, 64:] + gain[8 * u : 8 * u + 8, :])
        down = spread[:, :64]
    own_line = flat(down)
    z = device & 7
    last = iota((32, 512), 0) == 31
    for peer in range(8):
        x = lax.bitwise_xor(z, peer)
        line = jnp.where(x == 0, own_line, lines[0])
        line = jnp.where(x >= 2, lines[1], line)
        line = jnp.where(x >= 4, lines[2], line)
        block = jnp.where(last, line, sums[32 * peer : 32 * peer + 32])
        send[32 * peer : 32 * peer + 32, :] = block.astype(bf16)


def flat(x):
    return jnp.concatenate([x[v : v + 1] for v in range(8)], axis=1)


def final_kernel(recv, near_mine, near_other, et, tr, bases, perm, out, cpl, dwn, dn, tree):
    device = lax.axis_index("leaf")
    core = lax.axis_index("vec")
    z = device & 7
    total = jnp.zeros((32, 512), f32)
    levels = [jnp.zeros((1, 512), f32)] * 3
    for peer in range(8):
        block = recv[32 * peer : 32 * peer + 32, :].astype(f32)
        total = total + block
        x = lax.bitwise_xor(z, peer)
        line = block[31:32]
        for i, use in enumerate((x >= 4, (x >= 2) & (x < 4), x < 2)):
            levels[i] = levels[i] + jnp.where(use, line, 0.0)
    levels = jnp.concatenate(levels + [jnp.zeros((5, 512), f32)], axis=0)
    for v in range(8):
        cpl[pl.ds(v, 32, stride=8), :] = wide(total[:, 64 * v : 64 * v + 64])
        dwn[pl.ds(v, 8, stride=8), :] = wide(levels[:, 64 * v : 64 * v + 64])
    down = dot_pair(dwn[0:8, :64], own_matrix(et, OWN + 1, T_ROWS), NT) + dwn[8:16, :64]
    down = dot_pair(down, own_matrix(et, OWN, T_ROWS), NT) + dwn[16:24, :64]

    dn[240:248, :] = down + cpl[240:248, :64]
    n = 1
    while n < 16:
        off_parent = 32 - 2 * n
        n *= 2
        off = 32 - 2 * n
        for m in range(n // 2):
            r = 8 * (off_parent + m)
            w = tr[off + 2 * m : off + 2 * m + 2].reshape(128, 64)
            both = dot_pair(dn[r : r + 8, :], w, NT)
            t = 8 * (off + 2 * m)
            dn[t : t + 8, :] = both[:, :64] + cpl[t : t + 8, :64]
            dn[t + 8 : t + 16, :] = both[:, 64:] + cpl[t + 8 : t + 16, :64]
    for leaf in range(16):
        tree[:, LEAF * leaf : LEAF * leaf + LEAF] = dot(
            dn[8 * leaf : 8 * leaf + 8, :].astype(bf16), bases[leaf]
        )

    @pl.when(core == 0)
    def _():
        tree[:, :HALF] += near_mine[...]
        tree[:, HALF:] += near_other[...]

    @pl.when(core == 1)
    def _():
        tree[:, :HALF] += near_other[...]
        tree[:, HALF:] += near_mine[...]

    width = 512
    total = jnp.zeros((256, 256), f32)
    for b in range(COLS // width):
        cols = slice(b * width, (b + 1) * width)
        index = perm[:, cols]
        select = hot(iota((256, width), 0) == (index & 255))
        high = jnp.broadcast_to(lax.shift_right_logical(index, 8), (8, width))
        values = tree[:, cols]
        spread = jnp.concatenate(
            [jnp.where(high == q, values, 0.0) for q in range(32)], axis=0
        ).astype(bf16)
        total = total + dot(spread, select, NT)
    for q in range(32):
        out[:, 256 * q : 256 * q + 256] = total[8 * q : 8 * q + 8].astype(bf16)


def shards(
    points, vectors, leaf_order, leaf_bases, transfers, coupling_blocks,
    block_source, block_owner, block_target, up_transfer, up_coupling,
):
    peers = lax.axis_size("leaf")
    axes = ("leaf", "vec")
    vt, pt, send_a, send_b, send_c = call(
        gather_kernel,
        [((8, COLS), bf16), ((8, COLS), bf16), ((16, HALO), bf16), ((8, HALO), bf16), ((8, LOCAL), bf16)],
        [pltpu.VMEM((256, 256), bf16), pltpu.VMEM((128, 256), f32)],
        (points, vectors, leaf_order),
        2 * 384 * 256 * COLS, 1 << 20,
    )
    pairs_a, pairs_b, pairs_c = [], [], []
    for d in range(peers):
        pairs_c += [(2 * d, 2 * d + 1), (2 * d + 1, 2 * d)]
        if d + 1 < peers:
            pairs_a += [(2 * d + 1, 2 * d + 2), (2 * d + 2, 2 * d + 1)]
            pairs_b += [(2 * d, 2 * d + 2), (2 * d + 3, 2 * d + 1)]
    rec_c = lax.ppermute(send_c, axes, pairs_c)
    rec_a = lax.ppermute(send_a, axes, pairs_a)
    rec_b = lax.ppermute(send_b, axes, pairs_b)
    ut = jnp.transpose(up_transfer, (1, 2, 0))
    uc = jnp.transpose(up_coupling, (1, 2, 0))
    et, eu = call(
        matrices_kernel,
        [((64 * T_ROWS, 128), f32), ((64 * C_ROWS, 128), f32)],
        [],
        (ut, uc),
        2 * 8192 * 256 * 48, 8 << 20,
    )
    cf, path = call(
        coeff_kernel,
        [((256, 128), f32), ((32, 64), f32)],
        [],
        (vt, leaf_bases, transfers, et),
        2 * 512 * 512 * 256, 2 << 20,
    )
    (send,) = call(
        product_kernel,
        [((512, 640), bf16)],
        [pltpu.VMEM((1024, 128), f32), pltpu.VMEM((640, 256), bf16)],
        (
            cf, path, jnp.transpose(coupling_blocks, (1, 2, 0)),
            block_source.reshape(1, -1), block_owner.reshape(1, -1), block_target.reshape(1, -1),
            rec_a, rec_b, rec_c,
        ),
        2 * 512 * 256 * 640, 4 << 20,
        anywhere=3,
    )
    near_groups = [[xy * 8 + z for z in range(8)] for xy in range(peers // 8)]
    far_groups = [[xy * 8 + z for xy in range(peers // 8)] for z in range(8)]
    recv = lax.all_to_all(
        send, "leaf", split_axis=0, concat_axis=0, tiled=True, axis_index_groups=far_groups
    )
    vw, fs, ft, begun = call(
        near_setup_kernel,
        [((16, 6144), bf16), ((6144, 16), bf16), ((16, 6144), bf16), ((16, HALF), f32)],
        [pltpu.VMEM((8, 6144), f32)],
        (vt, pt, rec_a, rec_b, rec_c),
        2 * 40 * 512 * 512 * 256, 1 << 20, vmem=24,
    )
    (send,) = call(
        middle_kernel,
        [((256, 512), bf16)],
        [pltpu.VMEM((512, 128), f32), pltpu.VMEM((256, 64), f32), pltpu.VMEM((56, 64), f32)],
        (recv, path, et, eu),
        2 * 256 * 512 * 512, 2 << 20,
    )
    recv = lax.all_to_all(
        send, "leaf", split_axis=0, concat_axis=0, tiled=True, axis_index_groups=near_groups
    )
    near_mine, near_send = call(
        near_rest_kernel,
        [((8, HALF), f32), ((8, HALF), f32)],
        [pltpu.VMEM((16, HALF), f32)],
        (vw, fs, ft, begun),
        2 * 27 * 512 * 512 * 256, 1 << 20, vmem=24,
    )
    near_other = lax.ppermute(near_send, axes, pairs_c)
    (out,) = call(
        final_kernel,
        [((8, COLS), bf16)],
        [
            pltpu.VMEM((256, 128), f32), pltpu.VMEM((64, 128), f32),
            pltpu.VMEM((248, 64), f32), pltpu.VMEM((8, COLS), f32),
        ],
        (recv, near_mine, near_other, et, transfers, leaf_bases, leaf_order),
        2 * 256 * 256 * COLS, 8 << 20,
    )
    return out


def solution(mesh):
    return jax.shard_map(
        shards,
        mesh=mesh,
        in_specs=(
            P(None, "leaf"),
            P("vec", "leaf"),
            P("leaf", None),
            P("leaf", None, None),
            P("leaf", None, None),
            P("leaf", None, None),
            P("leaf"),
            P("leaf", None),
            P("leaf"),
            P(),
            P(),
        ),
        out_specs=P("vec", "leaf"),
        check_vma=False,
    )
```

```python
import jax
import jax.numpy as jnp
import ml_dtypes
from jax import lax
from jax.experimental import pallas as pl
from jax.experimental.pallas import tpu as pltpu
from jax.sharding import PartitionSpec as P

f32 = jnp.float32
bf16 = jnp.bfloat16
i32 = jnp.int32

LEAF = 512
COLS = 8192
HALO = 1024
LOCAL = 5120
HALF = 4096
NT = (((1,), (1,)), ((), ()))
TN = (((0,), (0,)), ((), ()))
SMOOTH_HI = float(ml_dtypes.bfloat16(0.0025))
SMOOTH_LO = float(ml_dtypes.bfloat16(0.0025 - SMOOTH_HI))
VM = pl.BlockSpec(memory_space=pltpu.VMEM)


def dot(a, b, dims=(((1,), (0,)), ((), ()))):
    return lax.dot_general(a, b, dims, preferred_element_type=f32)


def iota(shape, dim):
    return lax.broadcasted_iota(i32, shape, dim)


def hot(mask):
    return jnp.where(mask, 1.0, 0.0).astype(bf16)


def halves(x):
    hi = x.astype(bf16)
    lo = (x - hi.astype(f32)).astype(bf16)
    return jnp.concatenate([hi, lo], axis=0)


def wide(x):
    return jnp.concatenate([x, jnp.zeros_like(x)], axis=1)


def dot_pair(x, w, dims=(((1,), (0,)), ((), ()))):
    y = dot(halves(x), w, dims)
    n = x.shape[0]
    return y[:n] + y[n:]


ANY = pl.BlockSpec(memory_space=pl.ANY)
SPEC = {"v": VM, "a": ANY, "h": pl.BlockSpec(memory_space=pltpu.HBM)}


def call(kernel, outs, scratch, args, kinds, flops, nbytes, vmem=16):
    ins, results = kinds.split(">")
    return pl.pallas_call(
        kernel,
        out_shape=[jax.ShapeDtypeStruct(s, d) for s, d in outs],
        in_specs=[SPEC[k] for k in ins],
        out_specs=[SPEC[k] for k in results],
        scratch_shapes=scratch,
        compiler_params=pltpu.CompilerParams(vmem_limit_bytes=vmem << 20),
        cost_estimate=pl.CostEstimate(flops=flops, bytes_accessed=nbytes, transcendentals=0),
    )(*args)


def fetch(sems, *pairs):
    copies = [
        pltpu.make_async_copy(src, dst, sems.at[i]) for i, (src, dst) in enumerate(pairs)
    ]
    for copy in copies:
        copy.start()
    return copies


def gather_kernel(
    pts_in, vec_in, perm_in, vt, pt, send_a, send_b, send_c, pts, vec, perm, dv, dp, sems
):
    core = lax.axis_index("vec")
    for copy in fetch(sems, (perm_in, perm), (vec_in, vec), (pts_in, pts)):
        copy.wait()
    for m in range(16):
        a, b = 512 * m, 512 * m + 256
        dv[16 * m : 16 * m + 16, :] = jnp.concatenate(
            [vec[:, a : a + 256], vec[:, b : b + 256]], axis=0
        )
        three = pts[:, a : a + 512].astype(f32)
        four = jnp.concatenate([three, jnp.zeros((1, 512), f32)], axis=0)
        dp[8 * m : 8 * m + 8, :] = jnp.concatenate([four[:, :256], four[:, 256:]], axis=0)
    data_v = dv[...]
    data_p = dp[...].astype(bf16)
    width = 512
    for n in range(COLS // width):
        cols = slice(n * width, (n + 1) * width)
        index = perm[:, cols]
        low = index & 255
        high = jnp.broadcast_to(lax.shift_right_logical(index, 8), (8, width))
        select = hot(iota((256, width), 0) == low)
        got = dot(data_v, select)
        out = got[:8]
        for q in range(1, 32):
            out = jnp.where(high == q, got[8 * q : 8 * q + 8], out)
        vt[:, cols] = out.astype(bf16)
        got = dot(data_p, select)
        pair = high - iota((8, width), 0) // 4
        out = jnp.zeros((8, width), f32)
        for m in range(16):
            out = jnp.where(pair == 2 * m, got[8 * m : 8 * m + 8], out)
        out = out[:4] + out[4:]
        pt[:, cols] = jnp.concatenate([out, jnp.zeros((4, width), f32)], axis=0).astype(bf16)
    first, last = slice(0, HALO), slice(COLS - HALO, COLS)

    @pl.when(core == 0)
    def _():
        send_a[0:8, :] = vt[:, first]
        send_a[8:16, :] = pt[:, first]
        send_b[...] = vt[:, last]
        send_c[...] = vt[:, COLS - LOCAL :]

    @pl.when(core == 1)
    def _():
        send_a[0:8, :] = vt[:, last]
        send_a[8:16, :] = pt[:, last]
        send_b[...] = vt[:, first]
        send_c[...] = vt[:, :LOCAL]


def coeff_kernel(vt, bases, tr, mats, cf, path):
    cf[248:256, :] = jnp.zeros((8, 128), f32)
    for leaf in range(16):
        cf[8 * leaf : 8 * leaf + 8, :64] = dot(
            vt[:, LEAF * leaf : LEAF * leaf + LEAF], bases[leaf], NT
        )
    off, n = 0, 16
    while n > 1:
        for m in range(n // 2):
            r = 8 * (off + 2 * m)
            pair = jnp.concatenate([cf[r : r + 8, :64], cf[r + 8 : r + 16, :64]], axis=1)
            w = tr[off + 2 * m : off + 2 * m + 2].reshape(128, 64)
            t = 8 * (off + n + m)
            cf[t : t + 8, :64] = dot_pair(pair, w)
        off += n
        n //= 2
    value = cf[240:248, :64]
    for u in range(3):
        path[8 * u : 8 * u + 8, :] = value
        value = dot_pair(value, own_matrix(mats, OWN + u))
    path[24:32, :] = value


def own_matrix(mats, row, count=1):
    return mats[64 * row : 64 * (row + count), :]


def product_kernel(cf, path, cp, bsrc, bown, btgt, seen_a, seen_b, seen_c, send, pick, prod):
    source = hot(iota((32, 256), 0) == bsrc[...])
    for v in range(8):
        mine = cf[pl.ds(v, 32, stride=8), :][:, :64].astype(bf16)
        chosen = dot(mine, source, TN)
        pick[pl.ds(v, 64, stride=8), :] = chosen[:, :128]
        pick[pl.ds(512 + v, 64, stride=8), :] = chosen[:, 128:]
    for half in range(2):
        lanes = slice(128 * half, 128 * half + 128)
        for pb in range(4):
            rows = slice(16 * pb, 16 * pb + 16)

            def step(k, acc):
                block = cp[k, rows, lanes].astype(f32)
                picked = pick[pl.ds(pl.multiple_of(512 * half + 8 * k, 8), 8), :]
                return tuple(acc[v] + picked[v : v + 1] * block for v in range(8))

            acc = lax.fori_loop(0, 64, step, (jnp.zeros((16, 128), f32),) * 8, unroll=8)
            for v in range(8):
                top = 64 * v + 16 * pb
                prod[top : top + 16, lanes] = acc[v].astype(bf16)
    prod[512:576, :] = jnp.zeros((64, 256), bf16)
    prod[576:640, :] = jnp.broadcast_to((btgt[...] + 1).astype(f32), (64, 256)).astype(bf16)
    owner = bown[...]
    owner_f = owner.astype(f32)
    column = jnp.transpose(jnp.broadcast_to(owner_f, (128, 256)))
    ranks = []
    for half in range(2):
        row = owner_f[:, 128 * half : 128 * half + 128]
        before = iota((256, 128), 0) < iota((256, 128), 1) + 128 * half
        same = jnp.where((column == row) & before, 1.0, 0.0)
        ranks.append(jnp.sum(same, axis=0, keepdims=True))
    place = owner * 4 + jnp.concatenate(ranks, axis=1).astype(i32)
    top = path[24:32, :]
    high = top.astype(bf16).astype(f32)
    extra = jnp.concatenate([high, top - high, jnp.zeros((16, 64), f32)], axis=0)
    extra = wide(extra)
    payload = prod[...]
    for part in range(2):
        rows = slice(256 * part, 256 * part + 256)
        slots = hot(iota((256, 256), 0) + 256 * part == place)
        out = dot(slots, payload, NT)
        send[rows, 0:512] = out[:, :512].astype(bf16)
        tail = out[:, 512:].reshape(8, 32, 128) + extra[None]
        send[rows, 512:640] = tail.reshape(256, 128).astype(bf16)


def split3(x):
    a = x.astype(bf16).astype(f32)
    b = (x - a).astype(bf16).astype(f32)
    return a, b, x - a - b


def near_window(ins, bufs, sems, leaves, vw, fs, ft, pw):
    core = lax.axis_index("vec")
    for copy in fetch(sems, *zip(ins, bufs)):
        copy.wait()
    vt, pt, rec_a, rec_b, rec_c = bufs

    @pl.when(core == 0)
    def _():
        vw[0:8, HALO:] = vt[:, :LOCAL]
        vw[8:16, HALO:] = rec_c[...]
        vw[0:8, :HALO] = rec_b[...]
        vw[8:16, :HALO] = rec_a[0:8, :]
        pw[:, HALO:] = pt[:, :LOCAL].astype(f32)
        pw[:, :HALO] = rec_a[8:16, :].astype(f32)

    @pl.when(core == 1)
    def _():
        vw[0:8, :LOCAL] = vt[:, COLS - LOCAL :]
        vw[8:16, :LOCAL] = rec_c[...]
        vw[0:8, LOCAL:] = rec_b[...]
        vw[8:16, LOCAL:] = rec_a[0:8, :]
        pw[:, :LOCAL] = pt[:, COLS - LOCAL :].astype(f32)
        pw[:, LOCAL:] = rec_a[8:16, :].astype(f32)

    for leaf in leaves:
        cols = slice(LEAF * leaf, LEAF * leaf + LEAF)
        p = pw[0:3, cols]
        norm = p[0:1] * p[0:1] + p[1:2] * p[1:2] + p[2:3] * p[2:3]
        parts = jnp.concatenate(split3(norm), axis=0)
        one = jnp.ones((3, LEAF), f32)
        two = jnp.ones((2, LEAF), f32)
        pad = jnp.zeros((5, LEAF), f32)
        source = jnp.concatenate([p, parts, one, two, pad], axis=0)
        smooth = jnp.where(iota((2, LEAF), 0) == 0, SMOOTH_HI, SMOOTH_LO)
        target = jnp.concatenate([-2.0 * p, one, parts, smooth, pad], axis=0)
        fs[cols, :] = jnp.transpose(source).astype(bf16)
        ft[:, cols] = target.astype(bf16)


def near_target(t, vw, fs, ft, acc):
    tc = slice(LEAF * t, LEAF * t + LEAF)
    to = slice(LEAF * (t - 2), LEAF * (t - 1))
    total = jnp.zeros((16, LEAF), f32)
    for s in range(t - 2, t + 3):
        if 2 <= s < t:
            continue
        sc = slice(LEAF * s, LEAF * s + LEAF)
        kernel = lax.rsqrt(dot(fs[sc, :], ft[:, tc])).astype(bf16)
        total = total + dot(vw[:, sc], kernel)
        if t < s < 10:
            so = slice(LEAF * (s - 2), LEAF * (s - 1))
            acc[:, so] += dot(vw[:, tc], kernel, NT)
    acc[:, to] += total


def near_first_kernel(*refs):
    ins, begun, bufs = refs[:5], refs[5], refs[6:11]
    vw, fs, ft, pw, acc, sems, out_sems = refs[11:]
    near_window(ins, bufs, sems, range(0, 8), vw, fs, ft, pw)
    acc[...] = jnp.zeros_like(acc)
    copies = []
    for t in range(2, 6):
        near_target(t, vw, fs, ft, acc)
        cols = slice(LEAF * (t - 2), LEAF * (t - 1) if t < 5 else HALF)
        copies += [pltpu.make_async_copy(acc.at[:, cols], begun.at[:, cols], out_sems.at[t - 2])]
        copies[-1].start()
    for copy in copies:
        copy.wait()


def near_rest_kernel(*refs):
    ins, begun, mine, other, bufs = refs[:5], refs[5], refs[6], refs[7], refs[8:13]
    vw, fs, ft, pw, acc, sems, begun_sem = refs[13:]
    first = pltpu.make_async_copy(begun, acc, begun_sem)
    first.start()
    near_window(ins, bufs, sems, range(6, 12), vw, fs, ft, pw)
    first.wait()
    for t in range(6, 10):
        near_target(t, vw, fs, ft, acc)
    mine[...] = acc[0:8, :] * (8.0 / LEAF)
    other[...] = acc[8:16, :] * (8.0 / LEAF)


LEVEL_START = [256 - (256 >> u) for u in range(7)]
UPPER = 224
OWN = 30
SIBLING = 33
OWN_UPPER = 36
COUPLING = 40
MATRICES = 48
T_ROWS = 40
C_ROWS = 8


def matrices_kernel(ut, uc, mats, et, eu):
    device = lax.axis_index("leaf")

    def node(u, other=False):
        n = lax.shift_right_logical(device, u)
        return LEVEL_START[u] + (lax.bitwise_xor(n, 1) if other else n)

    row, lane = iota((T_ROWS, 254), 0), iota((T_ROWS, 254), 1)
    want = jnp.where(row < 30, row + UPPER, -1)
    for u in range(3):
        want = jnp.where(row == OWN + u, node(u), want)
        want = jnp.where(row == SIBLING + u, node(u, True), want)
        want = jnp.where(row == OWN_UPPER + u, node(u + 3), want)
    pick_t = hot(lane == want)
    row, lane = iota((C_ROWS, 254), 0), iota((C_ROWS, 254), 1)
    want = jnp.zeros((C_ROWS, 254), i32) - 1
    for u in range(7):
        want = jnp.where(row == u, node(u, u < 3), want)
    pick_c = hot(lane == want)

    def step(g, carry):
        for ref, pick, dest, rows in ((ut, pick_t, et, T_ROWS), (uc, pick_c, eu, C_ROWS)):
            block = ref[pl.ds(4 * g, 4)].reshape(256, 254)
            out = dot(pick, block, NT)
            for j in range(4):
                at = pl.multiple_of((4 * g + j) * rows, 8)
                dest[pl.ds(at, rows), :64] = out[:, 64 * j : 64 * j + 64]
        return carry

    lax.fori_loop(0, 16, step, 0, unroll=4)
    for m in range(39):
        mats[64 * m : 64 * m + 64, :] = et[pl.ds(m, 64, stride=T_ROWS), :][:, :64].astype(bf16)
    for m in range(7):
        at = 64 * (COUPLING + m)
        mats[at : at + 64, :] = eu[pl.ds(m, 64, stride=C_ROWS), :][:, :64].astype(bf16)


def middle_kernel(recv_in, path_in, mats_in, send, recv, path, mats, ext, xs, gain, sems):
    device = lax.axis_index("leaf")
    for copy in fetch(sems, (recv_in, recv), (path_in, path), (mats_in, mats)):
        copy.wait()
    ext[...] = recv[:, 512:640].astype(f32)

    labels = jnp.concatenate(
        [jnp.transpose(ext[128 * i : 128 * i + 128, :])[64:65, :] for i in range(4)], axis=1
    )
    row, lane = iota((256, 512), 0), iota((256, 512), 1)
    wanted = ((row & 31) + 1).astype(f32)
    fits = lax.shift_right_logical(row, 5) == (lax.shift_right_logical(lane, 2) & 7)
    sums = dot(hot((labels == wanted) & fits), recv[:, 0:512])

    for g in range(16):
        rows = ext[32 * g : 32 * g + 16, :64]
        xs[8 * g : 8 * g + 8, :] = rows[:8] + rows[8:]
    first, n = 0, 16
    firsts = {3: 0}
    for u in range(3, 6):
        for m in range(n // 2):
            r = 8 * (first + 2 * m)
            e = LEVEL_START[u] - UPPER + 2 * m
            pair = jnp.concatenate([xs[r : r + 8, :], xs[r + 8 : r + 16, :]], axis=1)
            w = own_matrix(mats, e, 2)
            t = 8 * (first + n + m)
            xs[t : t + 8, :] = dot_pair(pair, w)
        first += n
        n //= 2
        firsts[u + 1] = first
    for u in range(7):
        if u < 3:
            partner = path[8 * u : 8 * u + 8, :]
        else:
            sib = lax.bitwise_xor(lax.shift_right_logical(device, u), 1)
            partner = xs[pl.ds(pl.multiple_of((firsts[u] + sib) * 8, 8), 8), :]
        gain[8 * u : 8 * u + 8, :] = dot_pair(partner, own_matrix(mats, COUPLING + u))
    down = gain[48:56, :]
    for u in (5, 4, 3):
        w = own_matrix(mats, OWN_UPPER + u - 3)
        down = dot_pair(down, w, NT) + gain[8 * u : 8 * u + 8, :]
    lines = {}
    for u in (2, 1, 0):
        both = jnp.concatenate(
            [own_matrix(mats, OWN + u), own_matrix(mats, SIBLING + u)], axis=0
        )
        spread = dot_pair(down, both, NT)
        lines[u] = flat(spread[:, 64:] + gain[8 * u : 8 * u + 8, :])
        down = spread[:, :64]
    own_line = flat(down)
    z = device & 7
    last = iota((32, 512), 0) == 31
    for peer in range(8):
        x = lax.bitwise_xor(z, peer)
        line = jnp.where(x == 0, own_line, lines[0])
        line = jnp.where(x >= 2, lines[1], line)
        line = jnp.where(x >= 4, lines[2], line)
        block = jnp.where(last, line, sums[32 * peer : 32 * peer + 32])
        send[32 * peer : 32 * peer + 32, :] = block.astype(bf16)


def flat(x):
    return jnp.concatenate([x[v : v + 1] for v in range(8)], axis=1)


def final_kernel(
    recv_in, mine_in, other_in, mats_in, tr, bases, perm_in, out,
    recv, near_mine, near_other, mats, perm, cpl, dwn, dn, tree, sems,
):
    copies = fetch(
        sems,
        (recv_in, recv),
        (mats_in.at[64 * OWN : 64 * OWN + 128], mats),
        (mine_in, near_mine),
        (other_in, near_other),
        (perm_in, perm),
    )
    for copy in copies:
        copy.wait()
    device = lax.axis_index("leaf")
    core = lax.axis_index("vec")
    z = device & 7
    total = jnp.zeros((32, 512), f32)
    levels = [jnp.zeros((1, 512), f32)] * 3
    for peer in range(8):
        block = recv[32 * peer : 32 * peer + 32, :].astype(f32)
        total = total + block
        x = lax.bitwise_xor(z, peer)
        line = block[31:32]
        for i, use in enumerate((x >= 4, (x >= 2) & (x < 4), x < 2)):
            levels[i] = levels[i] + jnp.where(use, line, 0.0)
    levels = jnp.concatenate(levels + [jnp.zeros((5, 512), f32)], axis=0)
    for v in range(8):
        cpl[pl.ds(v, 32, stride=8), :] = wide(total[:, 64 * v : 64 * v + 64])
        dwn[pl.ds(v, 8, stride=8), :] = wide(levels[:, 64 * v : 64 * v + 64])
    down = dot_pair(dwn[0:8, :64], own_matrix(mats, 1), NT) + dwn[8:16, :64]
    down = dot_pair(down, own_matrix(mats, 0), NT) + dwn[16:24, :64]

    dn[240:248, :] = down + cpl[240:248, :64]
    n = 1
    while n < 16:
        off_parent = 32 - 2 * n
        n *= 2
        off = 32 - 2 * n
        for m in range(n // 2):
            r = 8 * (off_parent + m)
            w = tr[off + 2 * m : off + 2 * m + 2].reshape(128, 64)
            both = dot_pair(dn[r : r + 8, :], w, NT)
            t = 8 * (off + 2 * m)
            dn[t : t + 8, :] = both[:, :64] + cpl[t : t + 8, :64]
            dn[t + 8 : t + 16, :] = both[:, 64:] + cpl[t + 8 : t + 16, :64]
    for leaf in range(16):
        tree[:, LEAF * leaf : LEAF * leaf + LEAF] = dot(
            dn[8 * leaf : 8 * leaf + 8, :].astype(bf16), bases[leaf]
        )

    @pl.when(core == 0)
    def _():
        tree[:, :HALF] += near_mine[...]
        tree[:, HALF:] += near_other[...]

    @pl.when(core == 1)
    def _():
        tree[:, :HALF] += near_other[...]
        tree[:, HALF:] += near_mine[...]

    width = 512
    total = jnp.zeros((256, 256), f32)
    for b in range(COLS // width):
        cols = slice(b * width, (b + 1) * width)
        index = perm[:, cols]
        select = hot(iota((256, width), 0) == (index & 255))
        high = jnp.broadcast_to(lax.shift_right_logical(index, 8), (8, width))
        values = tree[:, cols]
        spread = jnp.concatenate(
            [jnp.where(high == q, values, 0.0) for q in range(32)], axis=0
        ).astype(bf16)
        total = total + dot(spread, select, NT)
    for q in range(32):
        out[:, 256 * q : 256 * q + 256] = total[8 * q : 8 * q + 8].astype(bf16)


def shards(
    points, vectors, leaf_order, leaf_bases, transfers, coupling_blocks,
    block_source, block_owner, block_target, up_transfer, up_coupling,
):
    peers = lax.axis_size("leaf")
    axes = ("leaf", "vec")
    vt, pt, send_a, send_b, send_c = call(
        gather_kernel,
        [((8, COLS), bf16), ((8, COLS), bf16), ((16, HALO), bf16), ((8, HALO), bf16), ((8, LOCAL), bf16)],
        [
            pltpu.VMEM((3, COLS), bf16), pltpu.VMEM((8, COLS), bf16), pltpu.VMEM((1, COLS), i32),
            pltpu.VMEM((256, 256), bf16), pltpu.VMEM((128, 256), f32), pltpu.SemaphoreType.DMA((3,)),
        ],
        (points, vectors, leaf_order), "hhh>vvvvv",
        2 * 384 * 256 * COLS, 1 << 20,
    )
    pairs_a, pairs_b, pairs_c = [], [], []
    for d in range(peers):
        pairs_c += [(2 * d, 2 * d + 1), (2 * d + 1, 2 * d)]
        if d + 1 < peers:
            pairs_a += [(2 * d + 1, 2 * d + 2), (2 * d + 2, 2 * d + 1)]
            pairs_b += [(2 * d, 2 * d + 2), (2 * d + 3, 2 * d + 1)]
    rec_c = lax.ppermute(send_c, axes, pairs_c)
    rec_a = lax.ppermute(send_a, axes, pairs_a)
    rec_b = lax.ppermute(send_b, axes, pairs_b)
    ut = jnp.transpose(up_transfer, (1, 2, 0))
    uc = jnp.transpose(up_coupling, (1, 2, 0))
    (mats,) = call(
        matrices_kernel,
        [((64 * MATRICES, 64), bf16)],
        [pltpu.VMEM((64 * T_ROWS, 128), f32), pltpu.VMEM((64 * C_ROWS, 128), f32)],
        (ut, uc), "vv>v",
        2 * 8192 * 256 * 48, 8 << 20,
    )
    cf, path = call(
        coeff_kernel,
        [((256, 128), f32), ((32, 64), f32)],
        [],
        (vt, leaf_bases, transfers, mats), "vvvv>vv",
        2 * 512 * 512 * 256, 2 << 20,
    )
    (send,) = call(
        product_kernel,
        [((512, 640), bf16)],
        [pltpu.VMEM((1024, 128), f32), pltpu.VMEM((640, 256), bf16)],
        (
            cf, path, jnp.transpose(coupling_blocks, (1, 2, 0)),
            block_source.reshape(1, -1), block_owner.reshape(1, -1), block_target.reshape(1, -1),
            rec_a, rec_b, rec_c,
        ), "vvvvvvaaa>v",
        2 * 512 * 256 * 640, 4 << 20,
    )
    near_groups = [[xy * 8 + z for z in range(8)] for xy in range(peers // 8)]
    far_groups = [[xy * 8 + z for xy in range(peers // 8)] for z in range(8)]
    recv = lax.all_to_all(
        send, "leaf", split_axis=0, concat_axis=0, tiled=True, axis_index_groups=far_groups
    )
    buffers = [
        pltpu.VMEM((8, COLS), bf16), pltpu.VMEM((8, COLS), bf16), pltpu.VMEM((16, HALO), bf16),
        pltpu.VMEM((8, HALO), bf16), pltpu.VMEM((8, LOCAL), bf16),
        pltpu.VMEM((16, 6144), bf16), pltpu.VMEM((6144, 16), bf16), pltpu.VMEM((16, 6144), bf16),
        pltpu.VMEM((8, 6144), f32), pltpu.VMEM((16, HALF), f32), pltpu.SemaphoreType.DMA((5,)),
    ]
    (begun,) = call(
        near_first_kernel,
        [((16, HALF), f32)],
        buffers + [pltpu.SemaphoreType.DMA((4,))],
        (vt, pt, rec_a, rec_b, rec_c), "aaaaa>h",
        2 * 40 * 512 * 512 * 256, 1 << 20, vmem=24,
    )
    (send,) = call(
        middle_kernel,
        [((256, 512), bf16)],
        [
            pltpu.VMEM((512, 640), bf16), pltpu.VMEM((32, 64), f32),
            pltpu.VMEM((64 * MATRICES, 64), bf16), pltpu.VMEM((512, 128), f32),
            pltpu.VMEM((256, 64), f32), pltpu.VMEM((56, 64), f32), pltpu.SemaphoreType.DMA((3,)),
        ],
        (recv, path, mats), "aaa>v",
        2 * 256 * 512 * 512, 2 << 20,
    )
    recv = lax.all_to_all(
        send, "leaf", split_axis=0, concat_axis=0, tiled=True, axis_index_groups=near_groups
    )
    near_mine, near_send = call(
        near_rest_kernel,
        [((8, HALF), f32), ((8, HALF), f32)],
        buffers + [pltpu.SemaphoreType.DMA(())],
        (vt, pt, rec_a, rec_b, rec_c, begun), "aaaaah>vv",
        2 * 27 * 512 * 512 * 256, 1 << 20, vmem=24,
    )
    near_other = lax.ppermute(near_send, axes, pairs_c)
    (out,) = call(
        final_kernel,
        [((8, COLS), bf16)],
        [
            pltpu.VMEM((256, 512), bf16), pltpu.VMEM((8, HALF), f32), pltpu.VMEM((8, HALF), f32),
            pltpu.VMEM((128, 64), bf16), pltpu.VMEM((1, COLS), i32),
            pltpu.VMEM((256, 128), f32), pltpu.VMEM((64, 128), f32),
            pltpu.VMEM((248, 64), f32), pltpu.VMEM((8, COLS), f32), pltpu.SemaphoreType.DMA((5,)),
        ],
        (recv, near_mine, near_other, mats, transfers, leaf_bases, leaf_order), "aaaavvh>v",
        2 * 256 * 256 * COLS, 8 << 20,
    )
    return out


def solution(mesh):
    return jax.shard_map(
        shards,
        mesh=mesh,
        in_specs=(
            P(None, "leaf"),
            P("vec", "leaf"),
            P("leaf", None),
            P("leaf", None, None),
            P("leaf", None, None),
            P("leaf", None, None),
            P("leaf"),
            P("leaf", None),
            P("leaf"),
            P(),
            P(),
        ),
        out_specs=P("vec", "leaf"),
        check_vma=False,
    )
```

```python
import jax
import jax.numpy as jnp
import ml_dtypes
from jax import lax
from jax.experimental import pallas as pl
from jax.experimental.pallas import tpu as pltpu
from jax.sharding import PartitionSpec as P

f32 = jnp.float32
bf16 = jnp.bfloat16
i32 = jnp.int32

LEAF = 512
COLS = 8192
HALO = 1024
LOCAL = 5120
HALF = 4096
NT = (((1,), (1,)), ((), ()))
TN = (((0,), (0,)), ((), ()))
SMOOTH_HI = float(ml_dtypes.bfloat16(0.0025))
SMOOTH_LO = float(ml_dtypes.bfloat16(0.0025 - SMOOTH_HI))
VM = pl.BlockSpec(memory_space=pltpu.VMEM)


def dot(a, b, dims=(((1,), (0,)), ((), ()))):
    return lax.dot_general(a, b, dims, preferred_element_type=f32)


def iota(shape, dim):
    return lax.broadcasted_iota(i32, shape, dim)


def hot(mask):
    return jnp.where(mask, 1.0, 0.0).astype(bf16)


def halves(x):
    hi = x.astype(bf16)
    lo = (x - hi.astype(f32)).astype(bf16)
    return jnp.concatenate([hi, lo], axis=0)


def wide(x):
    return jnp.concatenate([x, jnp.zeros_like(x)], axis=1)


def dot_pair(x, w, dims=(((1,), (0,)), ((), ()))):
    y = dot(halves(x), w, dims)
    n = x.shape[0]
    return y[:n] + y[n:]


ANY = pl.BlockSpec(memory_space=pl.ANY)
SPEC = {"v": VM, "a": ANY, "h": pl.BlockSpec(memory_space=pltpu.HBM)}


def call(kernel, outs, scratch, args, kinds, flops, nbytes, vmem=16):
    ins, results = kinds.split(">")
    return pl.pallas_call(
        kernel,
        out_shape=[jax.ShapeDtypeStruct(s, d) for s, d in outs],
        in_specs=[SPEC[k] for k in ins],
        out_specs=[SPEC[k] for k in results],
        scratch_shapes=scratch,
        compiler_params=pltpu.CompilerParams(vmem_limit_bytes=vmem << 20),
        cost_estimate=pl.CostEstimate(flops=flops, bytes_accessed=nbytes, transcendentals=0),
    )(*args)


def fetch(sems, *pairs):
    copies = [
        pltpu.make_async_copy(src, dst, sems.at[i]) for i, (src, dst) in enumerate(pairs)
    ]
    for copy in copies:
        copy.start()
    return copies


def gather_kernel(
    pts_in, vec_in, perm_in, vt, pt, send_a, send_b, send_c, pts, vec, perm, dv, dp, sems
):
    core = lax.axis_index("vec")
    for copy in fetch(sems, (perm_in, perm), (vec_in, vec), (pts_in, pts)):
        copy.wait()
    for m in range(16):
        a, b = 512 * m, 512 * m + 256
        dv[16 * m : 16 * m + 16, :] = jnp.concatenate(
            [vec[:, a : a + 256], vec[:, b : b + 256]], axis=0
        )
        three = pts[:, a : a + 512].astype(f32)
        four = jnp.concatenate([three, jnp.zeros((1, 512), f32)], axis=0)
        dp[8 * m : 8 * m + 8, :] = jnp.concatenate([four[:, :256], four[:, 256:]], axis=0)
    data_v = dv[...]
    data_p = dp[...].astype(bf16)
    width = 512
    for n in range(COLS // width):
        cols = slice(n * width, (n + 1) * width)
        index = perm[:, cols]
        low = index & 255
        high = jnp.broadcast_to(lax.shift_right_logical(index, 8), (8, width))
        select = hot(iota((256, width), 0) == low)
        got = dot(data_v, select)
        out = got[:8]
        for q in range(1, 32):
            out = jnp.where(high == q, got[8 * q : 8 * q + 8], out)
        vt[:, cols] = out.astype(bf16)
        got = dot(data_p, select)
        pair = high - iota((8, width), 0) // 4
        out = jnp.zeros((8, width), f32)
        for m in range(16):
            out = jnp.where(pair == 2 * m, got[8 * m : 8 * m + 8], out)
        out = out[:4] + out[4:]
        pt[:, cols] = jnp.concatenate([out, jnp.zeros((4, width), f32)], axis=0).astype(bf16)
    first, last = slice(0, HALO), slice(COLS - HALO, COLS)

    @pl.when(core == 0)
    def _():
        send_a[0:8, :] = vt[:, first]
        send_a[8:16, :] = pt[:, first]
        send_b[...] = vt[:, last]
        send_c[...] = vt[:, COLS - LOCAL :]

    @pl.when(core == 1)
    def _():
        send_a[0:8, :] = vt[:, last]
        send_a[8:16, :] = pt[:, last]
        send_b[...] = vt[:, first]
        send_c[...] = vt[:, :LOCAL]


def coeff_kernel(vt, bases, tr, mats, cf, path):
    cf[248:256, :] = jnp.zeros((8, 128), f32)
    for leaf in range(16):
        cf[8 * leaf : 8 * leaf + 8, :64] = dot(
            vt[:, LEAF * leaf : LEAF * leaf + LEAF], bases[leaf], NT
        )
    off, n = 0, 16
    while n > 1:
        for m in range(n // 2):
            r = 8 * (off + 2 * m)
            pair = jnp.concatenate([cf[r : r + 8, :64], cf[r + 8 : r + 16, :64]], axis=1)
            w = tr[off + 2 * m : off + 2 * m + 2].reshape(128, 64)
            t = 8 * (off + n + m)
            cf[t : t + 8, :64] = dot_pair(pair, w)
        off += n
        n //= 2
    value = cf[240:248, :64]
    for u in range(3):
        path[8 * u : 8 * u + 8, :] = value
        value = dot_pair(value, own_matrix(mats, OWN + u))
    path[24:32, :] = value


def own_matrix(mats, row, count=1):
    return mats[64 * row : 64 * (row + count), :]


def product_kernel(
    cf, path, cp, bsrc, bown, btgt, halo_a, halo_b, seen_c, send, send_a, send_b, pick, prod
):
    send_a[...] = halo_a[...]
    send_b[...] = halo_b[...]
    source = hot(iota((32, 256), 0) == bsrc[...])
    for v in range(8):
        mine = cf[pl.ds(v, 32, stride=8), :][:, :64].astype(bf16)
        chosen = dot(mine, source, TN)
        pick[pl.ds(v, 64, stride=8), :] = chosen[:, :128]
        pick[pl.ds(512 + v, 64, stride=8), :] = chosen[:, 128:]
    for half in range(2):
        lanes = slice(128 * half, 128 * half + 128)
        for pb in range(4):
            rows = slice(16 * pb, 16 * pb + 16)

            def step(k, acc):
                block = cp[k, rows, lanes].astype(f32)
                picked = pick[pl.ds(pl.multiple_of(512 * half + 8 * k, 8), 8), :]
                return tuple(acc[v] + picked[v : v + 1] * block for v in range(8))

            acc = lax.fori_loop(0, 64, step, (jnp.zeros((16, 128), f32),) * 8, unroll=8)
            for v in range(8):
                top = 64 * v + 16 * pb
                prod[top : top + 16, lanes] = acc[v].astype(bf16)
    prod[512:576, :] = jnp.zeros((64, 256), bf16)
    prod[576:640, :] = jnp.broadcast_to((btgt[...] + 1).astype(f32), (64, 256)).astype(bf16)
    owner = bown[...]
    owner_f = owner.astype(f32)
    column = jnp.transpose(jnp.broadcast_to(owner_f, (128, 256)))
    ranks = []
    for half in range(2):
        row = owner_f[:, 128 * half : 128 * half + 128]
        before = iota((256, 128), 0) < iota((256, 128), 1) + 128 * half
        same = jnp.where((column == row) & before, 1.0, 0.0)
        ranks.append(jnp.sum(same, axis=0, keepdims=True))
    place = owner * 4 + jnp.concatenate(ranks, axis=1).astype(i32)
    top = path[24:32, :]
    high = top.astype(bf16).astype(f32)
    extra = jnp.concatenate([high, top - high, jnp.zeros((16, 64), f32)], axis=0)
    extra = wide(extra)
    payload = prod[...]
    for part in range(2):
        rows = slice(256 * part, 256 * part + 256)
        slots = hot(iota((256, 256), 0) + 256 * part == place)
        out = dot(slots, payload, NT)
        send[rows, 0:512] = out[:, :512].astype(bf16)
        tail = out[:, 512:].reshape(8, 32, 128) + extra[None]
        send[rows, 512:640] = tail.reshape(256, 128).astype(bf16)


def split3(x):
    a = x.astype(bf16).astype(f32)
    b = (x - a).astype(bf16).astype(f32)
    return a, b, x - a - b


def leaf_cols(leaf):
    return slice(LEAF * leaf, LEAF * leaf + LEAF)


def load_window(vt, pt, rec_c, halo, leaves, vw, pw):
    core = lax.axis_index("vec")
    for which in range(2):

        @pl.when(core == which)
        def _():
            for w in leaves:
                to = leaf_cols(w)
                if w < 2:
                    near_cols = leaf_cols(w if which == 0 else 1 - w)
                    vw[0:8, to] = halo[1][:, near_cols]
                    vw[8:16, to] = halo[0][0:8, near_cols]
                    pw[:, to] = halo[0][8:16, near_cols].astype(f32)
                else:
                    local = leaf_cols(w - 2 if which == 0 else 17 - w)
                    vw[0:8, to] = vt[:, local]
                    vw[8:16, to] = rec_c[:, leaf_cols(w - 2 if which == 0 else 11 - w)]
                    pw[:, to] = pt[:, local].astype(f32)


def features(leaves, pw, fs, ft):
    for leaf in leaves:
        cols = leaf_cols(leaf)
        p = pw[0:3, cols]
        norm = p[0:1] * p[0:1] + p[1:2] * p[1:2] + p[2:3] * p[2:3]
        parts = jnp.concatenate(split3(norm), axis=0)
        one = jnp.ones((3, LEAF), f32)
        two = jnp.ones((2, LEAF), f32)
        pad = jnp.zeros((5, LEAF), f32)
        source = jnp.concatenate([p, parts, one, two, pad], axis=0)
        smooth = jnp.where(iota((2, LEAF), 0) == 0, SMOOTH_HI, SMOOTH_LO)
        target = jnp.concatenate([-2.0 * p, one, parts, smooth, pad], axis=0)
        fs[cols, :] = jnp.transpose(source).astype(bf16)
        ft[:, cols] = target.astype(bf16)


def near_target(t, vw, fs, ft, acc):
    tc = leaf_cols(t)
    total = jnp.zeros((16, LEAF), f32)
    for s in range(t - 2, t + 3):
        if 2 <= s < t:
            continue
        sc = leaf_cols(s)
        kernel = lax.rsqrt(dot(fs[sc, :], ft[:, tc])).astype(bf16)
        total = total + dot(vw[:, sc], kernel)
        if t < s < 10:
            acc[:, leaf_cols(s - 2)] += dot(vw[:, tc], kernel, NT)
    acc[:, leaf_cols(t - 2)] += total


SPLIT = 5


def near_first_kernel(
    vt_in, pt_in, c_in, begun, vt, pt, rec_c, vw, fs, ft, pw, acc, sems, out_sems
):
    for copy in fetch(sems, (vt_in, vt), (pt_in, pt), (c_in, rec_c)):
        copy.wait()
    load_window(vt, pt, rec_c, None, range(SPLIT, 12), vw, pw)
    features(range(SPLIT, 12), pw, fs, ft)
    acc[...] = jnp.zeros_like(acc)
    copies = []
    for t in range(SPLIT, 10):
        near_target(t, vw, fs, ft, acc)
        src, dst = acc.at[:, leaf_cols(t - 2)], begun.at[:, leaf_cols(t - SPLIT)]
        copies += [pltpu.make_async_copy(src, dst, out_sems.at[t - SPLIT])]
        copies[-1].start()
    for copy in copies:
        copy.wait()


def near_rest_kernel(
    vt_in, pt_in, c_in, a_in, b_in, begun, mine, other,
    vt, pt, rec_c, vw, fs, ft, pw, acc, sems, rec_a, rec_b,
):
    left = LEAF * (SPLIT - 2)
    copies = fetch(
        sems, (vt_in, vt), (pt_in, pt), (c_in, rec_c), (a_in, rec_a), (b_in, rec_b),
        (begun, acc.at[:, left:]),
    )
    acc[:, :left] = jnp.zeros((16, left), f32)
    for copy in copies[:5]:
        copy.wait()
    load_window(vt, pt, rec_c, (rec_a, rec_b), range(0, SPLIT + 2), vw, pw)
    features(range(0, SPLIT + 2), pw, fs, ft)
    copies[5].wait()
    for t in range(2, SPLIT):
        near_target(t, vw, fs, ft, acc)
    core = lax.axis_index("vec")
    for which in range(2):

        @pl.when(core == which)
        def _():
            for i in range(8):
                to = leaf_cols(i if which == 0 else 7 - i)
                mine[:, to] = acc[0:8, leaf_cols(i)] * (8.0 / LEAF)
                other[:, to] = acc[8:16, leaf_cols(i)] * (8.0 / LEAF)


LEVEL_START = [256 - (256 >> u) for u in range(7)]
UPPER = 224
OWN = 30
SIBLING = 33
OWN_UPPER = 36
T_ROWS = 40
C_ROWS = 8


def node(u, other=False):
    n = lax.shift_right_logical(lax.axis_index("leaf"), u)
    return LEVEL_START[u] + (lax.bitwise_xor(n, 1) if other else n)


def pick_matrices(table, want, rows, count, mats, buf):
    pick = hot(iota((rows, 254), 1) == want)

    def step(g, carry):
        out = dot(pick, table[pl.ds(4 * g, 4)].reshape(256, 254), NT)
        for j in range(4):
            at = pl.multiple_of((4 * g + j) * rows, 8)
            buf[pl.ds(at, rows), :64] = out[:, 64 * j : 64 * j + 64]
        return carry

    lax.fori_loop(0, 16, step, 0, unroll=4)
    for m in range(count):
        mats[64 * m : 64 * m + 64, :] = buf[pl.ds(m, 64, stride=rows), :][:, :64].astype(bf16)


def transfers_kernel(ut, mats, buf):
    row = iota((T_ROWS, 254), 0)
    want = jnp.where(row < 30, row + UPPER, -1)
    for u in range(3):
        want = jnp.where(row == OWN + u, node(u), want)
        want = jnp.where(row == SIBLING + u, node(u, True), want)
        want = jnp.where(row == OWN_UPPER + u, node(u + 3), want)
    pick_matrices(ut, want, T_ROWS, 39, mats, buf)


def couplings_kernel(uc, seen, mats, buf):
    row = iota((C_ROWS, 254), 0)
    want = jnp.zeros((C_ROWS, 254), i32) - 1
    for u in range(7):
        want = jnp.where(row == u, node(u, u < 3), want)
    pick_matrices(uc, want, C_ROWS, 7, mats, buf)


def middle_kernel(
    recv_in, path_in, mats_in, coup_in, send, recv, path, mats, coup, ext, xs, gain, sems
):
    device = lax.axis_index("leaf")
    for copy in fetch(
        sems, (recv_in, recv), (path_in, path), (mats_in, mats), (coup_in, coup)
    ):
        copy.wait()
    ext[...] = recv[:, 512:640].astype(f32)

    labels = jnp.concatenate(
        [jnp.transpose(ext[128 * i : 128 * i + 128, :])[64:65, :] for i in range(4)], axis=1
    )
    row, lane = iota((256, 512), 0), iota((256, 512), 1)
    wanted = ((row & 31) + 1).astype(f32)
    fits = lax.shift_right_logical(row, 5) == (lax.shift_right_logical(lane, 2) & 7)
    sums = dot(hot((labels == wanted) & fits), recv[:, 0:512])

    for g in range(16):
        rows = ext[32 * g : 32 * g + 16, :64]
        xs[8 * g : 8 * g + 8, :] = rows[:8] + rows[8:]
    first, n = 0, 16
    firsts = {3: 0}
    for u in range(3, 6):
        for m in range(n // 2):
            r = 8 * (first + 2 * m)
            e = LEVEL_START[u] - UPPER + 2 * m
            pair = jnp.concatenate([xs[r : r + 8, :], xs[r + 8 : r + 16, :]], axis=1)
            w = own_matrix(mats, e, 2)
            t = 8 * (first + n + m)
            xs[t : t + 8, :] = dot_pair(pair, w)
        first += n
        n //= 2
        firsts[u + 1] = first
    for u in range(7):
        if u < 3:
            partner = path[8 * u : 8 * u + 8, :]
        else:
            sib = lax.bitwise_xor(lax.shift_right_logical(device, u), 1)
            partner = xs[pl.ds(pl.multiple_of((firsts[u] + sib) * 8, 8), 8), :]
        gain[8 * u : 8 * u + 8, :] = dot_pair(partner, own_matrix(coup, u))
    down = gain[48:56, :]
    for u in (5, 4, 3):
        w = own_matrix(mats, OWN_UPPER + u - 3)
        down = dot_pair(down, w, NT) + gain[8 * u : 8 * u + 8, :]
    lines = {}
    for u in (2, 1, 0):
        both = jnp.concatenate(
            [own_matrix(mats, OWN + u), own_matrix(mats, SIBLING + u)], axis=0
        )
        spread = dot_pair(down, both, NT)
        lines[u] = flat(spread[:, 64:] + gain[8 * u : 8 * u + 8, :])
        down = spread[:, :64]
    own_line = flat(down)
    z = device & 7
    last = iota((32, 512), 0) == 31
    for peer in range(8):
        x = lax.bitwise_xor(z, peer)
        line = jnp.where(x == 0, own_line, lines[0])
        line = jnp.where(x >= 2, lines[1], line)
        line = jnp.where(x >= 4, lines[2], line)
        block = jnp.where(last, line, sums[32 * peer : 32 * peer + 32])
        send[32 * peer : 32 * peer + 32, :] = block.astype(bf16)


def flat(x):
    return jnp.concatenate([x[v : v + 1] for v in range(8)], axis=1)


def final_kernel(
    recv_in, mine_in, other_in, mats_in, tr, bases, perm_in, out,
    recv, near_mine, near_other, mats, perm, cpl, dwn, dn, tree, sems,
):
    copies = fetch(
        sems,
        (recv_in, recv),
        (mats_in.at[64 * OWN : 64 * OWN + 128], mats),
        (mine_in, near_mine),
        (other_in, near_other),
        (perm_in, perm),
    )
    for copy in copies:
        copy.wait()
    device = lax.axis_index("leaf")
    core = lax.axis_index("vec")
    z = device & 7
    total = jnp.zeros((32, 512), f32)
    levels = [jnp.zeros((1, 512), f32)] * 3
    for peer in range(8):
        block = recv[32 * peer : 32 * peer + 32, :].astype(f32)
        total = total + block
        x = lax.bitwise_xor(z, peer)
        line = block[31:32]
        for i, use in enumerate((x >= 4, (x >= 2) & (x < 4), x < 2)):
            levels[i] = levels[i] + jnp.where(use, line, 0.0)
    levels = jnp.concatenate(levels + [jnp.zeros((5, 512), f32)], axis=0)
    for v in range(8):
        cpl[pl.ds(v, 32, stride=8), :] = wide(total[:, 64 * v : 64 * v + 64])
        dwn[pl.ds(v, 8, stride=8), :] = wide(levels[:, 64 * v : 64 * v + 64])
    down = dot_pair(dwn[0:8, :64], own_matrix(mats, 1), NT) + dwn[8:16, :64]
    down = dot_pair(down, own_matrix(mats, 0), NT) + dwn[16:24, :64]

    dn[240:248, :] = down + cpl[240:248, :64]
    n = 1
    while n < 16:
        off_parent = 32 - 2 * n
        n *= 2
        off = 32 - 2 * n
        for m in range(n // 2):
            r = 8 * (off_parent + m)
            w = tr[off + 2 * m : off + 2 * m + 2].reshape(128, 64)
            both = dot_pair(dn[r : r + 8, :], w, NT)
            t = 8 * (off + 2 * m)
            dn[t : t + 8, :] = both[:, :64] + cpl[t : t + 8, :64]
            dn[t + 8 : t + 16, :] = both[:, 64:] + cpl[t + 8 : t + 16, :64]
    for leaf in range(16):
        tree[:, LEAF * leaf : LEAF * leaf + LEAF] = dot(
            dn[8 * leaf : 8 * leaf + 8, :].astype(bf16), bases[leaf]
        )

    @pl.when(core == 0)
    def _():
        tree[:, :HALF] += near_mine[...]
        tree[:, HALF:] += near_other[...]

    @pl.when(core == 1)
    def _():
        tree[:, :HALF] += near_other[...]
        tree[:, HALF:] += near_mine[...]

    width = 512
    total = jnp.zeros((256, 256), f32)
    for b in range(COLS // width):
        cols = slice(b * width, (b + 1) * width)
        index = perm[:, cols]
        select = hot(iota((256, width), 0) == (index & 255))
        high = jnp.broadcast_to(lax.shift_right_logical(index, 8), (8, width))
        values = tree[:, cols]
        spread = jnp.concatenate(
            [jnp.where(high == q, values, 0.0) for q in range(32)], axis=0
        ).astype(bf16)
        total = total + dot(spread, select, NT)
    for q in range(32):
        out[:, 256 * q : 256 * q + 256] = total[8 * q : 8 * q + 8].astype(bf16)


def shards(
    points, vectors, leaf_order, leaf_bases, transfers, coupling_blocks,
    block_source, block_owner, block_target, up_transfer, up_coupling,
):
    peers = lax.axis_size("leaf")
    axes = ("leaf", "vec")
    vt, pt, send_a, send_b, send_c = call(
        gather_kernel,
        [((8, COLS), bf16), ((8, COLS), bf16), ((16, HALO), bf16), ((8, HALO), bf16), ((8, LOCAL), bf16)],
        [
            pltpu.VMEM((3, COLS), bf16), pltpu.VMEM((8, COLS), bf16), pltpu.VMEM((1, COLS), i32),
            pltpu.VMEM((256, 256), bf16), pltpu.VMEM((128, 256), f32), pltpu.SemaphoreType.DMA((3,)),
        ],
        (points, vectors, leaf_order), "hhh>vvvvv",
        2 * 384 * 256 * COLS, 1 << 20,
    )
    pairs_a, pairs_b, pairs_c = [], [], []
    for d in range(peers):
        pairs_c += [(2 * d, 2 * d + 1), (2 * d + 1, 2 * d)]
        if d + 1 < peers:
            pairs_a += [(2 * d + 1, 2 * d + 2), (2 * d + 2, 2 * d + 1)]
            pairs_b += [(2 * d, 2 * d + 2), (2 * d + 3, 2 * d + 1)]
    rec_c = lax.ppermute(send_c, axes, pairs_c)
    ut = jnp.transpose(up_transfer, (1, 2, 0))
    uc = jnp.transpose(up_coupling, (1, 2, 0))
    (mats,) = call(
        transfers_kernel,
        [((64 * T_ROWS, 64), bf16)],
        [pltpu.VMEM((64 * T_ROWS, 128), f32)],
        (ut,), "v>v",
        2 * 4096 * 256 * 40, 3 << 20,
    )
    cf, path = call(
        coeff_kernel,
        [((256, 128), f32), ((32, 64), f32)],
        [],
        (vt, leaf_bases, transfers, mats), "vvvv>vv",
        2 * 512 * 512 * 256, 2 << 20,
    )
    send, send_a, send_b = call(
        product_kernel,
        [((512, 640), bf16), ((16, HALO), bf16), ((8, HALO), bf16)],
        [pltpu.VMEM((1024, 128), f32), pltpu.VMEM((640, 256), bf16)],
        (
            cf, path, jnp.transpose(coupling_blocks, (1, 2, 0)),
            block_source.reshape(1, -1), block_owner.reshape(1, -1), block_target.reshape(1, -1),
            send_a, send_b, rec_c,
        ), "vvvvvvvva>vvv",
        2 * 512 * 256 * 640, 4 << 20,
    )
    near_groups = [[xy * 8 + z for z in range(8)] for xy in range(peers // 8)]
    far_groups = [[xy * 8 + z for xy in range(peers // 8)] for z in range(8)]
    recv = lax.all_to_all(
        send, "leaf", split_axis=0, concat_axis=0, tiled=True, axis_index_groups=far_groups
    )
    rec_a = lax.ppermute(send_a, axes, pairs_a)
    rec_b = lax.ppermute(send_b, axes, pairs_b)
    buffers = [
        pltpu.VMEM((8, COLS), bf16), pltpu.VMEM((8, COLS), bf16), pltpu.VMEM((8, LOCAL), bf16),
        pltpu.VMEM((16, 6144), bf16), pltpu.VMEM((6144, 16), bf16), pltpu.VMEM((16, 6144), bf16),
        pltpu.VMEM((8, 6144), f32), pltpu.VMEM((16, HALF), f32), pltpu.SemaphoreType.DMA((6,)),
    ]
    (coup,) = call(
        couplings_kernel,
        [((64 * C_ROWS, 64), bf16)],
        [pltpu.VMEM((64 * C_ROWS, 128), f32)],
        (uc, send), "va>v",
        2 * 4096 * 256 * 8, 3 << 20,
    )
    (begun,) = call(
        near_first_kernel,
        [((16, LEAF * (10 - SPLIT)), f32)],
        buffers + [pltpu.SemaphoreType.DMA((5,))],
        (vt, pt, rec_c), "aaa>h",
        2 * 37 * 512 * 512 * 256, 1 << 20, vmem=24,
    )
    (send,) = call(
        middle_kernel,
        [((256, 512), bf16)],
        [
            pltpu.VMEM((512, 640), bf16), pltpu.VMEM((32, 64), f32),
            pltpu.VMEM((64 * T_ROWS, 64), bf16), pltpu.VMEM((64 * C_ROWS, 64), bf16),
            pltpu.VMEM((512, 128), f32), pltpu.VMEM((256, 64), f32), pltpu.VMEM((56, 64), f32),
            pltpu.SemaphoreType.DMA((4,)),
        ],
        (recv, path, mats, coup), "aaaa>v",
        2 * 256 * 512 * 512, 2 << 20,
    )
    recv = lax.all_to_all(
        send, "leaf", split_axis=0, concat_axis=0, tiled=True, axis_index_groups=near_groups
    )
    near_mine, near_send = call(
        near_rest_kernel,
        [((8, HALF), f32), ((8, HALF), f32)],
        buffers + [pltpu.VMEM((16, HALO), bf16), pltpu.VMEM((8, HALO), bf16)],
        (vt, pt, rec_c, rec_a, rec_b, begun), "aaaaah>vv",
        2 * 30 * 512 * 512 * 256, 1 << 20, vmem=24,
    )
    near_other = lax.ppermute(near_send, axes, pairs_c)
    (out,) = call(
        final_kernel,
        [((8, COLS), bf16)],
        [
            pltpu.VMEM((256, 512), bf16), pltpu.VMEM((8, HALF), f32), pltpu.VMEM((8, HALF), f32),
            pltpu.VMEM((128, 64), bf16), pltpu.VMEM((1, COLS), i32),
            pltpu.VMEM((256, 128), f32), pltpu.VMEM((64, 128), f32),
            pltpu.VMEM((248, 64), f32), pltpu.VMEM((8, COLS), f32), pltpu.SemaphoreType.DMA((5,)),
        ],
        (recv, near_mine, near_other, mats, transfers, leaf_bases, leaf_order), "aaaavvh>v",
        2 * 256 * 256 * COLS, 8 << 20,
    )
    return out


def solution(mesh):
    return jax.shard_map(
        shards,
        mesh=mesh,
        in_specs=(
            P(None, "leaf"),
            P("vec", "leaf"),
            P("leaf", None),
            P("leaf", None, None),
            P("leaf", None, None),
            P("leaf", None, None),
            P("leaf"),
            P("leaf", None),
            P("leaf"),
            P(),
            P(),
        ),
        out_specs=P("vec", "leaf"),
        check_vma=False,
    )
```

```python
import jax
import jax.numpy as jnp
import ml_dtypes
from jax import lax
from jax.experimental import pallas as pl
from jax.experimental.pallas import tpu as pltpu
from jax.sharding import PartitionSpec as P

f32 = jnp.float32
bf16 = jnp.bfloat16
i32 = jnp.int32

LEAF = 512
COLS = 8192
HALO = 1024
LOCAL = 5120
HALF = 4096
NT = (((1,), (1,)), ((), ()))
TN = (((0,), (0,)), ((), ()))
SMOOTH_HI = float(ml_dtypes.bfloat16(0.0025))
SMOOTH_LO = float(ml_dtypes.bfloat16(0.0025 - SMOOTH_HI))
VM = pl.BlockSpec(memory_space=pltpu.VMEM)


def dot(a, b, dims=(((1,), (0,)), ((), ()))):
    return lax.dot_general(a, b, dims, preferred_element_type=f32)


def iota(shape, dim):
    return lax.broadcasted_iota(i32, shape, dim)


def hot(mask):
    return jnp.where(mask, 1.0, 0.0).astype(bf16)


def halves(x):
    hi = x.astype(bf16)
    lo = (x - hi.astype(f32)).astype(bf16)
    return jnp.concatenate([hi, lo], axis=0)


def wide(x):
    return jnp.concatenate([x, jnp.zeros_like(x)], axis=1)


def dot_pair(x, w, dims=(((1,), (0,)), ((), ()))):
    y = dot(halves(x), w, dims)
    n = x.shape[0]
    return y[:n] + y[n:]


ANY = pl.BlockSpec(memory_space=pl.ANY)
SPEC = {"v": VM, "a": ANY, "h": pl.BlockSpec(memory_space=pltpu.HBM)}


def call(kernel, outs, scratch, args, kinds, flops, nbytes, vmem=16):
    ins, results = kinds.split(">")
    args = [
        pltpu.with_memory_space_constraint(x, pltpu.HBM) if k == "h" else x
        for x, k in zip(args, ins)
    ]
    return pl.pallas_call(
        kernel,
        out_shape=[
            pltpu.HBM(s, d) if k == "h" else jax.ShapeDtypeStruct(s, d)
            for (s, d), k in zip(outs, results)
        ],
        in_specs=[SPEC[k] for k in ins],
        out_specs=[SPEC[k] for k in results],
        scratch_shapes=scratch,
        compiler_params=pltpu.CompilerParams(vmem_limit_bytes=vmem << 20),
        cost_estimate=pl.CostEstimate(flops=flops, bytes_accessed=nbytes, transcendentals=0),
    )(*args)


def fetch(sems, *pairs):
    copies = [
        pltpu.make_async_copy(src, dst, sems.at[i]) for i, (src, dst) in enumerate(pairs)
    ]
    for copy in copies:
        copy.start()
    return copies


def gather_kernel(
    pts_in, vec_in, perm_in, vt, pt, send_c, pts, vec, perm, dv, dp, sems
):
    core = lax.axis_index("vec")
    for copy in fetch(sems, (perm_in, perm), (vec_in, vec), (pts_in, pts)):
        copy.wait()
    for m in range(16):
        a, b = 512 * m, 512 * m + 256
        dv[16 * m : 16 * m + 16, :] = jnp.concatenate(
            [vec[:, a : a + 256], vec[:, b : b + 256]], axis=0
        )
        three = pts[:, a : a + 512].astype(f32)
        four = jnp.concatenate([three, jnp.zeros((1, 512), f32)], axis=0)
        dp[8 * m : 8 * m + 8, :] = jnp.concatenate([four[:, :256], four[:, 256:]], axis=0)
    data_v = dv[...]
    data_p = dp[...].astype(bf16)
    width = 512
    for n in range(COLS // width):
        cols = slice(n * width, (n + 1) * width)
        index = perm[:, cols]
        low = index & 255
        high = jnp.broadcast_to(lax.shift_right_logical(index, 8), (8, width))
        select = hot(iota((256, width), 0) == low)
        got = dot(data_v, select)
        out = got[:8]
        for q in range(1, 32):
            out = jnp.where(high == q, got[8 * q : 8 * q + 8], out)
        vt[:, cols] = out.astype(bf16)
        got = dot(data_p, select)
        pair = high - iota((8, width), 0) // 4
        out = jnp.zeros((8, width), f32)
        for m in range(16):
            out = jnp.where(pair == 2 * m, got[8 * m : 8 * m + 8], out)
        out = out[:4] + out[4:]
        pt[:, cols] = jnp.concatenate([out, jnp.zeros((4, width), f32)], axis=0).astype(bf16)

    @pl.when(core == 0)
    def _():
        send_c[...] = vt[:, COLS - LOCAL :]

    @pl.when(core == 1)
    def _():
        send_c[...] = vt[:, :LOCAL]


def coeff_kernel(vt, pt, rec_c, bases, tr, mats, cf, path, halo):
    core = lax.axis_index("vec")
    ends = ((slice(0, HALO), slice(0, HALO)), (slice(COLS - HALO, COLS), slice(LOCAL - HALO, LOCAL)))
    for which, (cols, other) in enumerate(ends):

        @pl.when(core == which)
        def _():
            halo[0:8, :] = vt[:, cols]
            halo[8:16, :] = rec_c[:, other]
            halo[16:24, :] = pt[:, cols]

    cf[248:256, :] = jnp.zeros((8, 128), f32)
    for leaf in range(16):
        cf[8 * leaf : 8 * leaf + 8, :64] = dot(
            vt[:, LEAF * leaf : LEAF * leaf + LEAF], bases[leaf], NT
        )
    off, n = 0, 16
    while n > 1:
        for m in range(n // 2):
            r = 8 * (off + 2 * m)
            pair = jnp.concatenate([cf[r : r + 8, :64], cf[r + 8 : r + 16, :64]], axis=1)
            w = tr[off + 2 * m : off + 2 * m + 2].reshape(128, 64)
            t = 8 * (off + n + m)
            cf[t : t + 8, :64] = dot_pair(pair, w)
        off += n
        n //= 2
    value = cf[240:248, :64]
    for u in range(3):
        path[8 * u : 8 * u + 8, :] = value
        value = dot_pair(value, own_matrix(mats, OWN + u))
    path[24:32, :] = value


def own_matrix(mats, row, count=1):
    return mats[64 * row : 64 * (row + count), :]


def product_kernel(
    cf, path, cp, bsrc, bown, btgt, send, pick, prod
):
    source = hot(iota((32, 256), 0) == bsrc[...])
    for v in range(8):
        mine = cf[pl.ds(v, 32, stride=8), :][:, :64].astype(bf16)
        chosen = dot(mine, source, TN)
        pick[pl.ds(v, 64, stride=8), :] = chosen[:, :128]
        pick[pl.ds(512 + v, 64, stride=8), :] = chosen[:, 128:]
    for half in range(2):
        lanes = slice(128 * half, 128 * half + 128)
        for pb in range(4):
            rows = slice(16 * pb, 16 * pb + 16)

            def step(k, acc):
                block = cp[k, rows, lanes].astype(f32)
                picked = pick[pl.ds(pl.multiple_of(512 * half + 8 * k, 8), 8), :]
                return tuple(acc[v] + picked[v : v + 1] * block for v in range(8))

            acc = lax.fori_loop(0, 64, step, (jnp.zeros((16, 128), f32),) * 8, unroll=8)
            for v in range(8):
                top = 64 * v + 16 * pb
                prod[top : top + 16, lanes] = acc[v].astype(bf16)
    prod[512:576, :] = jnp.zeros((64, 256), bf16)
    prod[576:640, :] = jnp.broadcast_to((btgt[...] + 1).astype(f32), (64, 256)).astype(bf16)
    owner = bown[...]
    owner_f = owner.astype(f32)
    column = jnp.transpose(jnp.broadcast_to(owner_f, (128, 256)))
    ranks = []
    for half in range(2):
        row = owner_f[:, 128 * half : 128 * half + 128]
        before = iota((256, 128), 0) < iota((256, 128), 1) + 128 * half
        same = jnp.where((column == row) & before, 1.0, 0.0)
        ranks.append(jnp.sum(same, axis=0, keepdims=True))
    place = owner * 4 + jnp.concatenate(ranks, axis=1).astype(i32)
    top = path[24:32, :]
    high = top.astype(bf16).astype(f32)
    extra = jnp.concatenate([high, top - high, jnp.zeros((16, 64), f32)], axis=0)
    extra = wide(extra)
    payload = prod[...]
    for part in range(2):
        rows = slice(256 * part, 256 * part + 256)
        slots = hot(iota((256, 256), 0) + 256 * part == place)
        out = dot(slots, payload, NT)
        send[rows, 0:512] = out[:, :512].astype(bf16)
        tail = out[:, 512:].reshape(8, 32, 128) + extra[None]
        send[rows, 512:640] = tail.reshape(256, 128).astype(bf16)


def split3(x):
    a = x.astype(bf16).astype(f32)
    b = (x - a).astype(bf16).astype(f32)
    return a, b, x - a - b


def leaf_cols(leaf):
    return slice(LEAF * leaf, LEAF * leaf + LEAF)


def load_window(vt, pt, rec_c, halo, leaves, vw, pw):
    core = lax.axis_index("vec")
    for which in range(2):

        @pl.when(core == which)
        def _():
            for w in leaves:
                to = leaf_cols(w)
                if w < 2:
                    near_cols = leaf_cols(w if which == 0 else 1 - w)
                    vw[0:8, to] = halo[8:16, near_cols]
                    vw[8:16, to] = halo[0:8, near_cols]
                    pw[:, to] = halo[16:24, near_cols].astype(f32)
                else:
                    local = leaf_cols(w - 2 if which == 0 else 17 - w)
                    vw[0:8, to] = vt[:, local]
                    vw[8:16, to] = rec_c[:, leaf_cols(w - 2 if which == 0 else 11 - w)]
                    pw[:, to] = pt[:, local].astype(f32)


def features(leaves, pw, fs, ft):
    for leaf in leaves:
        cols = leaf_cols(leaf)
        p = pw[0:3, cols]
        norm = p[0:1] * p[0:1] + p[1:2] * p[1:2] + p[2:3] * p[2:3]
        parts = jnp.concatenate(split3(norm), axis=0)
        one = jnp.ones((3, LEAF), f32)
        two = jnp.ones((2, LEAF), f32)
        pad = jnp.zeros((5, LEAF), f32)
        source = jnp.concatenate([p, parts, one, two, pad], axis=0)
        smooth = jnp.where(iota((2, LEAF), 0) == 0, SMOOTH_HI, SMOOTH_LO)
        target = jnp.concatenate([-2.0 * p, one, parts, smooth, pad], axis=0)
        fs[cols, :] = jnp.transpose(source).astype(bf16)
        ft[:, cols] = target.astype(bf16)


def near_target(t, vw, fs, ft, acc):
    tc = leaf_cols(t)
    total = jnp.zeros((16, LEAF), f32)
    for s in range(t - 2, t + 3):
        if 2 <= s < t:
            continue
        sc = leaf_cols(s)
        kernel = lax.rsqrt(dot(fs[sc, :], ft[:, tc])).astype(bf16)
        total = total + dot(vw[:, sc], kernel)
        if t < s < 10:
            acc[:, leaf_cols(s - 2)] += dot(vw[:, tc], kernel, NT)
    acc[:, leaf_cols(t - 2)] += total


SPLIT = 5


def near_first_kernel(
    vt_in, pt_in, c_in, begun, vt, pt, rec_c, vw, fs, ft, pw, acc, sems, out_sems
):
    for copy in fetch(sems, (vt_in, vt), (pt_in, pt), (c_in, rec_c)):
        copy.wait()
    load_window(vt, pt, rec_c, None, range(SPLIT, 12), vw, pw)
    features(range(SPLIT, 12), pw, fs, ft)
    acc[...] = jnp.zeros_like(acc)
    copies = []
    for t in range(SPLIT, 10):
        near_target(t, vw, fs, ft, acc)
        src, dst = acc.at[:, leaf_cols(t - 2)], begun.at[:, leaf_cols(t - SPLIT)]
        copies += [pltpu.make_async_copy(src, dst, out_sems.at[t - SPLIT])]
        copies[-1].start()
    for copy in copies:
        copy.wait()


def near_rest_kernel(
    vt_in, pt_in, c_in, halo_in, begun, mine, other,
    vt, pt, rec_c, vw, fs, ft, pw, acc, sems, halo,
):
    left = LEAF * (SPLIT - 2)
    copies = fetch(
        sems, (vt_in, vt), (pt_in, pt), (c_in, rec_c), (halo_in, halo),
        (begun, acc.at[:, left:]),
    )
    acc[:, :left] = jnp.zeros((16, left), f32)
    for copy in copies[:4]:
        copy.wait()
    load_window(vt, pt, rec_c, halo, range(0, SPLIT + 2), vw, pw)
    features(range(0, SPLIT + 2), pw, fs, ft)
    copies[4].wait()
    for t in range(2, SPLIT):
        near_target(t, vw, fs, ft, acc)
    core = lax.axis_index("vec")
    for which in range(2):

        @pl.when(core == which)
        def _():
            for i in range(8):
                to = leaf_cols(i if which == 0 else 7 - i)
                mine[:, to] = acc[0:8, leaf_cols(i)] * (8.0 / LEAF)
                other[:, to] = acc[8:16, leaf_cols(i)] * (8.0 / LEAF)


LEVEL_START = [256 - (256 >> u) for u in range(7)]
UPPER = 224
OWN = 30
SIBLING = 33
OWN_UPPER = 36
T_ROWS = 40
C_ROWS = 8


def node(u, other=False):
    n = lax.shift_right_logical(lax.axis_index("leaf"), u)
    return LEVEL_START[u] + (lax.bitwise_xor(n, 1) if other else n)


def pick_matrices(table, want, rows, count, mats, buf):
    pick = hot(iota((rows, 254), 1) == want)

    def step(g, carry):
        out = dot(pick, table[pl.ds(4 * g, 4)].reshape(256, 254), NT)
        for j in range(4):
            at = pl.multiple_of((4 * g + j) * rows, 8)
            buf[pl.ds(at, rows), :64] = out[:, 64 * j : 64 * j + 64]
        return carry

    lax.fori_loop(0, 16, step, 0, unroll=4)
    for m in range(count):
        mats[64 * m : 64 * m + 64, :] = buf[pl.ds(m, 64, stride=rows), :][:, :64].astype(bf16)


def transfers_kernel(ut, mats, buf):
    row = iota((T_ROWS, 254), 0)
    want = jnp.where(row < 30, row + UPPER, -1)
    for u in range(3):
        want = jnp.where(row == OWN + u, node(u), want)
        want = jnp.where(row == SIBLING + u, node(u, True), want)
        want = jnp.where(row == OWN_UPPER + u, node(u + 3), want)
    pick_matrices(ut, want, T_ROWS, 39, mats, buf)


def couplings_kernel(uc, seen, mats, buf):
    row = iota((C_ROWS, 254), 0)
    want = jnp.zeros((C_ROWS, 254), i32) - 1
    for u in range(7):
        want = jnp.where(row == u, node(u, u < 3), want)
    pick_matrices(uc, want, C_ROWS, 7, mats, buf)


def middle_kernel(
    recv_in, path_in, mats_in, coup_in, send, recv, path, mats, coup, ext, xs, gain, sems
):
    device = lax.axis_index("leaf")
    for copy in fetch(
        sems, (recv_in, recv), (path_in, path), (mats_in, mats), (coup_in, coup)
    ):
        copy.wait()
    ext[...] = recv[:, 512:640].astype(f32)

    labels = jnp.concatenate(
        [jnp.transpose(ext[128 * i : 128 * i + 128, :])[64:65, :] for i in range(4)], axis=1
    )
    row, lane = iota((256, 512), 0), iota((256, 512), 1)
    wanted = ((row & 31) + 1).astype(f32)
    fits = lax.shift_right_logical(row, 5) == (lax.shift_right_logical(lane, 2) & 7)
    sums = dot(hot((labels == wanted) & fits), recv[:, 0:512])

    for g in range(16):
        rows = ext[32 * g : 32 * g + 16, :64]
        xs[8 * g : 8 * g + 8, :] = rows[:8] + rows[8:]
    first, n = 0, 16
    firsts = {3: 0}
    for u in range(3, 6):
        for m in range(n // 2):
            r = 8 * (first + 2 * m)
            e = LEVEL_START[u] - UPPER + 2 * m
            pair = jnp.concatenate([xs[r : r + 8, :], xs[r + 8 : r + 16, :]], axis=1)
            w = own_matrix(mats, e, 2)
            t = 8 * (first + n + m)
            xs[t : t + 8, :] = dot_pair(pair, w)
        first += n
        n //= 2
        firsts[u + 1] = first
    for u in range(7):
        if u < 3:
            partner = path[8 * u : 8 * u + 8, :]
        else:
            sib = lax.bitwise_xor(lax.shift_right_logical(device, u), 1)
            partner = xs[pl.ds(pl.multiple_of((firsts[u] + sib) * 8, 8), 8), :]
        gain[8 * u : 8 * u + 8, :] = dot_pair(partner, own_matrix(coup, u))
    down = gain[48:56, :]
    for u in (5, 4, 3):
        w = own_matrix(mats, OWN_UPPER + u - 3)
        down = dot_pair(down, w, NT) + gain[8 * u : 8 * u + 8, :]
    lines = {}
    for u in (2, 1, 0):
        both = jnp.concatenate(
            [own_matrix(mats, OWN + u), own_matrix(mats, SIBLING + u)], axis=0
        )
        spread = dot_pair(down, both, NT)
        lines[u] = flat(spread[:, 64:] + gain[8 * u : 8 * u + 8, :])
        down = spread[:, :64]
    own_line = flat(down)
    z = device & 7
    last = iota((32, 512), 0) == 31
    for peer in range(8):
        x = lax.bitwise_xor(z, peer)
        line = jnp.where(x == 0, own_line, lines[0])
        line = jnp.where(x >= 2, lines[1], line)
        line = jnp.where(x >= 4, lines[2], line)
        block = jnp.where(last, line, sums[32 * peer : 32 * peer + 32])
        send[32 * peer : 32 * peer + 32, :] = block.astype(bf16)


def flat(x):
    return jnp.concatenate([x[v : v + 1] for v in range(8)], axis=1)


def final_kernel(
    recv_in, mine_in, other_in, mats_in, tr, bases, perm_in, out,
    recv, near_mine, near_other, mats, perm, cpl, dwn, dn, tree, sems,
):
    copies = fetch(
        sems,
        (recv_in, recv),
        (mats_in.at[64 * OWN : 64 * OWN + 128], mats),
        (mine_in, near_mine),
        (other_in, near_other),
        (perm_in, perm),
    )
    for copy in copies:
        copy.wait()
    device = lax.axis_index("leaf")
    core = lax.axis_index("vec")
    z = device & 7
    total = jnp.zeros((32, 512), f32)
    levels = [jnp.zeros((1, 512), f32)] * 3
    for peer in range(8):
        block = recv[32 * peer : 32 * peer + 32, :].astype(f32)
        total = total + block
        x = lax.bitwise_xor(z, peer)
        line = block[31:32]
        for i, use in enumerate((x >= 4, (x >= 2) & (x < 4), x < 2)):
            levels[i] = levels[i] + jnp.where(use, line, 0.0)
    levels = jnp.concatenate(levels + [jnp.zeros((5, 512), f32)], axis=0)
    for v in range(8):
        cpl[pl.ds(v, 32, stride=8), :] = wide(total[:, 64 * v : 64 * v + 64])
        dwn[pl.ds(v, 8, stride=8), :] = wide(levels[:, 64 * v : 64 * v + 64])
    down = dot_pair(dwn[0:8, :64], own_matrix(mats, 1), NT) + dwn[8:16, :64]
    down = dot_pair(down, own_matrix(mats, 0), NT) + dwn[16:24, :64]

    dn[240:248, :] = down + cpl[240:248, :64]
    n = 1
    while n < 16:
        off_parent = 32 - 2 * n
        n *= 2
        off = 32 - 2 * n
        for m in range(n // 2):
            r = 8 * (off_parent + m)
            w = tr[off + 2 * m : off + 2 * m + 2].reshape(128, 64)
            both = dot_pair(dn[r : r + 8, :], w, NT)
            t = 8 * (off + 2 * m)
            dn[t : t + 8, :] = both[:, :64] + cpl[t : t + 8, :64]
            dn[t + 8 : t + 16, :] = both[:, 64:] + cpl[t + 8 : t + 16, :64]
    for leaf in range(16):
        tree[:, LEAF * leaf : LEAF * leaf + LEAF] = dot(
            dn[8 * leaf : 8 * leaf + 8, :].astype(bf16), bases[leaf]
        )

    @pl.when(core == 0)
    def _():
        tree[:, :HALF] += near_mine[...]
        tree[:, HALF:] += near_other[...]

    @pl.when(core == 1)
    def _():
        tree[:, :HALF] += near_other[...]
        tree[:, HALF:] += near_mine[...]

    width = 512
    total = jnp.zeros((256, 256), f32)
    for b in range(COLS // width):
        cols = slice(b * width, (b + 1) * width)
        index = perm[:, cols]
        select = hot(iota((256, width), 0) == (index & 255))
        high = jnp.broadcast_to(lax.shift_right_logical(index, 8), (8, width))
        values = tree[:, cols]
        spread = jnp.concatenate(
            [jnp.where(high == q, values, 0.0) for q in range(32)], axis=0
        ).astype(bf16)
        total = total + dot(spread, select, NT)
    for q in range(32):
        out[:, 256 * q : 256 * q + 256] = total[8 * q : 8 * q + 8].astype(bf16)


def shards(
    points, vectors, leaf_order, leaf_bases, transfers, coupling_blocks,
    block_source, block_owner, block_target, up_transfer, up_coupling,
):
    peers = lax.axis_size("leaf")
    axes = ("leaf", "vec")
    vt, pt, send_c = call(
        gather_kernel,
        [((8, COLS), bf16), ((8, COLS), bf16), ((8, LOCAL), bf16)],
        [
            pltpu.VMEM((3, COLS), bf16), pltpu.VMEM((8, COLS), bf16), pltpu.VMEM((1, COLS), i32),
            pltpu.VMEM((256, 256), bf16), pltpu.VMEM((128, 256), f32), pltpu.SemaphoreType.DMA((3,)),
        ],
        (points, vectors, leaf_order), "hhh>vvv",
        2 * 384 * 256 * COLS, 1 << 20,
    )
    pairs_a, pairs_c = [], []
    for d in range(peers):
        pairs_c += [(2 * d, 2 * d + 1), (2 * d + 1, 2 * d)]
        if d + 1 < peers:
            pairs_a += [(2 * d + 1, 2 * d + 2), (2 * d + 2, 2 * d + 1)]
    rec_c = lax.ppermute(send_c, axes, pairs_c)
    ut = jnp.transpose(up_transfer, (1, 2, 0))
    uc = jnp.transpose(up_coupling, (1, 2, 0))
    (mats,) = call(
        transfers_kernel,
        [((64 * T_ROWS, 64), bf16)],
        [pltpu.VMEM((64 * T_ROWS, 128), f32)],
        (ut,), "v>v",
        2 * 4096 * 256 * 40, 3 << 20,
    )
    cf, path, halo = call(
        coeff_kernel,
        [((256, 128), f32), ((32, 64), f32), ((24, HALO), bf16)],
        [],
        (vt, pt, rec_c, leaf_bases, transfers, mats), "vvvvvv>vvv",
        2 * 512 * 512 * 256, 2 << 20,
    )
    halo = lax.ppermute(halo, axes, pairs_a)
    (send,) = call(
        product_kernel,
        [((512, 640), bf16)],
        [pltpu.VMEM((1024, 128), f32), pltpu.VMEM((640, 256), bf16)],
        (
            cf, path, jnp.transpose(coupling_blocks, (1, 2, 0)),
            block_source.reshape(1, -1), block_owner.reshape(1, -1), block_target.reshape(1, -1),
        ), "vvvvvv>v",
        2 * 512 * 256 * 640, 4 << 20,
    )
    send, halo = lax.optimization_barrier((send, halo))
    near_groups = [[xy * 8 + z for z in range(8)] for xy in range(peers // 8)]
    far_groups = [[xy * 8 + z for xy in range(peers // 8)] for z in range(8)]
    recv = lax.all_to_all(
        send, "leaf", split_axis=0, concat_axis=0, tiled=True, axis_index_groups=far_groups
    )
    buffers = [
        pltpu.VMEM((8, COLS), bf16), pltpu.VMEM((8, COLS), bf16), pltpu.VMEM((8, LOCAL), bf16),
        pltpu.VMEM((16, 6144), bf16), pltpu.VMEM((6144, 16), bf16), pltpu.VMEM((16, 6144), bf16),
        pltpu.VMEM((8, 6144), f32), pltpu.VMEM((16, HALF), f32), pltpu.SemaphoreType.DMA((6,)),
    ]
    (coup,) = call(
        couplings_kernel,
        [((64 * C_ROWS, 64), bf16)],
        [pltpu.VMEM((64 * C_ROWS, 128), f32)],
        (uc, send), "va>v",
        2 * 4096 * 256 * 8, 3 << 20,
    )
    (begun,) = call(
        near_first_kernel,
        [((16, LEAF * (10 - SPLIT)), f32)],
        buffers + [pltpu.SemaphoreType.DMA((5,))],
        (vt, pt, rec_c), "aaa>h",
        2 * 37 * 512 * 512 * 256, 1 << 20, vmem=24,
    )
    (send,) = call(
        middle_kernel,
        [((256, 512), bf16)],
        [
            pltpu.VMEM((512, 640), bf16), pltpu.VMEM((32, 64), f32),
            pltpu.VMEM((64 * T_ROWS, 64), bf16), pltpu.VMEM((64 * C_ROWS, 64), bf16),
            pltpu.VMEM((512, 128), f32), pltpu.VMEM((256, 64), f32), pltpu.VMEM((56, 64), f32),
            pltpu.SemaphoreType.DMA((4,)),
        ],
        (recv, path, mats, coup), "aaaa>v",
        2 * 256 * 512 * 512, 2 << 20,
    )
    recv = lax.all_to_all(
        send, "leaf", split_axis=0, concat_axis=0, tiled=True, axis_index_groups=near_groups
    )
    near_mine, near_send = call(
        near_rest_kernel,
        [((8, HALF), f32), ((8, HALF), f32)],
        buffers + [pltpu.VMEM((24, HALO), bf16)],
        (vt, pt, rec_c, halo, begun), "aaaah>vv",
        2 * 30 * 512 * 512 * 256, 1 << 20, vmem=24,
    )
    near_other = lax.ppermute(near_send, axes, pairs_c)
    (out,) = call(
        final_kernel,
        [((8, COLS), bf16)],
        [
            pltpu.VMEM((256, 512), bf16), pltpu.VMEM((8, HALF), f32), pltpu.VMEM((8, HALF), f32),
            pltpu.VMEM((128, 64), bf16), pltpu.VMEM((1, COLS), i32),
            pltpu.VMEM((256, 128), f32), pltpu.VMEM((64, 128), f32),
            pltpu.VMEM((248, 64), f32), pltpu.VMEM((8, COLS), f32), pltpu.SemaphoreType.DMA((5,)),
        ],
        (recv, near_mine, near_other, mats, transfers, leaf_bases, leaf_order), "aaaavvh>v",
        2 * 256 * 256 * COLS, 8 << 20,
    )
    return out


def solution(mesh):
    return jax.shard_map(
        shards,
        mesh=mesh,
        in_specs=(
            P(None, "leaf"),
            P("vec", "leaf"),
            P("leaf", None),
            P("leaf", None, None),
            P("leaf", None, None),
            P("leaf", None, None),
            P("leaf"),
            P("leaf", None),
            P("leaf"),
            P(),
            P(),
        ),
        out_specs=P("vec", "leaf"),
        check_vma=False,
    )
```

```python
import jax
import jax.numpy as jnp
import ml_dtypes
from jax import lax
from jax.experimental import pallas as pl
from jax.experimental.pallas import tpu as pltpu
from jax.sharding import PartitionSpec as P

f32 = jnp.float32
bf16 = jnp.bfloat16
i32 = jnp.int32

LEAF = 512
COLS = 8192
HALO = 1024
LOCAL = 5120
HALF = 4096
NT = (((1,), (1,)), ((), ()))
TN = (((0,), (0,)), ((), ()))
SMOOTH_HI = float(ml_dtypes.bfloat16(0.0025))
SMOOTH_LO = float(ml_dtypes.bfloat16(0.0025 - SMOOTH_HI))
VM = pl.BlockSpec(memory_space=pltpu.VMEM)


def dot(a, b, dims=(((1,), (0,)), ((), ()))):
    return lax.dot_general(a, b, dims, preferred_element_type=f32)


def iota(shape, dim):
    return lax.broadcasted_iota(i32, shape, dim)


def hot(mask):
    return jnp.where(mask, 1.0, 0.0).astype(bf16)


def halves(x):
    hi = x.astype(bf16)
    lo = (x - hi.astype(f32)).astype(bf16)
    return jnp.concatenate([hi, lo], axis=0)


def wide(x):
    return jnp.concatenate([x, jnp.zeros_like(x)], axis=1)


def dot_pair(x, w, dims=(((1,), (0,)), ((), ()))):
    y = dot(halves(x), w, dims)
    n = x.shape[0]
    return y[:n] + y[n:]


ANY = pl.BlockSpec(memory_space=pl.ANY)
SPEC = {"v": VM, "a": ANY, "h": pl.BlockSpec(memory_space=pltpu.HBM)}


def call(kernel, outs, scratch, args, kinds, flops, nbytes, vmem=16):
    ins, results = kinds.split(">")
    args = [
        pltpu.with_memory_space_constraint(x, pltpu.HBM) if k == "h" else x
        for x, k in zip(args, ins)
    ]
    return pl.pallas_call(
        kernel,
        out_shape=[
            pltpu.HBM(s, d) if k == "h" else jax.ShapeDtypeStruct(s, d)
            for (s, d), k in zip(outs, results)
        ],
        in_specs=[SPEC[k] for k in ins],
        out_specs=[SPEC[k] for k in results],
        scratch_shapes=scratch,
        compiler_params=pltpu.CompilerParams(vmem_limit_bytes=vmem << 20),
        cost_estimate=pl.CostEstimate(flops=flops, bytes_accessed=nbytes, transcendentals=0),
    )(*args)


def fetch(sems, *pairs):
    copies = [
        pltpu.make_async_copy(src, dst, sems.at[i]) for i, (src, dst) in enumerate(pairs)
    ]
    for copy in copies:
        copy.start()
    return copies


def gather_kernel(
    pts_in, vec_in, perm_in, vt, pt, send_c, pts, vec, perm, dv, dp, sems
):
    core = lax.axis_index("vec")
    for copy in fetch(sems, (perm_in, perm), (vec_in, vec), (pts_in, pts)):
        copy.wait()
    for m in range(16):
        a, b = 512 * m, 512 * m + 256
        dv[16 * m : 16 * m + 16, :] = jnp.concatenate(
            [vec[:, a : a + 256], vec[:, b : b + 256]], axis=0
        )
        three = pts[:, a : a + 512].astype(f32)
        four = jnp.concatenate([three, jnp.zeros((1, 512), f32)], axis=0)
        dp[8 * m : 8 * m + 8, :] = jnp.concatenate([four[:, :256], four[:, 256:]], axis=0)
    data_v = dv[...]
    data_p = dp[...].astype(bf16)
    width = 512
    for n in range(COLS // width):
        cols = slice(n * width, (n + 1) * width)
        index = perm[:, cols]
        low = index & 255
        high = jnp.broadcast_to(lax.shift_right_logical(index, 8), (8, width))
        select = hot(iota((256, width), 0) == low)
        got = dot(data_v, select)
        out = got[:8]
        for q in range(1, 32):
            out = jnp.where(high == q, got[8 * q : 8 * q + 8], out)
        vt[:, cols] = out.astype(bf16)
        got = dot(data_p, select)
        pair = high - iota((8, width), 0) // 4
        out = jnp.zeros((8, width), f32)
        for m in range(16):
            out = jnp.where(pair == 2 * m, got[8 * m : 8 * m + 8], out)
        out = out[:4] + out[4:]
        pt[:, cols] = jnp.concatenate([out, jnp.zeros((4, width), f32)], axis=0).astype(bf16)

    @pl.when(core == 0)
    def _():
        send_c[...] = vt[:, COLS - LOCAL :]

    @pl.when(core == 1)
    def _():
        send_c[...] = vt[:, :LOCAL]


def coeff_kernel(vt, pt, rec_c, bases, tr, mats, cf, path, halo):
    core = lax.axis_index("vec")
    ends = ((slice(0, HALO), slice(0, HALO)), (slice(COLS - HALO, COLS), slice(LOCAL - HALO, LOCAL)))
    for which, (cols, other) in enumerate(ends):

        @pl.when(core == which)
        def _():
            halo[0:8, :] = vt[:, cols]
            halo[8:16, :] = rec_c[:, other]
            halo[16:24, :] = pt[:, cols]

    cf[248:256, :] = jnp.zeros((8, 128), f32)
    for leaf in range(16):
        cf[8 * leaf : 8 * leaf + 8, :64] = dot(
            vt[:, LEAF * leaf : LEAF * leaf + LEAF], bases[leaf], NT
        )
    off, n = 0, 16
    while n > 1:
        for m in range(n // 2):
            r = 8 * (off + 2 * m)
            pair = jnp.concatenate([cf[r : r + 8, :64], cf[r + 8 : r + 16, :64]], axis=1)
            w = tr[off + 2 * m : off + 2 * m + 2].reshape(128, 64)
            t = 8 * (off + n + m)
            cf[t : t + 8, :64] = dot_pair(pair, w)
        off += n
        n //= 2
    value = cf[240:248, :64]
    for u in range(3):
        path[8 * u : 8 * u + 8, :] = value
        value = dot_pair(value, own_matrix(mats, OWN + u))
    path[24:32, :] = value


def own_matrix(mats, row, count=1):
    return mats[64 * row : 64 * (row + count), :]


def product_kernel(
    cf, path, cp, bsrc, bown, btgt, send, pick, prod
):
    source = hot(iota((32, 256), 0) == bsrc[...])
    for v in range(8):
        mine = cf[pl.ds(v, 32, stride=8), :][:, :64].astype(bf16)
        chosen = dot(mine, source, TN)
        pick[pl.ds(v, 64, stride=8), :] = chosen[:, :128]
        pick[pl.ds(512 + v, 64, stride=8), :] = chosen[:, 128:]
    for half in range(2):
        lanes = slice(128 * half, 128 * half + 128)
        for pb in range(4):
            rows = slice(16 * pb, 16 * pb + 16)

            def step(k, acc):
                block = cp[k, rows, lanes].astype(f32)
                picked = pick[pl.ds(pl.multiple_of(512 * half + 8 * k, 8), 8), :]
                return tuple(acc[v] + picked[v : v + 1] * block for v in range(8))

            acc = lax.fori_loop(0, 64, step, (jnp.zeros((16, 128), f32),) * 8, unroll=8)
            for v in range(8):
                top = 64 * v + 16 * pb
                prod[top : top + 16, lanes] = acc[v].astype(bf16)
    prod[512:576, :] = jnp.zeros((64, 256), bf16)
    prod[576:640, :] = jnp.broadcast_to((btgt[...] + 1).astype(f32), (64, 256)).astype(bf16)
    owner = bown[...]
    owner_f = owner.astype(f32)
    column = jnp.transpose(jnp.broadcast_to(owner_f, (128, 256)))
    ranks = []
    for half in range(2):
        row = owner_f[:, 128 * half : 128 * half + 128]
        before = iota((256, 128), 0) < iota((256, 128), 1) + 128 * half
        same = jnp.where((column == row) & before, 1.0, 0.0)
        ranks.append(jnp.sum(same, axis=0, keepdims=True))
    place = owner * 4 + jnp.concatenate(ranks, axis=1).astype(i32)
    top = path[24:32, :]
    high = top.astype(bf16).astype(f32)
    extra = jnp.concatenate([high, top - high, jnp.zeros((16, 64), f32)], axis=0)
    extra = wide(extra)
    payload = prod[...]
    for part in range(2):
        rows = slice(256 * part, 256 * part + 256)
        slots = hot(iota((256, 256), 0) + 256 * part == place)
        out = dot(slots, payload, NT)
        send[rows, 0:512] = out[:, :512].astype(bf16)
        tail = out[:, 512:].reshape(8, 32, 128) + extra[None]
        send[rows, 512:640] = tail.reshape(256, 128).astype(bf16)


def split3(x):
    a = x.astype(bf16).astype(f32)
    b = (x - a).astype(bf16).astype(f32)
    return a, b, x - a - b


def leaf_cols(leaf):
    return slice(LEAF * leaf, LEAF * leaf + LEAF)


def load_window(vt, pt, rec_c, halo, leaves, vw, pw):
    core = lax.axis_index("vec")
    for which in range(2):

        @pl.when(core == which)
        def _():
            for w in leaves:
                to = leaf_cols(w)
                if w < 2:
                    near_cols = leaf_cols(w if which == 0 else 1 - w)
                    vw[0:8, to] = halo[8:16, near_cols]
                    vw[8:16, to] = halo[0:8, near_cols]
                    pw[:, to] = halo[16:24, near_cols].astype(f32)
                else:
                    local = leaf_cols(w - 2 if which == 0 else 17 - w)
                    vw[0:8, to] = vt[:, local]
                    vw[8:16, to] = rec_c[:, leaf_cols(w - 2 if which == 0 else 11 - w)]
                    pw[:, to] = pt[:, local].astype(f32)


def features(leaves, pw, fs, ft):
    for leaf in leaves:
        cols = leaf_cols(leaf)
        p = pw[0:3, cols]
        norm = p[0:1] * p[0:1] + p[1:2] * p[1:2] + p[2:3] * p[2:3]
        parts = jnp.concatenate(split3(norm), axis=0)
        one = jnp.ones((3, LEAF), f32)
        two = jnp.ones((2, LEAF), f32)
        pad = jnp.zeros((5, LEAF), f32)
        source = jnp.concatenate([p, parts, one, two, pad], axis=0)
        smooth = jnp.where(iota((2, LEAF), 0) == 0, SMOOTH_HI, SMOOTH_LO)
        target = jnp.concatenate([-2.0 * p, one, parts, smooth, pad], axis=0)
        fs[cols, :] = jnp.transpose(source).astype(bf16)
        ft[:, cols] = target.astype(bf16)


def near_target(t, vw, fs, ft, acc):
    tc = leaf_cols(t)
    total = jnp.zeros((16, LEAF), f32)
    for s in range(t - 2, t + 3):
        if 2 <= s < t:
            continue
        sc = leaf_cols(s)
        kernel = lax.rsqrt(dot(fs[sc, :], ft[:, tc])).astype(bf16)
        total = total + dot(vw[:, sc], kernel)
        if t < s < 10:
            acc[:, leaf_cols(s - 2)] += dot(vw[:, tc], kernel, NT)
    acc[:, leaf_cols(t - 2)] += total


SPLIT = 5


def near_first_kernel(
    vt_in, pt_in, c_in, begun, vt, pt, rec_c, vw, fs, ft, pw, acc, sems, out_sems
):
    for copy in fetch(sems, (vt_in, vt), (pt_in, pt), (c_in, rec_c)):
        copy.wait()
    load_window(vt, pt, rec_c, None, range(SPLIT, 12), vw, pw)
    features(range(SPLIT, 12), pw, fs, ft)
    acc[...] = jnp.zeros_like(acc)
    copies = []
    for t in range(SPLIT, 10):
        near_target(t, vw, fs, ft, acc)
        src, dst = acc.at[:, leaf_cols(t - 2)], begun.at[:, leaf_cols(t - SPLIT)]
        copies += [pltpu.make_async_copy(src, dst, out_sems.at[t - SPLIT])]
        copies[-1].start()
    for copy in copies:
        copy.wait()


def near_rest_kernel(
    vt_in, pt_in, c_in, halo_in, begun, mine, other,
    vt, pt, rec_c, vw, fs, ft, pw, acc, sems, halo,
):
    left = LEAF * (SPLIT - 2)
    copies = fetch(
        sems, (vt_in, vt), (pt_in, pt), (c_in, rec_c), (halo_in, halo),
        (begun, acc.at[:, left:]),
    )
    acc[:, :left] = jnp.zeros((16, left), f32)
    for copy in copies[:4]:
        copy.wait()
    core = lax.axis_index("vec")
    end = lax.axis_index("leaf") == (lax.axis_size("leaf") - 1) * core

    @pl.when(end)
    def _():
        halo[...] = jnp.zeros_like(halo)

    load_window(vt, pt, rec_c, halo, range(0, SPLIT + 2), vw, pw)
    features(range(0, SPLIT + 2), pw, fs, ft)
    copies[4].wait()
    for t in range(2, SPLIT):
        near_target(t, vw, fs, ft, acc)
    for which in range(2):

        @pl.when(core == which)
        def _():
            for i in range(8):
                to = leaf_cols(i if which == 0 else 7 - i)
                mine[:, to] = acc[0:8, leaf_cols(i)] * (8.0 / LEAF)
                other[:, to] = acc[8:16, leaf_cols(i)] * (8.0 / LEAF)


LEVEL_START = [256 - (256 >> u) for u in range(7)]
UPPER = 224
OWN = 30
SIBLING = 33
OWN_UPPER = 36
T_ROWS = 40
C_ROWS = 8


def node(u, other=False):
    n = lax.shift_right_logical(lax.axis_index("leaf"), u)
    return LEVEL_START[u] + (lax.bitwise_xor(n, 1) if other else n)


def pick_matrices(table, want, rows, count, mats, buf):
    pick = hot(iota((rows, 254), 1) == want)

    def step(g, carry):
        out = dot(pick, table[pl.ds(4 * g, 4)].reshape(256, 254), NT)
        for j in range(4):
            at = pl.multiple_of((4 * g + j) * rows, 8)
            buf[pl.ds(at, rows), :64] = out[:, 64 * j : 64 * j + 64]
        return carry

    lax.fori_loop(0, 16, step, 0, unroll=4)
    for m in range(count):
        mats[64 * m : 64 * m + 64, :] = buf[pl.ds(m, 64, stride=rows), :][:, :64].astype(bf16)


def transfers_kernel(ut, mats, buf):
    row = iota((T_ROWS, 254), 0)
    want = jnp.where(row < 30, row + UPPER, -1)
    for u in range(3):
        want = jnp.where(row == OWN + u, node(u), want)
        want = jnp.where(row == SIBLING + u, node(u, True), want)
        want = jnp.where(row == OWN_UPPER + u, node(u + 3), want)
    pick_matrices(ut, want, T_ROWS, 39, mats, buf)


def couplings_kernel(uc, seen, mats, buf):
    row = iota((C_ROWS, 254), 0)
    want = jnp.zeros((C_ROWS, 254), i32) - 1
    for u in range(7):
        want = jnp.where(row == u, node(u, u < 3), want)
    pick_matrices(uc, want, C_ROWS, 7, mats, buf)


def middle_kernel(
    recv_in, path_in, mats_in, coup_in, send, recv, path, mats, coup, ext, xs, gain, sems
):
    device = lax.axis_index("leaf")
    for copy in fetch(
        sems, (recv_in, recv), (path_in, path), (mats_in, mats), (coup_in, coup)
    ):
        copy.wait()
    ext[...] = recv[:, 512:640].astype(f32)

    labels = jnp.concatenate(
        [jnp.transpose(ext[128 * i : 128 * i + 128, :])[64:65, :] for i in range(4)], axis=1
    )
    row, lane = iota((256, 512), 0), iota((256, 512), 1)
    wanted = ((row & 31) + 1).astype(f32)
    fits = lax.shift_right_logical(row, 5) == (lax.shift_right_logical(lane, 2) & 7)
    sums = dot(hot((labels == wanted) & fits), recv[:, 0:512])

    for g in range(16):
        rows = ext[32 * g : 32 * g + 16, :64]
        xs[8 * g : 8 * g + 8, :] = rows[:8] + rows[8:]
    first, n = 0, 16
    firsts = {3: 0}
    for u in range(3, 6):
        for m in range(n // 2):
            r = 8 * (first + 2 * m)
            e = LEVEL_START[u] - UPPER + 2 * m
            pair = jnp.concatenate([xs[r : r + 8, :], xs[r + 8 : r + 16, :]], axis=1)
            w = own_matrix(mats, e, 2)
            t = 8 * (first + n + m)
            xs[t : t + 8, :] = dot_pair(pair, w)
        first += n
        n //= 2
        firsts[u + 1] = first
    for u in range(7):
        if u < 3:
            partner = path[8 * u : 8 * u + 8, :]
        else:
            sib = lax.bitwise_xor(lax.shift_right_logical(device, u), 1)
            partner = xs[pl.ds(pl.multiple_of((firsts[u] + sib) * 8, 8), 8), :]
        gain[8 * u : 8 * u + 8, :] = dot_pair(partner, own_matrix(coup, u))
    down = gain[48:56, :]
    for u in (5, 4, 3):
        w = own_matrix(mats, OWN_UPPER + u - 3)
        down = dot_pair(down, w, NT) + gain[8 * u : 8 * u + 8, :]
    lines = {}
    for u in (2, 1, 0):
        both = jnp.concatenate(
            [own_matrix(mats, OWN + u), own_matrix(mats, SIBLING + u)], axis=0
        )
        spread = dot_pair(down, both, NT)
        lines[u] = flat(spread[:, 64:] + gain[8 * u : 8 * u + 8, :])
        down = spread[:, :64]
    own_line = flat(down)
    z = device & 7
    last = iota((32, 512), 0) == 31
    for peer in range(8):
        x = lax.bitwise_xor(z, peer)
        line = jnp.where(x == 0, own_line, lines[0])
        line = jnp.where(x >= 2, lines[1], line)
        line = jnp.where(x >= 4, lines[2], line)
        block = jnp.where(last, line, sums[32 * peer : 32 * peer + 32])
        send[32 * peer : 32 * peer + 32, :] = block.astype(bf16)


def flat(x):
    return jnp.concatenate([x[v : v + 1] for v in range(8)], axis=1)


def final_kernel(
    recv_in, mine_in, other_in, mats_in, tr, bases, perm_in, out,
    recv, near_mine, near_other, mats, perm, cpl, dwn, dn, tree, sems,
):
    copies = fetch(
        sems,
        (recv_in, recv),
        (mats_in.at[64 * OWN : 64 * OWN + 128], mats),
        (mine_in, near_mine),
        (other_in, near_other),
        (perm_in, perm),
    )
    for copy in copies:
        copy.wait()
    device = lax.axis_index("leaf")
    core = lax.axis_index("vec")
    z = device & 7
    total = jnp.zeros((32, 512), f32)
    levels = [jnp.zeros((1, 512), f32)] * 3
    for peer in range(8):
        block = recv[32 * peer : 32 * peer + 32, :].astype(f32)
        total = total + block
        x = lax.bitwise_xor(z, peer)
        line = block[31:32]
        for i, use in enumerate((x >= 4, (x >= 2) & (x < 4), x < 2)):
            levels[i] = levels[i] + jnp.where(use, line, 0.0)
    levels = jnp.concatenate(levels + [jnp.zeros((5, 512), f32)], axis=0)
    for v in range(8):
        cpl[pl.ds(v, 32, stride=8), :] = wide(total[:, 64 * v : 64 * v + 64])
        dwn[pl.ds(v, 8, stride=8), :] = wide(levels[:, 64 * v : 64 * v + 64])
    down = dot_pair(dwn[0:8, :64], own_matrix(mats, 1), NT) + dwn[8:16, :64]
    down = dot_pair(down, own_matrix(mats, 0), NT) + dwn[16:24, :64]

    dn[240:248, :] = down + cpl[240:248, :64]
    n = 1
    while n < 16:
        off_parent = 32 - 2 * n
        n *= 2
        off = 32 - 2 * n
        for m in range(n // 2):
            r = 8 * (off_parent + m)
            w = tr[off + 2 * m : off + 2 * m + 2].reshape(128, 64)
            both = dot_pair(dn[r : r + 8, :], w, NT)
            t = 8 * (off + 2 * m)
            dn[t : t + 8, :] = both[:, :64] + cpl[t : t + 8, :64]
            dn[t + 8 : t + 16, :] = both[:, 64:] + cpl[t + 8 : t + 16, :64]
    for leaf in range(16):
        tree[:, LEAF * leaf : LEAF * leaf + LEAF] = dot(
            dn[8 * leaf : 8 * leaf + 8, :].astype(bf16), bases[leaf]
        )

    @pl.when(core == 0)
    def _():
        tree[:, :HALF] += near_mine[...]
        tree[:, HALF:] += near_other[...]

    @pl.when(core == 1)
    def _():
        tree[:, :HALF] += near_other[...]
        tree[:, HALF:] += near_mine[...]

    width = 512
    total = jnp.zeros((256, 256), f32)
    for b in range(COLS // width):
        cols = slice(b * width, (b + 1) * width)
        index = perm[:, cols]
        select = hot(iota((256, width), 0) == (index & 255))
        high = jnp.broadcast_to(lax.shift_right_logical(index, 8), (8, width))
        values = tree[:, cols]
        spread = jnp.concatenate(
            [jnp.where(high == q, values, 0.0) for q in range(32)], axis=0
        ).astype(bf16)
        total = total + dot(spread, select, NT)
    for q in range(32):
        out[:, 256 * q : 256 * q + 256] = total[8 * q : 8 * q + 8].astype(bf16)


def shards(
    points, vectors, leaf_order, leaf_bases, transfers, coupling_blocks,
    block_source, block_owner, block_target, up_transfer, up_coupling,
):
    peers = lax.axis_size("leaf")
    axes = ("leaf", "vec")
    vt, pt, send_c = call(
        gather_kernel,
        [((8, COLS), bf16), ((8, COLS), bf16), ((8, LOCAL), bf16)],
        [
            pltpu.VMEM((3, COLS), bf16), pltpu.VMEM((8, COLS), bf16), pltpu.VMEM((1, COLS), i32),
            pltpu.VMEM((256, 256), bf16), pltpu.VMEM((128, 256), f32), pltpu.SemaphoreType.DMA((3,)),
        ],
        (points, vectors, leaf_order), "hhh>vvv",
        2 * 384 * 256 * COLS, 1 << 20,
    )
    pairs_c = []
    pairs_a = [(0, 2 * peers - 1), (2 * peers - 1, 0)]
    for d in range(peers):
        pairs_c += [(2 * d, 2 * d + 1), (2 * d + 1, 2 * d)]
        if d + 1 < peers:
            pairs_a += [(2 * d + 1, 2 * d + 2), (2 * d + 2, 2 * d + 1)]
    rec_c = lax.ppermute(send_c, axes, pairs_c)
    ut = jnp.transpose(up_transfer, (1, 2, 0))
    uc = jnp.transpose(up_coupling, (1, 2, 0))
    (mats,) = call(
        transfers_kernel,
        [((64 * T_ROWS, 64), bf16)],
        [pltpu.VMEM((64 * T_ROWS, 128), f32)],
        (ut,), "v>v",
        2 * 4096 * 256 * 40, 3 << 20,
    )
    cf, path, halo = call(
        coeff_kernel,
        [((256, 128), f32), ((32, 64), f32), ((24, HALO), bf16)],
        [],
        (vt, pt, rec_c, leaf_bases, transfers, mats), "vvvvvv>vvv",
        2 * 512 * 512 * 256, 2 << 20,
    )
    halo = lax.ppermute(halo, axes, pairs_a)
    (send,) = call(
        product_kernel,
        [((512, 640), bf16)],
        [pltpu.VMEM((1024, 128), f32), pltpu.VMEM((640, 256), bf16)],
        (
            cf, path, jnp.transpose(coupling_blocks, (1, 2, 0)),
            block_source.reshape(1, -1), block_owner.reshape(1, -1), block_target.reshape(1, -1),
        ), "vvvvvv>v",
        2 * 512 * 256 * 640, 4 << 20,
    )
    send, halo = lax.optimization_barrier((send, halo))
    near_groups = [[xy * 8 + z for z in range(8)] for xy in range(peers // 8)]
    far_groups = [[xy * 8 + z for xy in range(peers // 8)] for z in range(8)]
    recv = lax.all_to_all(
        send, "leaf", split_axis=0, concat_axis=0, tiled=True, axis_index_groups=far_groups
    )
    buffers = [
        pltpu.VMEM((8, COLS), bf16), pltpu.VMEM((8, COLS), bf16), pltpu.VMEM((8, LOCAL), bf16),
        pltpu.VMEM((16, 6144), bf16), pltpu.VMEM((6144, 16), bf16), pltpu.VMEM((16, 6144), bf16),
        pltpu.VMEM((8, 6144), f32), pltpu.VMEM((16, HALF), f32), pltpu.SemaphoreType.DMA((6,)),
    ]
    (coup,) = call(
        couplings_kernel,
        [((64 * C_ROWS, 64), bf16)],
        [pltpu.VMEM((64 * C_ROWS, 128), f32)],
        (uc, send), "va>v",
        2 * 4096 * 256 * 8, 3 << 20,
    )
    (begun,) = call(
        near_first_kernel,
        [((16, LEAF * (10 - SPLIT)), f32)],
        buffers + [pltpu.SemaphoreType.DMA((5,))],
        (vt, pt, rec_c), "aaa>h",
        2 * 37 * 512 * 512 * 256, 1 << 20, vmem=24,
    )
    (send,) = call(
        middle_kernel,
        [((256, 512), bf16)],
        [
            pltpu.VMEM((512, 640), bf16), pltpu.VMEM((32, 64), f32),
            pltpu.VMEM((64 * T_ROWS, 64), bf16), pltpu.VMEM((64 * C_ROWS, 64), bf16),
            pltpu.VMEM((512, 128), f32), pltpu.VMEM((256, 64), f32), pltpu.VMEM((56, 64), f32),
            pltpu.SemaphoreType.DMA((4,)),
        ],
        (recv, path, mats, coup), "aaaa>v",
        2 * 256 * 512 * 512, 2 << 20,
    )
    recv = lax.all_to_all(
        send, "leaf", split_axis=0, concat_axis=0, tiled=True, axis_index_groups=near_groups
    )
    near_mine, near_send = call(
        near_rest_kernel,
        [((8, HALF), f32), ((8, HALF), f32)],
        buffers + [pltpu.VMEM((24, HALO), bf16)],
        (vt, pt, rec_c, halo, begun), "aaaah>vv",
        2 * 30 * 512 * 512 * 256, 1 << 20, vmem=24,
    )
    near_other = lax.ppermute(near_send, axes, pairs_c)
    (out,) = call(
        final_kernel,
        [((8, COLS), bf16)],
        [
            pltpu.VMEM((256, 512), bf16), pltpu.VMEM((8, HALF), f32), pltpu.VMEM((8, HALF), f32),
            pltpu.VMEM((128, 64), bf16), pltpu.VMEM((1, COLS), i32),
            pltpu.VMEM((256, 128), f32), pltpu.VMEM((64, 128), f32),
            pltpu.VMEM((248, 64), f32), pltpu.VMEM((8, COLS), f32), pltpu.SemaphoreType.DMA((5,)),
        ],
        (recv, near_mine, near_other, mats, transfers, leaf_bases, leaf_order), "aaaavvh>v",
        2 * 256 * 256 * COLS, 8 << 20,
    )
    return out


def solution(mesh):
    return jax.shard_map(
        shards,
        mesh=mesh,
        in_specs=(
            P(None, "leaf"),
            P("vec", "leaf"),
            P("leaf", None),
            P("leaf", None, None),
            P("leaf", None, None),
            P("leaf", None, None),
            P("leaf"),
            P("leaf", None),
            P("leaf"),
            P(),
            P(),
        ),
        out_specs=P("vec", "leaf"),
        check_vma=False,
    )
```

```python
import jax
import jax.numpy as jnp
import ml_dtypes
from jax import lax
from jax.experimental import pallas as pl
from jax.experimental.pallas import tpu as pltpu
from jax.sharding import PartitionSpec as P

f32 = jnp.float32
bf16 = jnp.bfloat16
i32 = jnp.int32

LEAF = 512
COLS = 8192
HALO = 1024
LOCAL = 5120
HALF = 4096
NT = (((1,), (1,)), ((), ()))
TN = (((0,), (0,)), ((), ()))
SMOOTH_HI = float(ml_dtypes.bfloat16(0.0025))
SMOOTH_LO = float(ml_dtypes.bfloat16(0.0025 - SMOOTH_HI))
VM = pl.BlockSpec(memory_space=pltpu.VMEM)


def dot(a, b, dims=(((1,), (0,)), ((), ()))):
    return lax.dot_general(a, b, dims, preferred_element_type=f32)


def iota(shape, dim):
    return lax.broadcasted_iota(i32, shape, dim)


def hot(mask):
    return jnp.where(mask, 1.0, 0.0).astype(bf16)


def halves(x):
    hi = x.astype(bf16)
    lo = (x - hi.astype(f32)).astype(bf16)
    return jnp.concatenate([hi, lo], axis=0)


def wide(x):
    return jnp.concatenate([x, jnp.zeros_like(x)], axis=1)


def dot_pair(x, w, dims=(((1,), (0,)), ((), ()))):
    y = dot(halves(x), w, dims)
    n = x.shape[0]
    return y[:n] + y[n:]


ANY = pl.BlockSpec(memory_space=pl.ANY)
SPEC = {"v": VM, "a": ANY, "h": pl.BlockSpec(memory_space=pltpu.HBM)}


def call(kernel, outs, scratch, args, kinds, flops, nbytes, vmem=16):
    ins, results = kinds.split(">")
    args = [
        pltpu.with_memory_space_constraint(x, pltpu.HBM) if k == "h" else x
        for x, k in zip(args, ins)
    ]
    return pl.pallas_call(
        kernel,
        out_shape=[
            pltpu.HBM(s, d) if k == "h" else jax.ShapeDtypeStruct(s, d)
            for (s, d), k in zip(outs, results)
        ],
        in_specs=[SPEC[k] for k in ins],
        out_specs=[SPEC[k] for k in results],
        scratch_shapes=scratch,
        compiler_params=pltpu.CompilerParams(vmem_limit_bytes=vmem << 20),
        cost_estimate=pl.CostEstimate(flops=flops, bytes_accessed=nbytes, transcendentals=0),
    )(*args)


def fetch(sems, *pairs):
    copies = [
        pltpu.make_async_copy(src, dst, sems.at[i]) for i, (src, dst) in enumerate(pairs)
    ]
    for copy in copies:
        copy.start()
    return copies


def gather_kernel(
    pts_in, vec_in, perm_in, vt, pt, send_c, pts, vec, perm, dv, dp, sems
):
    core = lax.axis_index("vec")
    for copy in fetch(sems, (perm_in, perm), (vec_in, vec), (pts_in, pts)):
        copy.wait()
    for m in range(16):
        a, b = 512 * m, 512 * m + 256
        dv[16 * m : 16 * m + 16, :] = jnp.concatenate(
            [vec[:, a : a + 256], vec[:, b : b + 256]], axis=0
        )
        three = pts[:, a : a + 512].astype(f32)
        four = jnp.concatenate([three, jnp.zeros((1, 512), f32)], axis=0)
        dp[8 * m : 8 * m + 8, :] = jnp.concatenate([four[:, :256], four[:, 256:]], axis=0)
    data_v = dv[...]
    data_p = dp[...].astype(bf16)
    width = 512
    for n in range(COLS // width):
        cols = slice(n * width, (n + 1) * width)
        index = perm[:, cols]
        low = index & 255
        high = jnp.broadcast_to(lax.shift_right_logical(index, 8), (8, width))
        select = hot(iota((256, width), 0) == low)
        got = dot(data_v, select)
        out = got[:8]
        for q in range(1, 32):
            out = jnp.where(high == q, got[8 * q : 8 * q + 8], out)
        vt[:, cols] = out.astype(bf16)
        got = dot(data_p, select)
        pair = high - iota((8, width), 0) // 4
        out = jnp.zeros((8, width), f32)
        for m in range(16):
            out = jnp.where(pair == 2 * m, got[8 * m : 8 * m + 8], out)
        out = out[:4] + out[4:]
        pt[:, cols] = jnp.concatenate([out, jnp.zeros((4, width), f32)], axis=0).astype(bf16)

    @pl.when(core == 0)
    def _():
        send_c[...] = vt[:, COLS - LOCAL :]

    @pl.when(core == 1)
    def _():
        send_c[...] = vt[:, :LOCAL]


def coeff_kernel(vt, pt, rec_c, bases, tr, mats, cf, path, halo):
    core = lax.axis_index("vec")
    ends = ((slice(0, HALO), slice(0, HALO)), (slice(COLS - HALO, COLS), slice(LOCAL - HALO, LOCAL)))
    for which, (cols, other) in enumerate(ends):

        @pl.when(core == which)
        def _():
            halo[0:8, :] = vt[:, cols]
            halo[8:16, :] = rec_c[:, other]
            halo[16:24, :] = pt[:, cols]

    cf[248:256, :] = jnp.zeros((8, 128), f32)
    for leaf in range(16):
        cf[8 * leaf : 8 * leaf + 8, :64] = dot(
            vt[:, LEAF * leaf : LEAF * leaf + LEAF], bases[leaf], NT
        )
    off, n = 0, 16
    while n > 1:
        for m in range(n // 2):
            r = 8 * (off + 2 * m)
            pair = jnp.concatenate([cf[r : r + 8, :64], cf[r + 8 : r + 16, :64]], axis=1)
            w = tr[off + 2 * m : off + 2 * m + 2].reshape(128, 64)
            t = 8 * (off + n + m)
            cf[t : t + 8, :64] = dot_pair(pair, w)
        off += n
        n //= 2
    value = cf[240:248, :64]
    for u in range(3):
        path[8 * u : 8 * u + 8, :] = value
        value = dot_pair(value, own_matrix(mats, OWN + u))
    path[24:32, :] = value


def own_matrix(mats, row, count=1):
    return mats[64 * row : 64 * (row + count), :]


def product_kernel(
    cf, path, cp, bsrc, bown, btgt, send, pick, prod
):
    source = hot(iota((32, 256), 0) == bsrc[...])
    for v in range(8):
        mine = cf[pl.ds(v, 32, stride=8), :][:, :64].astype(bf16)
        chosen = dot(mine, source, TN)
        pick[pl.ds(v, 64, stride=8), :] = chosen[:, :128]
        pick[pl.ds(512 + v, 64, stride=8), :] = chosen[:, 128:]
    for half in range(2):
        lanes = slice(128 * half, 128 * half + 128)
        for pb in range(4):
            rows = slice(16 * pb, 16 * pb + 16)

            acc = [jnp.zeros((16, 128), f32)] * 8
            for k in range(64):
                block = cp[k, rows, lanes].astype(f32)
                for v in range(8):
                    row = pick[pl.ds(512 * half + 8 * k + v, 8, stride=0), :]
                    acc[v] = acc[v] + jnp.concatenate([row, row], axis=0) * block
            for v in range(8):
                top = 64 * v + 16 * pb
                prod[top : top + 16, lanes] = acc[v].astype(bf16)
    prod[512:576, :] = jnp.zeros((64, 256), bf16)
    prod[576:640, :] = jnp.broadcast_to((btgt[...] + 1).astype(f32), (64, 256)).astype(bf16)
    owner = bown[...]
    owner_f = owner.astype(f32)
    column = jnp.transpose(jnp.broadcast_to(owner_f, (128, 256)))
    ranks = []
    for half in range(2):
        row = owner_f[:, 128 * half : 128 * half + 128]
        before = iota((256, 128), 0) < iota((256, 128), 1) + 128 * half
        same = jnp.where((column == row) & before, 1.0, 0.0)
        ranks.append(jnp.sum(same, axis=0, keepdims=True))
    place = owner * 4 + jnp.concatenate(ranks, axis=1).astype(i32)
    top = path[24:32, :]
    high = top.astype(bf16).astype(f32)
    extra = jnp.concatenate([high, top - high, jnp.zeros((16, 64), f32)], axis=0)
    extra = wide(extra)
    payload = prod[...]
    for part in range(2):
        rows = slice(256 * part, 256 * part + 256)
        slots = hot(iota((256, 256), 0) + 256 * part == place)
        out = dot(slots, payload, NT)
        send[rows, 0:512] = out[:, :512].astype(bf16)
        tail = out[:, 512:].reshape(8, 32, 128) + extra[None]
        send[rows, 512:640] = tail.reshape(256, 128).astype(bf16)


def split3(x):
    a = x.astype(bf16).astype(f32)
    b = (x - a).astype(bf16).astype(f32)
    return a, b, x - a - b


def leaf_cols(leaf):
    return slice(LEAF * leaf, LEAF * leaf + LEAF)


def load_window(vt, pt, rec_c, halo, leaves, vw, pw):
    core = lax.axis_index("vec")
    for which in range(2):

        @pl.when(core == which)
        def _():
            for w in leaves:
                to = leaf_cols(w)
                if w < 2:
                    near_cols = leaf_cols(w if which == 0 else 1 - w)
                    vw[0:8, to] = halo[8:16, near_cols]
                    vw[8:16, to] = halo[0:8, near_cols]
                    pw[:, to] = halo[16:24, near_cols].astype(f32)
                else:
                    local = leaf_cols(w - 2 if which == 0 else 17 - w)
                    vw[0:8, to] = vt[:, local]
                    vw[8:16, to] = rec_c[:, leaf_cols(w - 2 if which == 0 else 11 - w)]
                    pw[:, to] = pt[:, local].astype(f32)


def features(leaves, pw, fs, ft):
    for leaf in leaves:
        cols = leaf_cols(leaf)
        p = pw[0:3, cols]
        norm = p[0:1] * p[0:1] + p[1:2] * p[1:2] + p[2:3] * p[2:3]
        parts = jnp.concatenate(split3(norm), axis=0)
        one = jnp.ones((3, LEAF), f32)
        two = jnp.ones((2, LEAF), f32)
        pad = jnp.zeros((5, LEAF), f32)
        source = jnp.concatenate([p, parts, one, two, pad], axis=0)
        smooth = jnp.where(iota((2, LEAF), 0) == 0, SMOOTH_HI, SMOOTH_LO)
        target = jnp.concatenate([-2.0 * p, one, parts, smooth, pad], axis=0)
        fs[cols, :] = jnp.transpose(source).astype(bf16)
        ft[:, cols] = target.astype(bf16)


def near_target(t, vw, fs, ft, acc):
    tc = leaf_cols(t)
    total = jnp.zeros((16, LEAF), f32)
    for s in range(t - 2, t + 3):
        if 2 <= s < t:
            continue
        sc = leaf_cols(s)
        kernel = lax.rsqrt(dot(fs[sc, :], ft[:, tc])).astype(bf16)
        total = total + dot(vw[:, sc], kernel)
        if t < s < 10:
            acc[:, leaf_cols(s - 2)] += dot(vw[:, tc], kernel, NT)
    acc[:, leaf_cols(t - 2)] += total


SPLIT = 5


def near_first_kernel(
    vt_in, pt_in, c_in, begun, vt, pt, rec_c, vw, fs, ft, pw, acc, sems, out_sems
):
    for copy in fetch(sems, (vt_in, vt), (pt_in, pt), (c_in, rec_c)):
        copy.wait()
    load_window(vt, pt, rec_c, None, range(SPLIT, 12), vw, pw)
    features(range(SPLIT, 12), pw, fs, ft)
    acc[...] = jnp.zeros_like(acc)
    copies = []
    for t in range(SPLIT, 10):
        near_target(t, vw, fs, ft, acc)
        src, dst = acc.at[:, leaf_cols(t - 2)], begun.at[:, leaf_cols(t - SPLIT)]
        copies += [pltpu.make_async_copy(src, dst, out_sems.at[t - SPLIT])]
        copies[-1].start()
    for copy in copies:
        copy.wait()


def near_rest_kernel(
    vt_in, pt_in, c_in, halo_in, begun, mine, other,
    vt, pt, rec_c, vw, fs, ft, pw, acc, sems, halo,
):
    left = LEAF * (SPLIT - 2)
    copies = fetch(
        sems, (vt_in, vt), (pt_in, pt), (c_in, rec_c), (halo_in, halo),
        (begun, acc.at[:, left:]),
    )
    acc[:, :left] = jnp.zeros((16, left), f32)
    for copy in copies[:4]:
        copy.wait()
    core = lax.axis_index("vec")
    end = lax.axis_index("leaf") == (lax.axis_size("leaf") - 1) * core

    @pl.when(end)
    def _():
        halo[...] = jnp.zeros_like(halo)

    load_window(vt, pt, rec_c, halo, range(0, SPLIT + 2), vw, pw)
    features(range(0, SPLIT + 2), pw, fs, ft)
    copies[4].wait()
    for t in range(2, SPLIT):
        near_target(t, vw, fs, ft, acc)
    for which in range(2):

        @pl.when(core == which)
        def _():
            for i in range(8):
                to = leaf_cols(i if which == 0 else 7 - i)
                mine[:, to] = acc[0:8, leaf_cols(i)] * (8.0 / LEAF)
                other[:, to] = acc[8:16, leaf_cols(i)] * (8.0 / LEAF)


LEVEL_START = [256 - (256 >> u) for u in range(7)]
UPPER = 224
OWN = 30
SIBLING = 33
OWN_UPPER = 36
T_ROWS = 40
C_ROWS = 8


def node(u, other=False):
    n = lax.shift_right_logical(lax.axis_index("leaf"), u)
    return LEVEL_START[u] + (lax.bitwise_xor(n, 1) if other else n)


def pick_matrices(table, want, rows, count, mats, buf):
    pick = hot(iota((rows, 254), 1) == want)

    def step(g, carry):
        out = dot(pick, table[pl.ds(4 * g, 4)].reshape(256, 254), NT)
        for j in range(4):
            at = pl.multiple_of((4 * g + j) * rows, 8)
            buf[pl.ds(at, rows), :64] = out[:, 64 * j : 64 * j + 64]
        return carry

    lax.fori_loop(0, 16, step, 0, unroll=4)
    for m in range(count):
        mats[64 * m : 64 * m + 64, :] = buf[pl.ds(m, 64, stride=rows), :][:, :64].astype(bf16)


def transfers_kernel(ut, mats, buf):
    row = iota((T_ROWS, 254), 0)
    want = jnp.where(row < 30, row + UPPER, -1)
    for u in range(3):
        want = jnp.where(row == OWN + u, node(u), want)
        want = jnp.where(row == SIBLING + u, node(u, True), want)
        want = jnp.where(row == OWN_UPPER + u, node(u + 3), want)
    pick_matrices(ut, want, T_ROWS, 39, mats, buf)


def couplings_kernel(uc, seen, mats, buf):
    row = iota((C_ROWS, 254), 0)
    want = jnp.zeros((C_ROWS, 254), i32) - 1
    for u in range(7):
        want = jnp.where(row == u, node(u, u < 3), want)
    pick_matrices(uc, want, C_ROWS, 7, mats, buf)


def middle_kernel(
    recv_in, path_in, mats_in, coup_in, send, recv, path, mats, coup, ext, xs, gain, sems
):
    device = lax.axis_index("leaf")
    for copy in fetch(
        sems, (recv_in, recv), (path_in, path), (mats_in, mats), (coup_in, coup)
    ):
        copy.wait()
    ext[...] = recv[:, 512:640].astype(f32)

    labels = jnp.concatenate(
        [jnp.transpose(ext[128 * i : 128 * i + 128, :])[64:65, :] for i in range(4)], axis=1
    )
    row, lane = iota((256, 512), 0), iota((256, 512), 1)
    wanted = ((row & 31) + 1).astype(f32)
    fits = lax.shift_right_logical(row, 5) == (lax.shift_right_logical(lane, 2) & 7)
    sums = dot(hot((labels == wanted) & fits), recv[:, 0:512])

    for g in range(16):
        rows = ext[32 * g : 32 * g + 16, :64]
        xs[8 * g : 8 * g + 8, :] = rows[:8] + rows[8:]
    first, n = 0, 16
    firsts = {3: 0}
    for u in range(3, 6):
        for m in range(n // 2):
            r = 8 * (first + 2 * m)
            e = LEVEL_START[u] - UPPER + 2 * m
            pair = jnp.concatenate([xs[r : r + 8, :], xs[r + 8 : r + 16, :]], axis=1)
            w = own_matrix(mats, e, 2)
            t = 8 * (first + n + m)
            xs[t : t + 8, :] = dot_pair(pair, w)
        first += n
        n //= 2
        firsts[u + 1] = first
    for u in range(7):
        if u < 3:
            partner = path[8 * u : 8 * u + 8, :]
        else:
            sib = lax.bitwise_xor(lax.shift_right_logical(device, u), 1)
            partner = xs[pl.ds(pl.multiple_of((firsts[u] + sib) * 8, 8), 8), :]
        gain[8 * u : 8 * u + 8, :] = dot_pair(partner, own_matrix(coup, u))
    down = gain[48:56, :]
    for u in (5, 4, 3):
        w = own_matrix(mats, OWN_UPPER + u - 3)
        down = dot_pair(down, w, NT) + gain[8 * u : 8 * u + 8, :]
    lines = {}
    for u in (2, 1, 0):
        both = jnp.concatenate(
            [own_matrix(mats, OWN + u), own_matrix(mats, SIBLING + u)], axis=0
        )
        spread = dot_pair(down, both, NT)
        lines[u] = flat(spread[:, 64:] + gain[8 * u : 8 * u + 8, :])
        down = spread[:, :64]
    own_line = flat(down)
    z = device & 7
    last = iota((32, 512), 0) == 31
    for peer in range(8):
        x = lax.bitwise_xor(z, peer)
        line = jnp.where(x == 0, own_line, lines[0])
        line = jnp.where(x >= 2, lines[1], line)
        line = jnp.where(x >= 4, lines[2], line)
        block = jnp.where(last, line, sums[32 * peer : 32 * peer + 32])
        send[32 * peer : 32 * peer + 32, :] = block.astype(bf16)


def flat(x):
    return jnp.concatenate([x[v : v + 1] for v in range(8)], axis=1)


def final_kernel(
    recv_in, mine_in, other_in, mats_in, tr, bases, perm_in, out,
    recv, near_mine, near_other, mats, perm, cpl, dwn, dn, tree, sems,
):
    copies = fetch(
        sems,
        (recv_in, recv),
        (mats_in.at[64 * OWN : 64 * OWN + 128], mats),
        (mine_in, near_mine),
        (other_in, near_other),
        (perm_in, perm),
    )
    for copy in copies:
        copy.wait()
    device = lax.axis_index("leaf")
    core = lax.axis_index("vec")
    z = device & 7
    total = jnp.zeros((32, 512), f32)
    levels = [jnp.zeros((1, 512), f32)] * 3
    for peer in range(8):
        block = recv[32 * peer : 32 * peer + 32, :].astype(f32)
        total = total + block
        x = lax.bitwise_xor(z, peer)
        line = block[31:32]
        for i, use in enumerate((x >= 4, (x >= 2) & (x < 4), x < 2)):
            levels[i] = levels[i] + jnp.where(use, line, 0.0)
    levels = jnp.concatenate(levels + [jnp.zeros((5, 512), f32)], axis=0)
    for v in range(8):
        cpl[pl.ds(v, 32, stride=8), :] = wide(total[:, 64 * v : 64 * v + 64])
        dwn[pl.ds(v, 8, stride=8), :] = wide(levels[:, 64 * v : 64 * v + 64])
    down = dot_pair(dwn[0:8, :64], own_matrix(mats, 1), NT) + dwn[8:16, :64]
    down = dot_pair(down, own_matrix(mats, 0), NT) + dwn[16:24, :64]

    dn[240:248, :] = down + cpl[240:248, :64]
    n = 1
    while n < 16:
        off_parent = 32 - 2 * n
        n *= 2
        off = 32 - 2 * n
        for m in range(n // 2):
            r = 8 * (off_parent + m)
            w = tr[off + 2 * m : off + 2 * m + 2].reshape(128, 64)
            both = dot_pair(dn[r : r + 8, :], w, NT)
            t = 8 * (off + 2 * m)
            dn[t : t + 8, :] = both[:, :64] + cpl[t : t + 8, :64]
            dn[t + 8 : t + 16, :] = both[:, 64:] + cpl[t + 8 : t + 16, :64]
    for leaf in range(16):
        tree[:, LEAF * leaf : LEAF * leaf + LEAF] = dot(
            dn[8 * leaf : 8 * leaf + 8, :].astype(bf16), bases[leaf]
        )

    @pl.when(core == 0)
    def _():
        tree[:, :HALF] += near_mine[...]
        tree[:, HALF:] += near_other[...]

    @pl.when(core == 1)
    def _():
        tree[:, :HALF] += near_other[...]
        tree[:, HALF:] += near_mine[...]

    width = 512
    total = jnp.zeros((256, 256), f32)
    for b in range(COLS // width):
        cols = slice(b * width, (b + 1) * width)
        index = perm[:, cols]
        select = hot(iota((256, width), 0) == (index & 255))
        high = jnp.broadcast_to(lax.shift_right_logical(index, 8), (8, width))
        values = tree[:, cols]
        spread = jnp.concatenate(
            [jnp.where(high == q, values, 0.0) for q in range(32)], axis=0
        ).astype(bf16)
        total = total + dot(spread, select, NT)
    for q in range(32):
        out[:, 256 * q : 256 * q + 256] = total[8 * q : 8 * q + 8].astype(bf16)


def shards(
    points, vectors, leaf_order, leaf_bases, transfers, coupling_blocks,
    block_source, block_owner, block_target, up_transfer, up_coupling,
):
    peers = lax.axis_size("leaf")
    axes = ("leaf", "vec")
    vt, pt, send_c = call(
        gather_kernel,
        [((8, COLS), bf16), ((8, COLS), bf16), ((8, LOCAL), bf16)],
        [
            pltpu.VMEM((3, COLS), bf16), pltpu.VMEM((8, COLS), bf16), pltpu.VMEM((1, COLS), i32),
            pltpu.VMEM((256, 256), bf16), pltpu.VMEM((128, 256), f32), pltpu.SemaphoreType.DMA((3,)),
        ],
        (points, vectors, leaf_order), "hhh>vvv",
        2 * 384 * 256 * COLS, 1 << 20,
    )
    pairs_c = []
    pairs_a = [(0, 2 * peers - 1), (2 * peers - 1, 0)]
    for d in range(peers):
        pairs_c += [(2 * d, 2 * d + 1), (2 * d + 1, 2 * d)]
        if d + 1 < peers:
            pairs_a += [(2 * d + 1, 2 * d + 2), (2 * d + 2, 2 * d + 1)]
    rec_c = lax.ppermute(send_c, axes, pairs_c)
    ut = jnp.transpose(up_transfer, (1, 2, 0))
    uc = jnp.transpose(up_coupling, (1, 2, 0))
    (mats,) = call(
        transfers_kernel,
        [((64 * T_ROWS, 64), bf16)],
        [pltpu.VMEM((64 * T_ROWS, 128), f32)],
        (ut,), "v>v",
        2 * 4096 * 256 * 40, 3 << 20,
    )
    cf, path, halo = call(
        coeff_kernel,
        [((256, 128), f32), ((32, 64), f32), ((24, HALO), bf16)],
        [],
        (vt, pt, rec_c, leaf_bases, transfers, mats), "vvvvvv>vvv",
        2 * 512 * 512 * 256, 2 << 20,
    )
    halo = lax.ppermute(halo, axes, pairs_a)
    (send,) = call(
        product_kernel,
        [((512, 640), bf16)],
        [pltpu.VMEM((1024, 128), f32), pltpu.VMEM((640, 256), bf16)],
        (
            cf, path, jnp.transpose(coupling_blocks, (1, 2, 0)),
            block_source.reshape(1, -1), block_owner.reshape(1, -1), block_target.reshape(1, -1),
        ), "vvvvvv>v",
        2 * 512 * 256 * 640, 4 << 20,
    )
    near_groups = [[xy * 8 + z for z in range(8)] for xy in range(peers // 8)]
    far_groups = [[xy * 8 + z for xy in range(peers // 8)] for z in range(8)]
    recv = lax.all_to_all(
        send, "leaf", split_axis=0, concat_axis=0, tiled=True, axis_index_groups=far_groups
    )
    buffers = [
        pltpu.VMEM((8, COLS), bf16), pltpu.VMEM((8, COLS), bf16), pltpu.VMEM((8, LOCAL), bf16),
        pltpu.VMEM((16, 6144), bf16), pltpu.VMEM((6144, 16), bf16), pltpu.VMEM((16, 6144), bf16),
        pltpu.VMEM((8, 6144), f32), pltpu.VMEM((16, HALF), f32), pltpu.SemaphoreType.DMA((6,)),
    ]
    (coup,) = call(
        couplings_kernel,
        [((64 * C_ROWS, 64), bf16)],
        [pltpu.VMEM((64 * C_ROWS, 128), f32)],
        (uc, send), "va>v",
        2 * 4096 * 256 * 8, 3 << 20,
    )
    (begun,) = call(
        near_first_kernel,
        [((16, LEAF * (10 - SPLIT)), f32)],
        buffers + [pltpu.SemaphoreType.DMA((5,))],
        (vt, pt, rec_c), "aaa>h",
        2 * 37 * 512 * 512 * 256, 1 << 20, vmem=24,
    )
    (send,) = call(
        middle_kernel,
        [((256, 512), bf16)],
        [
            pltpu.VMEM((512, 640), bf16), pltpu.VMEM((32, 64), f32),
            pltpu.VMEM((64 * T_ROWS, 64), bf16), pltpu.VMEM((64 * C_ROWS, 64), bf16),
            pltpu.VMEM((512, 128), f32), pltpu.VMEM((256, 64), f32), pltpu.VMEM((56, 64), f32),
            pltpu.SemaphoreType.DMA((4,)),
        ],
        (recv, path, mats, coup), "aaaa>v",
        2 * 256 * 512 * 512, 2 << 20,
    )
    recv = lax.all_to_all(
        send, "leaf", split_axis=0, concat_axis=0, tiled=True, axis_index_groups=near_groups
    )
    near_mine, near_send = call(
        near_rest_kernel,
        [((8, HALF), f32), ((8, HALF), f32)],
        buffers + [pltpu.VMEM((24, HALO), bf16)],
        (vt, pt, rec_c, halo, begun), "aaaah>vv",
        2 * 30 * 512 * 512 * 256, 1 << 20, vmem=24,
    )
    near_other = lax.ppermute(near_send, axes, pairs_c)
    (out,) = call(
        final_kernel,
        [((8, COLS), bf16)],
        [
            pltpu.VMEM((256, 512), bf16), pltpu.VMEM((8, HALF), f32), pltpu.VMEM((8, HALF), f32),
            pltpu.VMEM((128, 64), bf16), pltpu.VMEM((1, COLS), i32),
            pltpu.VMEM((256, 128), f32), pltpu.VMEM((64, 128), f32),
            pltpu.VMEM((248, 64), f32), pltpu.VMEM((8, COLS), f32), pltpu.SemaphoreType.DMA((5,)),
        ],
        (recv, near_mine, near_other, mats, transfers, leaf_bases, leaf_order), "aaaavvh>v",
        2 * 256 * 256 * COLS, 8 << 20,
    )
    return out


def solution(mesh):
    return jax.shard_map(
        shards,
        mesh=mesh,
        in_specs=(
            P(None, "leaf"),
            P("vec", "leaf"),
            P("leaf", None),
            P("leaf", None, None),
            P("leaf", None, None),
            P("leaf", None, None),
            P("leaf"),
            P("leaf", None),
            P("leaf"),
            P(),
            P(),
        ),
        out_specs=P("vec", "leaf"),
        check_vma=False,
    )
```

```python
import jax
import jax.numpy as jnp
import ml_dtypes
from jax import lax
from jax.experimental import pallas as pl
from jax.experimental.pallas import tpu as pltpu
from jax.sharding import PartitionSpec as P

f32 = jnp.float32
bf16 = jnp.bfloat16
i32 = jnp.int32

LEAF = 512
COLS = 8192
HALO = 1024
LOCAL = 5120
HALF = 4096
NT = (((1,), (1,)), ((), ()))
TN = (((0,), (0,)), ((), ()))
SMOOTH_HI = float(ml_dtypes.bfloat16(0.0025))
SMOOTH_LO = float(ml_dtypes.bfloat16(0.0025 - SMOOTH_HI))
VM = pl.BlockSpec(memory_space=pltpu.VMEM)


def dot(a, b, dims=(((1,), (0,)), ((), ()))):
    return lax.dot_general(a, b, dims, preferred_element_type=f32)


def iota(shape, dim):
    return lax.broadcasted_iota(i32, shape, dim)


def hot(mask):
    return jnp.where(mask, 1.0, 0.0).astype(bf16)


def hot_rows(low, width):
    rows = iota((256, width), 0).astype(bf16)
    match = rows == low.astype(bf16)
    return jnp.where(match, jnp.ones((), bf16), jnp.zeros((), bf16))


def halves(x):
    hi = x.astype(bf16)
    lo = (x - hi.astype(f32)).astype(bf16)
    return jnp.concatenate([hi, lo], axis=0)


def wide(x):
    return jnp.concatenate([x, jnp.zeros_like(x)], axis=1)


def dot_pair(x, w, dims=(((1,), (0,)), ((), ()))):
    y = dot(halves(x), w, dims)
    n = x.shape[0]
    return y[:n] + y[n:]


ANY = pl.BlockSpec(memory_space=pl.ANY)
SPEC = {"v": VM, "a": ANY, "h": pl.BlockSpec(memory_space=pltpu.HBM)}


def call(kernel, outs, scratch, args, kinds, flops, nbytes, vmem=16):
    ins, results = kinds.split(">")
    args = [
        pltpu.with_memory_space_constraint(x, pltpu.HBM) if k == "h" else x
        for x, k in zip(args, ins)
    ]
    return pl.pallas_call(
        kernel,
        out_shape=[
            pltpu.HBM(s, d) if k == "h" else jax.ShapeDtypeStruct(s, d)
            for (s, d), k in zip(outs, results)
        ],
        in_specs=[SPEC[k] for k in ins],
        out_specs=[SPEC[k] for k in results],
        scratch_shapes=scratch,
        compiler_params=pltpu.CompilerParams(vmem_limit_bytes=vmem << 20),
        cost_estimate=pl.CostEstimate(flops=flops, bytes_accessed=nbytes, transcendentals=0),
    )(*args)


def fetch(sems, *pairs):
    copies = [
        pltpu.make_async_copy(src, dst, sems.at[i]) for i, (src, dst) in enumerate(pairs)
    ]
    for copy in copies:
        copy.start()
    return copies


def gather_kernel(
    pts_in, vec_in, perm_in, vt, pt, send_c, pts, vec, perm, dv, dp, sems
):
    core = lax.axis_index("vec")
    for copy in fetch(sems, (perm_in, perm), (vec_in, vec), (pts_in, pts)):
        copy.wait()
    for m in range(16):
        a, b = 512 * m, 512 * m + 256
        dv[16 * m : 16 * m + 16, :] = jnp.concatenate(
            [vec[:, a : a + 256], vec[:, b : b + 256]], axis=0
        )
        three = pts[:, a : a + 512].astype(f32)
        four = jnp.concatenate([three, jnp.zeros((1, 512), f32)], axis=0)
        dp[8 * m : 8 * m + 8, :] = jnp.concatenate([four[:, :256], four[:, 256:]], axis=0)
    data_v = dv[...]
    data_p = dp[...].astype(bf16)
    width = 512
    for n in range(COLS // width):
        cols = slice(n * width, (n + 1) * width)
        index = perm[:, cols]
        low = index & 255
        high = jnp.broadcast_to(lax.shift_right_logical(index, 8), (8, width))
        select = hot_rows(low, width)
        got = dot(data_v, select)
        out = got[:8]
        for q in range(1, 32):
            out = jnp.where(high == q, got[8 * q : 8 * q + 8], out)
        vt[:, cols] = out.astype(bf16)
        got = dot(data_p, select)
        pair = high - iota((8, width), 0) // 4
        out = jnp.zeros((8, width), f32)
        for m in range(16):
            out = jnp.where(pair == 2 * m, got[8 * m : 8 * m + 8], out)
        out = out[:4] + out[4:]
        pt[:, cols] = jnp.concatenate([out, jnp.zeros((4, width), f32)], axis=0).astype(bf16)

    @pl.when(core == 0)
    def _():
        send_c[...] = vt[:, COLS - LOCAL :]

    @pl.when(core == 1)
    def _():
        send_c[...] = vt[:, :LOCAL]


def coeff_kernel(vt, pt, rec_c, bases, tr, mats, cf, path, halo):
    core = lax.axis_index("vec")
    ends = ((slice(0, HALO), slice(0, HALO)), (slice(COLS - HALO, COLS), slice(LOCAL - HALO, LOCAL)))
    for which, (cols, other) in enumerate(ends):

        @pl.when(core == which)
        def _():
            halo[0:8, :] = vt[:, cols]
            halo[8:16, :] = rec_c[:, other]
            halo[16:24, :] = pt[:, cols]

    cf[248:256, :] = jnp.zeros((8, 128), f32)
    for leaf in range(16):
        cf[8 * leaf : 8 * leaf + 8, :64] = dot(
            vt[:, LEAF * leaf : LEAF * leaf + LEAF], bases[leaf], NT
        )
    off, n = 0, 16
    while n > 1:
        for m in range(n // 2):
            r = 8 * (off + 2 * m)
            pair = jnp.concatenate([cf[r : r + 8, :64], cf[r + 8 : r + 16, :64]], axis=1)
            w = tr[off + 2 * m : off + 2 * m + 2].reshape(128, 64)
            t = 8 * (off + n + m)
            cf[t : t + 8, :64] = dot_pair(pair, w)
        off += n
        n //= 2
    value = cf[240:248, :64]
    for u in range(3):
        path[8 * u : 8 * u + 8, :] = value
        value = dot_pair(value, own_matrix(mats, OWN + u))
    path[24:32, :] = value


def own_matrix(mats, row, count=1):
    return mats[64 * row : 64 * (row + count), :]


def product_kernel(
    cf, path, cp, bsrc, bown, btgt, send, pick, prod
):
    source = hot(iota((32, 256), 0) == bsrc[...])
    for v in range(8):
        mine = cf[pl.ds(v, 32, stride=8), :][:, :64].astype(bf16)
        chosen = dot(mine, source, TN)
        pick[pl.ds(v, 64, stride=8), :] = chosen[:, :128]
        pick[pl.ds(512 + v, 64, stride=8), :] = chosen[:, 128:]
    for half in range(2):
        lanes = slice(128 * half, 128 * half + 128)
        for pb in range(4):
            rows = slice(16 * pb, 16 * pb + 16)

            acc = [jnp.zeros((16, 128), f32)] * 8
            for k in range(64):
                block = cp[k, rows, lanes].astype(f32)
                for v in range(8):
                    row = pick[pl.ds(512 * half + 8 * k + v, 8, stride=0), :]
                    acc[v] = acc[v] + jnp.concatenate([row, row], axis=0) * block
            for v in range(8):
                top = 64 * v + 16 * pb
                prod[top : top + 16, lanes] = acc[v].astype(bf16)
    prod[512:576, :] = jnp.zeros((64, 256), bf16)
    prod[576:640, :] = jnp.broadcast_to((btgt[...] + 1).astype(f32), (64, 256)).astype(bf16)
    owner = bown[...]
    owner_f = owner.astype(f32)
    column = jnp.transpose(jnp.broadcast_to(owner_f, (128, 256)))
    ranks = []
    for half in range(2):
        row = owner_f[:, 128 * half : 128 * half + 128]
        before = iota((256, 128), 0) < iota((256, 128), 1) + 128 * half
        same = jnp.where((column == row) & before, 1.0, 0.0)
        ranks.append(jnp.sum(same, axis=0, keepdims=True))
    place = owner * 4 + jnp.concatenate(ranks, axis=1).astype(i32)
    top = path[24:32, :]
    high = top.astype(bf16).astype(f32)
    extra = jnp.concatenate([high, top - high, jnp.zeros((16, 64), f32)], axis=0)
    extra = wide(extra)
    payload = prod[...]
    for part in range(2):
        rows = slice(256 * part, 256 * part + 256)
        slots = hot(iota((256, 256), 0) + 256 * part == place)
        out = dot(slots, payload, NT)
        send[rows, 0:512] = out[:, :512].astype(bf16)
        tail = out[:, 512:].reshape(8, 32, 128) + extra[None]
        send[rows, 512:640] = tail.reshape(256, 128).astype(bf16)


def split3(x):
    a = x.astype(bf16).astype(f32)
    b = (x - a).astype(bf16).astype(f32)
    return a, b, x - a - b


def leaf_cols(leaf):
    return slice(LEAF * leaf, LEAF * leaf + LEAF)


def load_window(vt, pt, rec_c, halo, leaves, vw, pw):
    core = lax.axis_index("vec")
    for which in range(2):

        @pl.when(core == which)
        def _():
            for w in leaves:
                to = leaf_cols(w)
                if w < 2:
                    near_cols = leaf_cols(w if which == 0 else 1 - w)
                    vw[0:8, to] = halo[8:16, near_cols]
                    vw[8:16, to] = halo[0:8, near_cols]
                    pw[:, to] = halo[16:24, near_cols].astype(f32)
                else:
                    local = leaf_cols(w - 2 if which == 0 else 17 - w)
                    vw[0:8, to] = vt[:, local]
                    vw[8:16, to] = rec_c[:, leaf_cols(w - 2 if which == 0 else 11 - w)]
                    pw[:, to] = pt[:, local].astype(f32)


def features(leaves, pw, fs, ft):
    for leaf in leaves:
        cols = leaf_cols(leaf)
        p = pw[0:3, cols]
        norm = p[0:1] * p[0:1] + p[1:2] * p[1:2] + p[2:3] * p[2:3]
        parts = jnp.concatenate(split3(norm), axis=0)
        one = jnp.ones((3, LEAF), f32)
        two = jnp.ones((2, LEAF), f32)
        pad = jnp.zeros((5, LEAF), f32)
        source = jnp.concatenate([p, parts, one, two, pad], axis=0)
        smooth = jnp.where(iota((2, LEAF), 0) == 0, SMOOTH_HI, SMOOTH_LO)
        target = jnp.concatenate([-2.0 * p, one, parts, smooth, pad], axis=0)
        fs[cols, :] = jnp.transpose(source).astype(bf16)
        ft[:, cols] = target.astype(bf16)


def near_target(t, vw, fs, ft, acc):
    tc = leaf_cols(t)
    total = jnp.zeros((16, LEAF), f32)
    for s in range(t - 2, t + 3):
        if 2 <= s < t:
            continue
        sc = leaf_cols(s)
        kernel = lax.rsqrt(dot(fs[sc, :], ft[:, tc])).astype(bf16)
        total = total + dot(vw[:, sc], kernel)
        if t < s < 10:
            acc[:, leaf_cols(s - 2)] += dot(vw[:, tc], kernel, NT)
    acc[:, leaf_cols(t - 2)] += total


SPLIT = 7


def near_first_kernel(
    vt_in, pt_in, c_in, begun, vt, pt, rec_c, vw, fs, ft, pw, acc, sems, out_sems
):
    for copy in fetch(sems, (vt_in, vt), (pt_in, pt), (c_in, rec_c)):
        copy.wait()
    load_window(vt, pt, rec_c, None, range(SPLIT, 12), vw, pw)
    features(range(SPLIT, 12), pw, fs, ft)
    acc[...] = jnp.zeros_like(acc)
    copies = []
    for t in range(SPLIT, 10):
        near_target(t, vw, fs, ft, acc)
        src, dst = acc.at[:, leaf_cols(t - 2)], begun.at[:, leaf_cols(t - SPLIT)]
        copies += [pltpu.make_async_copy(src, dst, out_sems.at[t - SPLIT])]
        copies[-1].start()
    for copy in copies:
        copy.wait()


def near_rest_kernel(
    vt_in, pt_in, c_in, halo_in, begun, mine, other,
    vt, pt, rec_c, vw, fs, ft, pw, acc, sems, halo,
):
    left = LEAF * (SPLIT - 2)
    copies = fetch(
        sems, (vt_in, vt), (pt_in, pt), (c_in, rec_c), (halo_in, halo),
        (begun, acc.at[:, left:]),
    )
    acc[:, :left] = jnp.zeros((16, left), f32)
    for copy in copies[:4]:
        copy.wait()
    core = lax.axis_index("vec")
    end = lax.axis_index("leaf") == (lax.axis_size("leaf") - 1) * core

    @pl.when(end)
    def _():
        halo[...] = jnp.zeros_like(halo)

    load_window(vt, pt, rec_c, halo, range(0, SPLIT + 2), vw, pw)
    features(range(0, SPLIT + 2), pw, fs, ft)
    copies[4].wait()
    for t in range(2, SPLIT):
        near_target(t, vw, fs, ft, acc)
    for which in range(2):

        @pl.when(core == which)
        def _():
            for i in range(8):
                to = leaf_cols(i if which == 0 else 7 - i)
                mine[:, to] = acc[0:8, leaf_cols(i)] * (8.0 / LEAF)
                other[:, to] = acc[8:16, leaf_cols(i)] * (8.0 / LEAF)


LEVEL_START = [256 - (256 >> u) for u in range(7)]
UPPER = 224
OWN = 30
SIBLING = 33
OWN_UPPER = 36
T_ROWS = 40
C_ROWS = 8


def node(u, other=False):
    n = lax.shift_right_logical(lax.axis_index("leaf"), u)
    return LEVEL_START[u] + (lax.bitwise_xor(n, 1) if other else n)


def pick_matrices(table, want, rows, count, mats, buf):
    pick = hot(iota((rows, 254), 1) == want)

    def step(g, carry):
        out = dot(pick, table[pl.ds(4 * g, 4)].reshape(256, 254), NT)
        for j in range(4):
            at = pl.multiple_of((4 * g + j) * rows, 8)
            buf[pl.ds(at, rows), :64] = out[:, 64 * j : 64 * j + 64]
        return carry

    lax.fori_loop(0, 16, step, 0, unroll=4)
    for m in range(count):
        mats[64 * m : 64 * m + 64, :] = buf[pl.ds(m, 64, stride=rows), :][:, :64].astype(bf16)


def transfers_kernel(ut, mats, buf):
    row = iota((T_ROWS, 254), 0)
    want = jnp.where(row < 30, row + UPPER, -1)
    for u in range(3):
        want = jnp.where(row == OWN + u, node(u), want)
        want = jnp.where(row == SIBLING + u, node(u, True), want)
        want = jnp.where(row == OWN_UPPER + u, node(u + 3), want)
    pick_matrices(ut, want, T_ROWS, 39, mats, buf)


def couplings_kernel(uc, seen, mats, buf):
    row = iota((C_ROWS, 254), 0)
    want = jnp.zeros((C_ROWS, 254), i32) - 1
    for u in range(7):
        want = jnp.where(row == u, node(u, u < 3), want)
    pick_matrices(uc, want, C_ROWS, 7, mats, buf)


def middle_kernel(
    recv_in, path_in, mats_in, coup_in, send, recv, path, mats, coup, ext, xs, gain, sems
):
    device = lax.axis_index("leaf")
    copies = fetch(sems, (recv_in, recv), (mats_in, mats), (coup_in, coup), (path_in, path))
    copies[0].wait()
    ext[...] = recv[:, 512:640].astype(f32)

    labels = jnp.concatenate(
        [jnp.transpose(ext[128 * i : 128 * i + 128, :])[64:65, :] for i in range(4)], axis=1
    )
    row, lane = iota((256, 512), 0), iota((256, 512), 1)
    wanted = ((row & 31) + 1).astype(f32)
    fits = lax.shift_right_logical(row, 5) == (lax.shift_right_logical(lane, 2) & 7)
    sums = dot(hot((labels == wanted) & fits), recv[:, 0:512])

    for g in range(16):
        rows = ext[32 * g : 32 * g + 16, :64]
        xs[8 * g : 8 * g + 8, :] = rows[:8] + rows[8:]
    first, n = 0, 16
    firsts = {3: 0}
    for copy in copies[1:]:
        copy.wait()
    for u in range(3, 6):
        for m in range(n // 2):
            r = 8 * (first + 2 * m)
            e = LEVEL_START[u] - UPPER + 2 * m
            pair = jnp.concatenate([xs[r : r + 8, :], xs[r + 8 : r + 16, :]], axis=1)
            w = own_matrix(mats, e, 2)
            t = 8 * (first + n + m)
            xs[t : t + 8, :] = dot_pair(pair, w)
        first += n
        n //= 2
        firsts[u + 1] = first
    for u in range(7):
        if u < 3:
            partner = path[8 * u : 8 * u + 8, :]
        else:
            sib = lax.bitwise_xor(lax.shift_right_logical(device, u), 1)
            partner = xs[pl.ds(pl.multiple_of((firsts[u] + sib) * 8, 8), 8), :]
        gain[8 * u : 8 * u + 8, :] = dot_pair(partner, own_matrix(coup, u))
    down = gain[48:56, :]
    for u in (5, 4, 3):
        w = own_matrix(mats, OWN_UPPER + u - 3)
        down = dot_pair(down, w, NT) + gain[8 * u : 8 * u + 8, :]
    lines = {}
    for u in (2, 1, 0):
        both = jnp.concatenate(
            [own_matrix(mats, OWN + u), own_matrix(mats, SIBLING + u)], axis=0
        )
        spread = dot_pair(down, both, NT)
        lines[u] = flat(spread[:, 64:] + gain[8 * u : 8 * u + 8, :])
        down = spread[:, :64]
    own_line = flat(down)
    z = device & 7
    last = iota((32, 512), 0) == 31
    for peer in range(8):
        x = lax.bitwise_xor(z, peer)
        line = jnp.where(x == 0, own_line, lines[0])
        line = jnp.where(x >= 2, lines[1], line)
        line = jnp.where(x >= 4, lines[2], line)
        block = jnp.where(last, line, sums[32 * peer : 32 * peer + 32])
        send[32 * peer : 32 * peer + 32, :] = block.astype(bf16)


def flat(x):
    return jnp.concatenate([x[v : v + 1] for v in range(8)], axis=1)


def final_kernel(
    recv_in, mine_in, other_in, mats_in, tr, bases, perm_in, out,
    recv, near_mine, near_other, mats, perm, cpl, dwn, dn, tree, sems,
):
    copies = fetch(
        sems,
        (recv_in, recv),
        (mats_in.at[64 * OWN : 64 * OWN + 128], mats),
        (mine_in, near_mine),
        (other_in, near_other),
        (perm_in, perm),
    )
    for copy in copies[:2]:
        copy.wait()
    device = lax.axis_index("leaf")
    core = lax.axis_index("vec")
    z = device & 7
    total = jnp.zeros((32, 512), f32)
    levels = [jnp.zeros((1, 512), f32)] * 3
    for peer in range(8):
        block = recv[32 * peer : 32 * peer + 32, :].astype(f32)
        total = total + block
        x = lax.bitwise_xor(z, peer)
        line = block[31:32]
        for i, use in enumerate((x >= 4, (x >= 2) & (x < 4), x < 2)):
            levels[i] = levels[i] + jnp.where(use, line, 0.0)
    levels = jnp.concatenate(levels + [jnp.zeros((5, 512), f32)], axis=0)
    for v in range(8):
        cpl[pl.ds(v, 32, stride=8), :] = wide(total[:, 64 * v : 64 * v + 64])
        dwn[pl.ds(v, 8, stride=8), :] = wide(levels[:, 64 * v : 64 * v + 64])
    down = dot_pair(dwn[0:8, :64], own_matrix(mats, 1), NT) + dwn[8:16, :64]
    down = dot_pair(down, own_matrix(mats, 0), NT) + dwn[16:24, :64]

    dn[240:248, :] = down + cpl[240:248, :64]
    n = 1
    while n < 16:
        off_parent = 32 - 2 * n
        n *= 2
        off = 32 - 2 * n
        for m in range(n // 2):
            r = 8 * (off_parent + m)
            w = tr[off + 2 * m : off + 2 * m + 2].reshape(128, 64)
            both = dot_pair(dn[r : r + 8, :], w, NT)
            t = 8 * (off + 2 * m)
            dn[t : t + 8, :] = both[:, :64] + cpl[t : t + 8, :64]
            dn[t + 8 : t + 16, :] = both[:, 64:] + cpl[t + 8 : t + 16, :64]
    for leaf in range(16):
        tree[:, LEAF * leaf : LEAF * leaf + LEAF] = dot(
            dn[8 * leaf : 8 * leaf + 8, :].astype(bf16), bases[leaf]
        )

    for copy in copies[2:]:
        copy.wait()

    @pl.when(core == 0)
    def _():
        tree[:, :HALF] += near_mine[...]
        tree[:, HALF:] += near_other[...]

    @pl.when(core == 1)
    def _():
        tree[:, :HALF] += near_other[...]
        tree[:, HALF:] += near_mine[...]

    width = 512
    total = jnp.zeros((256, 256), f32)
    for b in range(COLS // width):
        cols = slice(b * width, (b + 1) * width)
        index = perm[:, cols]
        select = hot_rows(index & 255, width)
        high = jnp.broadcast_to(lax.shift_right_logical(index, 8), (8, width))
        values = tree[:, cols]
        spread = jnp.concatenate(
            [jnp.where(high == q, values, 0.0) for q in range(32)], axis=0
        ).astype(bf16)
        total = total + dot(spread, select, NT)
    for q in range(32):
        out[:, 256 * q : 256 * q + 256] = total[8 * q : 8 * q + 8].astype(bf16)


def shards(
    points, vectors, leaf_order, leaf_bases, transfers, coupling_blocks,
    block_source, block_owner, block_target, up_transfer, up_coupling,
):
    peers = lax.axis_size("leaf")
    axes = ("leaf", "vec")
    vt, pt, send_c = call(
        gather_kernel,
        [((8, COLS), bf16), ((8, COLS), bf16), ((8, LOCAL), bf16)],
        [
            pltpu.VMEM((3, COLS), bf16), pltpu.VMEM((8, COLS), bf16), pltpu.VMEM((1, COLS), i32),
            pltpu.VMEM((256, 256), bf16), pltpu.VMEM((128, 256), f32), pltpu.SemaphoreType.DMA((3,)),
        ],
        (points, vectors, leaf_order), "hhh>vvv",
        2 * 384 * 256 * COLS, 1 << 20,
    )
    pairs_c = []
    pairs_a = [(0, 2 * peers - 1), (2 * peers - 1, 0)]
    for d in range(peers):
        pairs_c += [(2 * d, 2 * d + 1), (2 * d + 1, 2 * d)]
        if d + 1 < peers:
            pairs_a += [(2 * d + 1, 2 * d + 2), (2 * d + 2, 2 * d + 1)]
    rec_c = lax.ppermute(send_c, axes, pairs_c)
    ut = jnp.transpose(up_transfer, (1, 2, 0))
    uc = jnp.transpose(up_coupling, (1, 2, 0))
    (mats,) = call(
        transfers_kernel,
        [((64 * T_ROWS, 64), bf16)],
        [pltpu.VMEM((64 * T_ROWS, 128), f32)],
        (ut,), "v>v",
        2 * 4096 * 256 * 40, 3 << 20,
    )
    cf, path, halo = call(
        coeff_kernel,
        [((256, 128), f32), ((32, 64), f32), ((24, HALO), bf16)],
        [],
        (vt, pt, rec_c, leaf_bases, transfers, mats), "vvvvvv>vvv",
        2 * 512 * 512 * 256, 2 << 20,
    )
    halo = lax.ppermute(halo, axes, pairs_a)
    (send,) = call(
        product_kernel,
        [((512, 640), bf16)],
        [pltpu.VMEM((1024, 128), f32), pltpu.VMEM((640, 256), bf16)],
        (
            cf, path, jnp.transpose(coupling_blocks, (1, 2, 0)),
            block_source.reshape(1, -1), block_owner.reshape(1, -1), block_target.reshape(1, -1),
        ), "vvvvvv>v",
        2 * 512 * 256 * 640, 4 << 20,
    )
    near_groups = [[xy * 8 + z for z in range(8)] for xy in range(peers // 8)]
    far_groups = [[xy * 8 + z for xy in range(peers // 8)] for z in range(8)]
    recv = lax.all_to_all(
        send, "leaf", split_axis=0, concat_axis=0, tiled=True, axis_index_groups=far_groups
    )
    buffers = [
        pltpu.VMEM((8, COLS), bf16), pltpu.VMEM((8, COLS), bf16), pltpu.VMEM((8, LOCAL), bf16),
        pltpu.VMEM((16, 6144), bf16), pltpu.VMEM((6144, 16), bf16), pltpu.VMEM((16, 6144), bf16),
        pltpu.VMEM((8, 6144), f32), pltpu.VMEM((16, HALF), f32), pltpu.SemaphoreType.DMA((6,)),
    ]
    (coup,) = call(
        couplings_kernel,
        [((64 * C_ROWS, 64), bf16)],
        [pltpu.VMEM((64 * C_ROWS, 128), f32)],
        (uc, send), "va>v",
        2 * 4096 * 256 * 8, 3 << 20,
    )
    (begun,) = call(
        near_first_kernel,
        [((16, LEAF * (10 - SPLIT)), f32)],
        buffers + [pltpu.SemaphoreType.DMA((10 - SPLIT,))],
        (vt, pt, rec_c), "aaa>h",
        2 * 37 * 512 * 512 * 256, 1 << 20, vmem=24,
    )
    (send,) = call(
        middle_kernel,
        [((256, 512), bf16)],
        [
            pltpu.VMEM((512, 640), bf16), pltpu.VMEM((32, 64), f32),
            pltpu.VMEM((64 * T_ROWS, 64), bf16), pltpu.VMEM((64 * C_ROWS, 64), bf16),
            pltpu.VMEM((512, 128), f32), pltpu.VMEM((256, 64), f32), pltpu.VMEM((56, 64), f32),
            pltpu.SemaphoreType.DMA((4,)),
        ],
        (recv, path, mats, coup), "aaaa>v",
        2 * 256 * 512 * 512, 2 << 20,
    )
    recv = lax.all_to_all(
        send, "leaf", split_axis=0, concat_axis=0, tiled=True, axis_index_groups=near_groups
    )
    near_mine, near_send = call(
        near_rest_kernel,
        [((8, HALF), f32), ((8, HALF), f32)],
        buffers + [pltpu.VMEM((24, HALO), bf16)],
        (vt, pt, rec_c, halo, begun), "aaaah>vv",
        2 * 30 * 512 * 512 * 256, 1 << 20, vmem=24,
    )
    near_other = lax.ppermute(near_send, axes, pairs_c)
    (out,) = call(
        final_kernel,
        [((8, COLS), bf16)],
        [
            pltpu.VMEM((256, 512), bf16), pltpu.VMEM((8, HALF), f32), pltpu.VMEM((8, HALF), f32),
            pltpu.VMEM((128, 64), bf16), pltpu.VMEM((1, COLS), i32),
            pltpu.VMEM((256, 128), f32), pltpu.VMEM((64, 128), f32),
            pltpu.VMEM((248, 64), f32), pltpu.VMEM((8, COLS), f32), pltpu.SemaphoreType.DMA((5,)),
        ],
        (recv, near_mine, near_other, mats, transfers, leaf_bases, leaf_order), "aaaavvh>v",
        2 * 256 * 256 * COLS, 8 << 20,
    )
    return out


def solution(mesh):
    return jax.shard_map(
        shards,
        mesh=mesh,
        in_specs=(
            P(None, "leaf"),
            P("vec", "leaf"),
            P("leaf", None),
            P("leaf", None, None),
            P("leaf", None, None),
            P("leaf", None, None),
            P("leaf"),
            P("leaf", None),
            P("leaf"),
            P(),
            P(),
        ),
        out_specs=P("vec", "leaf"),
        check_vma=False,
    )
```

```python
import jax
import jax.numpy as jnp
import ml_dtypes
from jax import lax
from jax.experimental import pallas as pl
from jax.experimental.pallas import tpu as pltpu
from jax.sharding import PartitionSpec as P

f32 = jnp.float32
bf16 = jnp.bfloat16
i32 = jnp.int32

LEAF = 512
COLS = 8192
HALO = 1024
LOCAL = 5120
HALF = 4096
NT = (((1,), (1,)), ((), ()))
TN = (((0,), (0,)), ((), ()))
SMOOTH_HI = float(ml_dtypes.bfloat16(0.0025))
SMOOTH_LO = float(ml_dtypes.bfloat16(0.0025 - SMOOTH_HI))
VM = pl.BlockSpec(memory_space=pltpu.VMEM)


def dot(a, b, dims=(((1,), (0,)), ((), ()))):
    return lax.dot_general(a, b, dims, preferred_element_type=f32)


def iota(shape, dim):
    return lax.broadcasted_iota(i32, shape, dim)


def hot(mask):
    return jnp.where(mask, 1.0, 0.0).astype(bf16)


def hot_rows(low, width):
    rows = iota((256, width), 0).astype(bf16)
    match = rows == low.astype(bf16)
    return jnp.where(match, jnp.ones((), bf16), jnp.zeros((), bf16))


def halves(x):
    hi = x.astype(bf16)
    lo = (x - hi.astype(f32)).astype(bf16)
    return jnp.concatenate([hi, lo], axis=0)


def wide(x):
    return jnp.concatenate([x, jnp.zeros_like(x)], axis=1)


def dot_pair(x, w, dims=(((1,), (0,)), ((), ()))):
    y = dot(halves(x), w, dims)
    n = x.shape[0]
    return y[:n] + y[n:]


ANY = pl.BlockSpec(memory_space=pl.ANY)
SPEC = {"v": VM, "a": ANY, "h": pl.BlockSpec(memory_space=pltpu.HBM)}


def call(kernel, outs, scratch, args, kinds, flops, nbytes, vmem=16):
    ins, results = kinds.split(">")
    args = [
        pltpu.with_memory_space_constraint(x, pltpu.HBM) if k == "h" else x
        for x, k in zip(args, ins)
    ]
    return pl.pallas_call(
        kernel,
        out_shape=[
            pltpu.HBM(s, d) if k == "h" else jax.ShapeDtypeStruct(s, d)
            for (s, d), k in zip(outs, results)
        ],
        in_specs=[SPEC[k] for k in ins],
        out_specs=[SPEC[k] for k in results],
        scratch_shapes=scratch,
        compiler_params=pltpu.CompilerParams(vmem_limit_bytes=vmem << 20),
        cost_estimate=pl.CostEstimate(flops=flops, bytes_accessed=nbytes, transcendentals=0),
    )(*args)


def fetch(sems, *pairs):
    copies = [
        pltpu.make_async_copy(src, dst, sems.at[i]) for i, (src, dst) in enumerate(pairs)
    ]
    for copy in copies:
        copy.start()
    return copies


def gather_kernel(
    pts_in, vec_in, perm_in, vt, pt, send_c, pts, vec, perm, dv, dp, sems
):
    core = lax.axis_index("vec")
    for copy in fetch(sems, (perm_in, perm), (vec_in, vec), (pts_in, pts)):
        copy.wait()
    for m in range(16):
        a, b = 512 * m, 512 * m + 256
        dv[16 * m : 16 * m + 16, :] = jnp.concatenate(
            [vec[:, a : a + 256], vec[:, b : b + 256]], axis=0
        )
        three = pts[:, a : a + 512].astype(f32)
        four = jnp.concatenate([three, jnp.zeros((1, 512), f32)], axis=0)
        dp[8 * m : 8 * m + 8, :] = jnp.concatenate([four[:, :256], four[:, 256:]], axis=0)
    data_v = dv[...]
    data_p = dp[...].astype(bf16)
    width = 512
    for n in range(COLS // width):
        cols = slice(n * width, (n + 1) * width)
        index = perm[:, cols]
        low = index & 255
        high = jnp.broadcast_to(lax.shift_right_logical(index, 8), (8, width))
        select = hot_rows(low, width)
        got = dot(data_v, select)
        out = got[:8]
        for q in range(1, 32):
            out = jnp.where(high == q, got[8 * q : 8 * q + 8], out)
        vt[:, cols] = out.astype(bf16)
        got = dot(data_p, select)
        pair = high - iota((8, width), 0) // 4
        out = jnp.zeros((8, width), f32)
        for m in range(16):
            out = jnp.where(pair == 2 * m, got[8 * m : 8 * m + 8], out)
        out = out[:4] + out[4:]
        pt[:, cols] = jnp.concatenate([out, jnp.zeros((4, width), f32)], axis=0).astype(bf16)

    @pl.when(core == 0)
    def _():
        send_c[...] = vt[:, COLS - LOCAL :]

    @pl.when(core == 1)
    def _():
        send_c[...] = vt[:, :LOCAL]


def coeff_kernel(vt, pt, rec_c, bases, tr, mats, cf, path, halo):
    core = lax.axis_index("vec")
    ends = ((slice(0, HALO), slice(0, HALO)), (slice(COLS - HALO, COLS), slice(LOCAL - HALO, LOCAL)))
    for which, (cols, other) in enumerate(ends):

        @pl.when(core == which)
        def _():
            halo[0:8, :] = vt[:, cols]
            halo[8:16, :] = rec_c[:, other]
            halo[16:24, :] = pt[:, cols]

    cf[248:256, :] = jnp.zeros((8, 128), f32)
    for leaf in range(16):
        cf[8 * leaf : 8 * leaf + 8, :64] = dot(
            vt[:, LEAF * leaf : LEAF * leaf + LEAF], bases[leaf], NT
        )
    off, n = 0, 16
    while n > 1:
        for m in range(n // 2):
            r = 8 * (off + 2 * m)
            pair = jnp.concatenate([cf[r : r + 8, :64], cf[r + 8 : r + 16, :64]], axis=1)
            w = tr[off + 2 * m : off + 2 * m + 2].reshape(128, 64)
            t = 8 * (off + n + m)
            cf[t : t + 8, :64] = dot_pair(pair, w)
        off += n
        n //= 2
    value = cf[240:248, :64]
    for u in range(3):
        path[8 * u : 8 * u + 8, :] = value
        value = dot_pair(value, own_matrix(mats, OWN + u))
    path[24:32, :] = value


def own_matrix(mats, row, count=1):
    return mats[64 * row : 64 * (row + count), :]


def product_kernel(
    cf, path, cp, bsrc, bown, btgt, send, pick, prod
):
    source = hot(iota((32, 256), 0) == bsrc[...])
    for v in range(8):
        mine = cf[pl.ds(v, 32, stride=8), :][:, :64].astype(bf16)
        chosen = dot(mine, source, TN)
        pick[pl.ds(v, 64, stride=8), :] = chosen[:, :128]
        pick[pl.ds(512 + v, 64, stride=8), :] = chosen[:, 128:]
    for half in range(2):
        lanes = slice(128 * half, 128 * half + 128)
        for pb in range(4):
            rows = slice(16 * pb, 16 * pb + 16)

            acc = [jnp.zeros((16, 128), f32)] * 8
            for k in range(64):
                block = cp[k, rows, lanes].astype(f32)
                for v in range(8):
                    row = pick[pl.ds(512 * half + 8 * k + v, 8, stride=0), :]
                    acc[v] = acc[v] + jnp.concatenate([row, row], axis=0) * block
            for v in range(8):
                top = 64 * v + 16 * pb
                prod[top : top + 16, lanes] = acc[v].astype(bf16)
    prod[512:576, :] = jnp.zeros((64, 256), bf16)
    prod[576:640, :] = jnp.broadcast_to((btgt[...] + 1).astype(f32), (64, 256)).astype(bf16)
    owner = bown[...]
    owner_f = owner.astype(f32)
    column = jnp.transpose(jnp.broadcast_to(owner_f, (128, 256)))
    ranks = []
    for half in range(2):
        row = owner_f[:, 128 * half : 128 * half + 128]
        before = iota((256, 128), 0) < iota((256, 128), 1) + 128 * half
        same = jnp.where((column == row) & before, 1.0, 0.0)
        ranks.append(jnp.sum(same, axis=0, keepdims=True))
    place = owner * 4 + jnp.concatenate(ranks, axis=1).astype(i32)
    group = lax.shift_right_logical(place, 3) & 3
    slot_row = lax.shift_right_logical(place, 5) * 8 + (place & 7)
    payload = prod[...]
    lane_group = lax.shift_right_logical(iota((128, 128), 1) - 64, 4)
    tail = jnp.zeros((128, 128), f32)
    for g in range(4):
        slots = hot((iota((128, 256), 0) == slot_row) & (group == g))
        out = dot(slots, payload, NT)
        send[:, 512 * g : 512 * g + 512] = out[:, :512].astype(bf16)
        tail = jnp.where(lane_group == g, out[:, 512:], tail)
    tail = tail.reshape(16, 8, 128) + wide(path[24:32, :])[None]
    send[:, 2048:2176] = tail.reshape(128, 128).astype(bf16)


def split3(x):
    a = x.astype(bf16).astype(f32)
    b = (x - a).astype(bf16).astype(f32)
    return a, b, x - a - b


def leaf_cols(leaf):
    return slice(LEAF * leaf, LEAF * leaf + LEAF)


def load_window(vt, pt, rec_c, halo, leaves, vw, pw):
    core = lax.axis_index("vec")
    for which in range(2):

        @pl.when(core == which)
        def _():
            for w in leaves:
                to = leaf_cols(w)
                if w < 2:
                    near_cols = leaf_cols(w if which == 0 else 1 - w)
                    vw[0:8, to] = halo[8:16, near_cols]
                    vw[8:16, to] = halo[0:8, near_cols]
                    pw[:, to] = halo[16:24, near_cols].astype(f32)
                else:
                    local = leaf_cols(w - 2 if which == 0 else 17 - w)
                    vw[0:8, to] = vt[:, local]
                    vw[8:16, to] = rec_c[:, leaf_cols(w - 2 if which == 0 else 11 - w)]
                    pw[:, to] = pt[:, local].astype(f32)


def features(leaves, pw, fs, ft):
    for leaf in leaves:
        cols = leaf_cols(leaf)
        p = pw[0:3, cols]
        norm = p[0:1] * p[0:1] + p[1:2] * p[1:2] + p[2:3] * p[2:3]
        parts = jnp.concatenate(split3(norm), axis=0)
        one = jnp.ones((3, LEAF), f32)
        two = jnp.ones((2, LEAF), f32)
        pad = jnp.zeros((5, LEAF), f32)
        source = jnp.concatenate([p, parts, one, two, pad], axis=0)
        smooth = jnp.where(iota((2, LEAF), 0) == 0, SMOOTH_HI, SMOOTH_LO)
        target = jnp.concatenate([-2.0 * p, one, parts, smooth, pad], axis=0)
        fs[cols, :] = jnp.transpose(source).astype(bf16)
        ft[:, cols] = target.astype(bf16)


def near_target(t, vw, fs, ft, acc):
    tc = leaf_cols(t)
    total = jnp.zeros((16, LEAF), f32)
    for s in range(t - 2, t + 3):
        if 2 <= s < t:
            continue
        sc = leaf_cols(s)
        kernel = lax.rsqrt(dot(fs[sc, :], ft[:, tc])).astype(bf16)
        total = total + dot(vw[:, sc], kernel)
        if t < s < 10:
            acc[:, leaf_cols(s - 2)] += dot(vw[:, tc], kernel, NT)
    acc[:, leaf_cols(t - 2)] += total


SPLIT = 6


def near_first_kernel(
    vt_in, pt_in, c_in, begun, vt, pt, rec_c, vw, fs, ft, pw, acc, sems, out_sems
):
    for copy in fetch(sems, (vt_in, vt), (pt_in, pt), (c_in, rec_c)):
        copy.wait()
    load_window(vt, pt, rec_c, None, range(SPLIT, 12), vw, pw)
    features(range(SPLIT, 12), pw, fs, ft)
    acc[...] = jnp.zeros_like(acc)
    copies = []
    for t in range(SPLIT, 10):
        near_target(t, vw, fs, ft, acc)
        src, dst = acc.at[:, leaf_cols(t - 2)], begun.at[:, leaf_cols(t - SPLIT)]
        copies += [pltpu.make_async_copy(src, dst, out_sems.at[t - SPLIT])]
        copies[-1].start()
    for copy in copies:
        copy.wait()


def near_rest_kernel(
    vt_in, pt_in, c_in, halo_in, begun, mine, other,
    vt, pt, rec_c, vw, fs, ft, pw, acc, sems, halo,
):
    left = LEAF * (SPLIT - 2)
    copies = fetch(
        sems, (vt_in, vt), (pt_in, pt), (c_in, rec_c), (halo_in, halo),
        (begun, acc.at[:, left:]),
    )
    acc[:, :left] = jnp.zeros((16, left), f32)
    for copy in copies[:4]:
        copy.wait()
    core = lax.axis_index("vec")
    end = lax.axis_index("leaf") == (lax.axis_size("leaf") - 1) * core

    @pl.when(end)
    def _():
        halo[...] = jnp.zeros_like(halo)

    load_window(vt, pt, rec_c, halo, range(0, SPLIT + 2), vw, pw)
    features(range(0, SPLIT + 2), pw, fs, ft)
    copies[4].wait()
    for t in range(2, SPLIT):
        near_target(t, vw, fs, ft, acc)
    for which in range(2):

        @pl.when(core == which)
        def _():
            for i in range(8):
                to = leaf_cols(i if which == 0 else 7 - i)
                mine[:, to] = acc[0:8, leaf_cols(i)] * (8.0 / LEAF)
                other[:, to] = acc[8:16, leaf_cols(i)] * (8.0 / LEAF)


LEVEL_START = [256 - (256 >> u) for u in range(7)]
UPPER = 224
OWN = 30
SIBLING = 33
OWN_UPPER = 36
T_ROWS = 40
C_ROWS = 8


def node(u, other=False):
    n = lax.shift_right_logical(lax.axis_index("leaf"), u)
    return LEVEL_START[u] + (lax.bitwise_xor(n, 1) if other else n)


def pick_matrices(table, want, rows, count, mats, buf):
    pick = hot(iota((rows, 254), 1) == want)

    def step(g, carry):
        out = dot(pick, table[pl.ds(4 * g, 4)].reshape(256, 254), NT)
        for j in range(4):
            at = pl.multiple_of((4 * g + j) * rows, 8)
            buf[pl.ds(at, rows), :64] = out[:, 64 * j : 64 * j + 64]
        return carry

    lax.fori_loop(0, 16, step, 0, unroll=4)
    for m in range(count):
        mats[64 * m : 64 * m + 64, :] = buf[pl.ds(m, 64, stride=rows), :][:, :64].astype(bf16)


def transfers_kernel(ut, mats, buf):
    row = iota((T_ROWS, 254), 0)
    want = jnp.where(row < 30, row + UPPER, -1)
    for u in range(3):
        want = jnp.where(row == OWN + u, node(u), want)
        want = jnp.where(row == SIBLING + u, node(u, True), want)
        want = jnp.where(row == OWN_UPPER + u, node(u + 3), want)
    pick_matrices(ut, want, T_ROWS, 39, mats, buf)


def couplings_kernel(uc, seen, mats, buf):
    row = iota((C_ROWS, 254), 0)
    want = jnp.zeros((C_ROWS, 254), i32) - 1
    for u in range(7):
        want = jnp.where(row == u, node(u, u < 3), want)
    pick_matrices(uc, want, C_ROWS, 7, mats, buf)


def middle_kernel(
    recv_in, path_in, mats_in, coup_in, send, recv, path, mats, coup, xs, gain, sems
):
    device = lax.axis_index("leaf")
    copies = fetch(sems, (recv_in, recv), (mats_in, mats), (coup_in, coup), (path_in, path))
    copies[0].wait()
    ext = recv[:, 2048:2176].astype(f32)

    turned = jnp.transpose(ext)
    row, lane = iota((64, 128), 0), iota((64, 128), 1)
    wanted = ((row & 31) + 1).astype(f32)
    fits = lax.shift_right_logical(row, 5) == (lax.shift_right_logical(lane, 2) & 1)
    sums = []
    for g in range(4):
        label = turned[64 + 16 * g : 65 + 16 * g, :]
        picked = dot(hot((label == wanted) & fits), recv[:, 512 * g : 512 * g + 512])
        sums += [picked[:32], picked[32:]]

    xs[0:128, :] = ext[:, :64]
    first, n = 0, 16
    firsts = {3: 0}
    for copy in copies[1:]:
        copy.wait()
    for u in range(3, 6):
        for m in range(n // 2):
            r = 8 * (first + 2 * m)
            e = LEVEL_START[u] - UPPER + 2 * m
            pair = jnp.concatenate([xs[r : r + 8, :], xs[r + 8 : r + 16, :]], axis=1)
            w = own_matrix(mats, e, 2)
            t = 8 * (first + n + m)
            xs[t : t + 8, :] = dot_pair(pair, w)
        first += n
        n //= 2
        firsts[u + 1] = first
    for u in range(7):
        if u < 3:
            partner = path[8 * u : 8 * u + 8, :]
        else:
            sib = lax.bitwise_xor(lax.shift_right_logical(device, u), 1)
            partner = xs[pl.ds(pl.multiple_of((firsts[u] + sib) * 8, 8), 8), :]
        gain[8 * u : 8 * u + 8, :] = dot_pair(partner, own_matrix(coup, u))
    down = gain[48:56, :]
    for u in (5, 4, 3):
        w = own_matrix(mats, OWN_UPPER + u - 3)
        down = dot_pair(down, w, NT) + gain[8 * u : 8 * u + 8, :]
    lines = {}
    for u in (2, 1, 0):
        both = jnp.concatenate(
            [own_matrix(mats, OWN + u), own_matrix(mats, SIBLING + u)], axis=0
        )
        spread = dot_pair(down, both, NT)
        lines[u] = flat(spread[:, 64:] + gain[8 * u : 8 * u + 8, :])
        down = spread[:, :64]
    own_line = flat(down)
    z = device & 7
    last = iota((32, 512), 0) == 31
    for peer in range(8):
        x = lax.bitwise_xor(z, peer)
        line = jnp.where(x == 0, own_line, lines[0])
        line = jnp.where(x >= 2, lines[1], line)
        line = jnp.where(x >= 4, lines[2], line)
        block = jnp.where(last, line, sums[peer])
        send[32 * peer : 32 * peer + 32, :] = block.astype(bf16)


def flat(x):
    return jnp.concatenate([x[v : v + 1] for v in range(8)], axis=1)


def final_kernel(
    recv_in, mine_in, other_in, mats_in, tr, bases, perm_in, out,
    recv, near_mine, near_other, mats, perm, cpl, dwn, dn, tree, sems,
):
    copies = fetch(
        sems,
        (recv_in, recv),
        (mats_in.at[64 * OWN : 64 * OWN + 128], mats),
        (mine_in, near_mine),
        (other_in, near_other),
        (perm_in, perm),
    )
    for copy in copies[:2]:
        copy.wait()
    device = lax.axis_index("leaf")
    core = lax.axis_index("vec")
    z = device & 7
    total = jnp.zeros((32, 512), f32)
    levels = [jnp.zeros((1, 512), f32)] * 3
    for peer in range(8):
        block = recv[32 * peer : 32 * peer + 32, :].astype(f32)
        total = total + block
        x = lax.bitwise_xor(z, peer)
        line = block[31:32]
        for i, use in enumerate((x >= 4, (x >= 2) & (x < 4), x < 2)):
            levels[i] = levels[i] + jnp.where(use, line, 0.0)
    levels = jnp.concatenate(levels + [jnp.zeros((5, 512), f32)], axis=0)
    for v in range(8):
        cpl[pl.ds(v, 32, stride=8), :] = wide(total[:, 64 * v : 64 * v + 64])
        dwn[pl.ds(v, 8, stride=8), :] = wide(levels[:, 64 * v : 64 * v + 64])
    down = dot_pair(dwn[0:8, :64], own_matrix(mats, 1), NT) + dwn[8:16, :64]
    down = dot_pair(down, own_matrix(mats, 0), NT) + dwn[16:24, :64]

    dn[240:248, :] = down + cpl[240:248, :64]
    n = 1
    while n < 16:
        off_parent = 32 - 2 * n
        n *= 2
        off = 32 - 2 * n
        for m in range(n // 2):
            r = 8 * (off_parent + m)
            w = tr[off + 2 * m : off + 2 * m + 2].reshape(128, 64)
            both = dot_pair(dn[r : r + 8, :], w, NT)
            t = 8 * (off + 2 * m)
            dn[t : t + 8, :] = both[:, :64] + cpl[t : t + 8, :64]
            dn[t + 8 : t + 16, :] = both[:, 64:] + cpl[t + 8 : t + 16, :64]
    for leaf in range(16):
        tree[:, LEAF * leaf : LEAF * leaf + LEAF] = dot(
            dn[8 * leaf : 8 * leaf + 8, :].astype(bf16), bases[leaf]
        )

    for copy in copies[2:]:
        copy.wait()

    @pl.when(core == 0)
    def _():
        tree[:, :HALF] += near_mine[...]
        tree[:, HALF:] += near_other[...]

    @pl.when(core == 1)
    def _():
        tree[:, :HALF] += near_other[...]
        tree[:, HALF:] += near_mine[...]

    width = 512
    total = jnp.zeros((256, 256), f32)
    for b in range(COLS // width):
        cols = slice(b * width, (b + 1) * width)
        index = perm[:, cols]
        select = hot_rows(index & 255, width)
        high = jnp.broadcast_to(lax.shift_right_logical(index, 8), (8, width))
        values = tree[:, cols]
        spread = jnp.concatenate(
            [jnp.where(high == q, values, 0.0) for q in range(32)], axis=0
        ).astype(bf16)
        total = total + dot(spread, select, NT)
    for q in range(32):
        out[:, 256 * q : 256 * q + 256] = total[8 * q : 8 * q + 8].astype(bf16)


def shards(
    points, vectors, leaf_order, leaf_bases, transfers, coupling_blocks,
    block_source, block_owner, block_target, up_transfer, up_coupling,
):
    peers = lax.axis_size("leaf")
    axes = ("leaf", "vec")
    vt, pt, send_c = call(
        gather_kernel,
        [((8, COLS), bf16), ((8, COLS), bf16), ((8, LOCAL), bf16)],
        [
            pltpu.VMEM((3, COLS), bf16), pltpu.VMEM((8, COLS), bf16), pltpu.VMEM((1, COLS), i32),
            pltpu.VMEM((256, 256), bf16), pltpu.VMEM((128, 256), f32), pltpu.SemaphoreType.DMA((3,)),
        ],
        (points, vectors, leaf_order), "hhh>vvv",
        2 * 384 * 256 * COLS, 1 << 20,
    )
    pairs_c = []
    pairs_a = [(0, 2 * peers - 1), (2 * peers - 1, 0)]
    for d in range(peers):
        pairs_c += [(2 * d, 2 * d + 1), (2 * d + 1, 2 * d)]
        if d + 1 < peers:
            pairs_a += [(2 * d + 1, 2 * d + 2), (2 * d + 2, 2 * d + 1)]
    rec_c = lax.ppermute(send_c, axes, pairs_c)
    ut = jnp.transpose(up_transfer, (1, 2, 0))
    uc = jnp.transpose(up_coupling, (1, 2, 0))
    (mats,) = call(
        transfers_kernel,
        [((64 * T_ROWS, 64), bf16)],
        [pltpu.VMEM((64 * T_ROWS, 128), f32)],
        (ut,), "v>v",
        2 * 4096 * 256 * 40, 3 << 20,
    )
    cf, path, halo = call(
        coeff_kernel,
        [((256, 128), f32), ((32, 64), f32), ((24, HALO), bf16)],
        [],
        (vt, pt, rec_c, leaf_bases, transfers, mats), "vvvvvv>vvv",
        2 * 512 * 512 * 256, 2 << 20,
    )
    halo = lax.ppermute(halo, axes, pairs_a)
    (send,) = call(
        product_kernel,
        [((128, 2176), bf16)],
        [pltpu.VMEM((1024, 128), f32), pltpu.VMEM((640, 256), bf16)],
        (
            cf, path, jnp.transpose(coupling_blocks, (1, 2, 0)),
            block_source.reshape(1, -1), block_owner.reshape(1, -1), block_target.reshape(1, -1),
        ), "vvvvvv>v",
        2 * 512 * 256 * 640, 4 << 20,
    )
    near_groups = [[xy * 8 + z for z in range(8)] for xy in range(peers // 8)]
    far_groups = [[xy * 8 + z for xy in range(peers // 8)] for z in range(8)]
    recv = lax.all_to_all(
        send, "leaf", split_axis=0, concat_axis=0, tiled=True, axis_index_groups=far_groups
    )
    buffers = [
        pltpu.VMEM((8, COLS), bf16), pltpu.VMEM((8, COLS), bf16), pltpu.VMEM((8, LOCAL), bf16),
        pltpu.VMEM((16, 6144), bf16), pltpu.VMEM((6144, 16), bf16), pltpu.VMEM((16, 6144), bf16),
        pltpu.VMEM((8, 6144), f32), pltpu.VMEM((16, HALF), f32), pltpu.SemaphoreType.DMA((6,)),
    ]
    (coup,) = call(
        couplings_kernel,
        [((64 * C_ROWS, 64), bf16)],
        [pltpu.VMEM((64 * C_ROWS, 128), f32)],
        (uc, send), "va>v",
        2 * 4096 * 256 * 8, 3 << 20,
    )
    (begun,) = call(
        near_first_kernel,
        [((16, LEAF * (10 - SPLIT)), f32)],
        buffers + [pltpu.SemaphoreType.DMA((10 - SPLIT,))],
        (vt, pt, rec_c), "aaa>h",
        2 * 37 * 512 * 512 * 256, 1 << 20, vmem=24,
    )
    (send,) = call(
        middle_kernel,
        [((256, 512), bf16)],
        [
            pltpu.VMEM((128, 2176), bf16), pltpu.VMEM((32, 64), f32),
            pltpu.VMEM((64 * T_ROWS, 64), bf16), pltpu.VMEM((64 * C_ROWS, 64), bf16),
            pltpu.VMEM((256, 64), f32), pltpu.VMEM((56, 64), f32), pltpu.SemaphoreType.DMA((4,)),
        ],
        (recv, path, mats, coup), "aaaa>v",
        2 * 256 * 512 * 512, 2 << 20,
    )
    recv = lax.all_to_all(
        send, "leaf", split_axis=0, concat_axis=0, tiled=True, axis_index_groups=near_groups
    )
    near_mine, near_send = call(
        near_rest_kernel,
        [((8, HALF), f32), ((8, HALF), f32)],
        buffers + [pltpu.VMEM((24, HALO), bf16)],
        (vt, pt, rec_c, halo, begun), "aaaah>vv",
        2 * 30 * 512 * 512 * 256, 1 << 20, vmem=24,
    )
    near_other = lax.ppermute(near_send, axes, pairs_c)
    (out,) = call(
        final_kernel,
        [((8, COLS), bf16)],
        [
            pltpu.VMEM((256, 512), bf16), pltpu.VMEM((8, HALF), f32), pltpu.VMEM((8, HALF), f32),
            pltpu.VMEM((128, 64), bf16), pltpu.VMEM((1, COLS), i32),
            pltpu.VMEM((256, 128), f32), pltpu.VMEM((64, 128), f32),
            pltpu.VMEM((248, 64), f32), pltpu.VMEM((8, COLS), f32), pltpu.SemaphoreType.DMA((5,)),
        ],
        (recv, near_mine, near_other, mats, transfers, leaf_bases, leaf_order), "aaaavvh>v",
        2 * 256 * 256 * COLS, 8 << 20,
    )
    return out


def solution(mesh):
    return jax.shard_map(
        shards,
        mesh=mesh,
        in_specs=(
            P(None, "leaf"),
            P("vec", "leaf"),
            P("leaf", None),
            P("leaf", None, None),
            P("leaf", None, None),
            P("leaf", None, None),
            P("leaf"),
            P("leaf", None),
            P("leaf"),
            P(),
            P(),
        ),
        out_specs=P("vec", "leaf"),
        check_vma=False,
    )
```

```python
import jax
import jax.numpy as jnp
import ml_dtypes
from jax import lax
from jax.experimental import pallas as pl
from jax.experimental.pallas import tpu as pltpu
from jax.sharding import PartitionSpec as P

f32 = jnp.float32
bf16 = jnp.bfloat16
i32 = jnp.int32

LEAF = 512
COLS = 8192
HALO = 1024
LOCAL = 5120
HALF = 4096
NT = (((1,), (1,)), ((), ()))
TN = (((0,), (0,)), ((), ()))
SMOOTH_HI = float(ml_dtypes.bfloat16(0.0025))
SMOOTH_LO = float(ml_dtypes.bfloat16(0.0025 - SMOOTH_HI))
VM = pl.BlockSpec(memory_space=pltpu.VMEM)


def dot(a, b, dims=(((1,), (0,)), ((), ()))):
    return lax.dot_general(a, b, dims, preferred_element_type=f32)


def iota(shape, dim):
    return lax.broadcasted_iota(i32, shape, dim)


def hot(mask):
    return jnp.where(mask, 1.0, 0.0).astype(bf16)


def hot_rows(low, width):
    rows = iota((256, width), 0).astype(bf16)
    match = rows == low.astype(bf16)
    return jnp.where(match, jnp.ones((), bf16), jnp.zeros((), bf16))


def halves(x):
    hi = x.astype(bf16)
    lo = (x - hi.astype(f32)).astype(bf16)
    return jnp.concatenate([hi, lo], axis=0)


def wide(x):
    return jnp.concatenate([x, jnp.zeros_like(x)], axis=1)


def dot_pair(x, w, dims=(((1,), (0,)), ((), ()))):
    y = dot(halves(x), w, dims)
    n = x.shape[0]
    return y[:n] + y[n:]


ANY = pl.BlockSpec(memory_space=pl.ANY)
SPEC = {"v": VM, "a": ANY, "h": pl.BlockSpec(memory_space=pltpu.HBM)}


def call(kernel, outs, scratch, args, kinds, flops, nbytes, vmem=16):
    ins, results = kinds.split(">")
    args = [
        pltpu.with_memory_space_constraint(x, pltpu.HBM) if k == "h" else x
        for x, k in zip(args, ins)
    ]
    return pl.pallas_call(
        kernel,
        out_shape=[
            pltpu.HBM(s, d) if k == "h" else jax.ShapeDtypeStruct(s, d)
            for (s, d), k in zip(outs, results)
        ],
        in_specs=[SPEC[k] for k in ins],
        out_specs=[SPEC[k] for k in results],
        scratch_shapes=scratch,
        compiler_params=pltpu.CompilerParams(vmem_limit_bytes=vmem << 20),
        cost_estimate=pl.CostEstimate(flops=flops, bytes_accessed=nbytes, transcendentals=0),
    )(*args)


def fetch(sems, *pairs):
    copies = [
        pltpu.make_async_copy(src, dst, sems.at[i]) for i, (src, dst) in enumerate(pairs)
    ]
    for copy in copies:
        copy.start()
    return copies


def gather_kernel(
    pts_in, vec_in, perm_in, vt, pt, send_c, pts, vec, perm, dv, dp, sems
):
    core = lax.axis_index("vec")
    for copy in fetch(sems, (perm_in, perm), (vec_in, vec), (pts_in, pts)):
        copy.wait()
    for m in range(16):
        a, b = 512 * m, 512 * m + 256
        dv[16 * m : 16 * m + 16, :] = jnp.concatenate(
            [vec[:, a : a + 256], vec[:, b : b + 256]], axis=0
        )
        three = pts[:, a : a + 512].astype(f32)
        four = jnp.concatenate([three, jnp.zeros((1, 512), f32)], axis=0)
        dp[8 * m : 8 * m + 8, :] = jnp.concatenate([four[:, :256], four[:, 256:]], axis=0)
    data_v = dv[...]
    data_p = dp[...].astype(bf16)
    width = 512
    for n in range(COLS // width):
        cols = slice(n * width, (n + 1) * width)
        index = perm[:, cols]
        low = index & 255
        high = jnp.broadcast_to(lax.shift_right_logical(index, 8), (8, width))
        select = hot_rows(low, width)
        got = dot(data_v, select)
        out = got[:8]
        for q in range(1, 32):
            out = jnp.where(high == q, got[8 * q : 8 * q + 8], out)
        vt[:, cols] = out.astype(bf16)
        got = dot(data_p, select)
        pair = high - iota((8, width), 0) // 4
        out = jnp.zeros((8, width), f32)
        for m in range(16):
            out = jnp.where(pair == 2 * m, got[8 * m : 8 * m + 8], out)
        out = out[:4] + out[4:]
        pt[:, cols] = jnp.concatenate([out, jnp.zeros((4, width), f32)], axis=0).astype(bf16)

    @pl.when(core == 0)
    def _():
        send_c[...] = vt[:, COLS - LOCAL :]

    @pl.when(core == 1)
    def _():
        send_c[...] = vt[:, :LOCAL]


def coeff_kernel(vt, bases, tr, ut, bown, cf, path, mats, place, buf):
    cf[248:256, :] = jnp.zeros((8, 128), f32)
    pick = transfers_wanted()

    def pick_steps(steps):
        for g in steps:
            out = dot(pick, ut[4 * g : 4 * g + 4].reshape(256, 254), NT)
            for j in range(4):
                at = (4 * g + j) * T_ROWS
                buf[at : at + T_ROWS, :64] = out[:, 64 * j : 64 * j + 64]

    for leaf in range(16):
        cf[8 * leaf : 8 * leaf + 8, :64] = dot(
            vt[:, LEAF * leaf : LEAF * leaf + LEAF], bases[leaf], NT
        )
    pick_steps(range(0, 4))
    off, n = 0, 16
    for level in range(4):
        for m in range(n // 2):
            r = 8 * (off + 2 * m)
            pair = jnp.concatenate([cf[r : r + 8, :64], cf[r + 8 : r + 16, :64]], axis=1)
            w = tr[off + 2 * m : off + 2 * m + 2].reshape(128, 64)
            t = 8 * (off + n + m)
            cf[t : t + 8, :64] = dot_pair(pair, w)
        off += n
        n //= 2
        pick_steps(range(4 + 3 * level, 7 + 3 * level))
    for m in list(range(OWN, OWN + 3)) + list(range(OWN)) + list(range(OWN + 3, 39)):
        mats[64 * m : 64 * m + 64, :] = buf[pl.ds(m, 64, stride=T_ROWS), :][:, :64].astype(bf16)
    value = cf[240:248, :64]
    for u in range(3):
        path[8 * u : 8 * u + 8, :] = value
        value = dot_pair(value, own_matrix(mats, OWN + u))
    path[24:32, :] = value
    owner = bown[...]
    owner_f = owner.astype(f32)
    column = jnp.transpose(jnp.broadcast_to(owner_f, (128, 256)))
    ranks = []
    for half in range(2):
        row = owner_f[:, 128 * half : 128 * half + 128]
        before = iota((256, 128), 0) < iota((256, 128), 1) + 128 * half
        same = jnp.where((column == row) & before, 1.0, 0.0)
        ranks.append(jnp.sum(same, axis=0, keepdims=True))
    place[...] = owner * 4 + jnp.concatenate(ranks, axis=1).astype(i32)


def own_matrix(mats, row, count=1):
    return mats[64 * row : 64 * (row + count), :]


def product_kernel(
    cf, path, cp, bsrc, place_in, btgt, vt, pt, rec_c, send, halo, pick, prod
):
    core = lax.axis_index("vec")
    ends = ((slice(0, HALO), slice(0, HALO)), (slice(COLS - HALO, COLS), slice(LOCAL - HALO, LOCAL)))
    for which, (cols, other) in enumerate(ends):

        @pl.when(core == which)
        def _():
            halo[0:8, :] = vt[:, cols]
            halo[8:16, :] = rec_c[:, other]
            halo[16:24, :] = pt[:, cols]

    source = hot(iota((32, 256), 0) == bsrc[...])
    for v in range(8):
        mine = cf[pl.ds(v, 32, stride=8), :][:, :64].astype(bf16)
        chosen = dot(mine, source, TN)
        pick[pl.ds(v, 64, stride=8), :] = chosen[:, :128]
        pick[pl.ds(512 + v, 64, stride=8), :] = chosen[:, 128:]
    for half in range(2):
        lanes = slice(128 * half, 128 * half + 128)
        for pb in range(4):
            rows = slice(16 * pb, 16 * pb + 16)

            acc = [jnp.zeros((16, 128), f32)] * 8
            for k in range(64):
                block = cp[k, rows, lanes].astype(f32)
                for v in range(8):
                    row = pick[pl.ds(512 * half + 8 * k + v, 8, stride=0), :]
                    acc[v] = acc[v] + jnp.concatenate([row, row], axis=0) * block
            for v in range(8):
                top = 64 * v + 16 * pb
                prod[top : top + 16, lanes] = acc[v].astype(bf16)
    prod[512:576, :] = jnp.zeros((64, 256), bf16)
    prod[576:640, :] = jnp.broadcast_to((btgt[...] + 1).astype(f32), (64, 256)).astype(bf16)
    place = place_in[...]
    group = lax.shift_right_logical(place, 3) & 3
    slot_row = lax.shift_right_logical(place, 5) * 8 + (place & 7)
    payload = prod[...]
    lane_group = lax.shift_right_logical(iota((128, 128), 1) - 64, 4)
    tail = jnp.zeros((128, 128), f32)
    for g in range(4):
        slots = hot((iota((128, 256), 0) == slot_row) & (group == g))
        out = dot(slots, payload, NT)
        send[:, 512 * g : 512 * g + 512] = out[:, :512].astype(bf16)
        tail = jnp.where(lane_group == g, out[:, 512:], tail)
    tail = tail.reshape(16, 8, 128) + wide(path[24:32, :])[None]
    send[:, 2048:2176] = tail.reshape(128, 128).astype(bf16)


def split3(x):
    a = x.astype(bf16).astype(f32)
    b = (x - a).astype(bf16).astype(f32)
    return a, b, x - a - b


def leaf_cols(leaf):
    return slice(LEAF * leaf, LEAF * leaf + LEAF)


def load_window(vt, pt, rec_c, halo, leaves, vw, pw):
    core = lax.axis_index("vec")
    for which in range(2):

        @pl.when(core == which)
        def _():
            for w in leaves:
                to = leaf_cols(w)
                if w < 2:
                    near_cols = leaf_cols(w if which == 0 else 1 - w)
                    vw[0:8, to] = halo[8:16, near_cols]
                    vw[8:16, to] = halo[0:8, near_cols]
                    pw[:, to] = halo[16:24, near_cols].astype(f32)
                else:
                    local = leaf_cols(w - 2 if which == 0 else 17 - w)
                    vw[0:8, to] = vt[:, local]
                    vw[8:16, to] = rec_c[:, leaf_cols(w - 2 if which == 0 else 11 - w)]
                    pw[:, to] = pt[:, local].astype(f32)


def features(leaves, pw, fs, ft):
    for leaf in leaves:
        cols = leaf_cols(leaf)
        p = pw[0:3, cols]
        norm = p[0:1] * p[0:1] + p[1:2] * p[1:2] + p[2:3] * p[2:3]
        parts = jnp.concatenate(split3(norm), axis=0)
        one = jnp.ones((3, LEAF), f32)
        two = jnp.ones((2, LEAF), f32)
        pad = jnp.zeros((5, LEAF), f32)
        source = jnp.concatenate([p, parts, one, two, pad], axis=0)
        smooth = jnp.where(iota((2, LEAF), 0) == 0, SMOOTH_HI, SMOOTH_LO)
        target = jnp.concatenate([-2.0 * p, one, parts, smooth, pad], axis=0)
        fs[cols, :] = jnp.transpose(source).astype(bf16)
        ft[:, cols] = target.astype(bf16)


def near_target(t, vw, fs, ft, acc):
    tc = leaf_cols(t)
    total = jnp.zeros((16, LEAF), f32)
    for s in range(t - 2, t + 3):
        if 2 <= s < t:
            continue
        sc = leaf_cols(s)
        kernel = lax.rsqrt(dot(fs[sc, :], ft[:, tc])).astype(bf16)
        total = total + dot(vw[:, sc], kernel)
        if t < s < 10:
            acc[:, leaf_cols(s - 2)] += dot(vw[:, tc], kernel, NT)
    acc[:, leaf_cols(t - 2)] += total


SPLIT = 6


def near_first_kernel(
    vt_in, pt_in, c_in, begun, vt, pt, rec_c, vw, fs, ft, pw, acc, sems, out_sems
):
    for copy in fetch(sems, (vt_in, vt), (pt_in, pt), (c_in, rec_c)):
        copy.wait()
    load_window(vt, pt, rec_c, None, range(SPLIT, 12), vw, pw)
    features(range(SPLIT, 12), pw, fs, ft)
    acc[...] = jnp.zeros_like(acc)
    copies = []
    for t in range(SPLIT, 10):
        near_target(t, vw, fs, ft, acc)
        src, dst = acc.at[:, leaf_cols(t - 2)], begun.at[:, leaf_cols(t - SPLIT)]
        copies += [pltpu.make_async_copy(src, dst, out_sems.at[t - SPLIT])]
        copies[-1].start()
    for copy in copies:
        copy.wait()


def near_rest_kernel(
    vt_in, pt_in, c_in, halo_in, begun, mine, other,
    vt, pt, rec_c, vw, fs, ft, pw, acc, sems, halo,
):
    left = LEAF * (SPLIT - 2)
    copies = fetch(
        sems, (vt_in, vt), (pt_in, pt), (c_in, rec_c), (halo_in, halo),
        (begun, acc.at[:, left:]),
    )
    acc[:, :left] = jnp.zeros((16, left), f32)
    for copy in copies[:4]:
        copy.wait()
    core = lax.axis_index("vec")
    end = lax.axis_index("leaf") == (lax.axis_size("leaf") - 1) * core

    @pl.when(end)
    def _():
        halo[...] = jnp.zeros_like(halo)

    load_window(vt, pt, rec_c, halo, range(0, SPLIT + 2), vw, pw)
    features(range(0, SPLIT + 2), pw, fs, ft)
    copies[4].wait()
    for t in range(2, SPLIT):
        near_target(t, vw, fs, ft, acc)
    for which in range(2):

        @pl.when(core == which)
        def _():
            for i in range(8):
                to = leaf_cols(i if which == 0 else 7 - i)
                mine[:, to] = acc[0:8, leaf_cols(i)] * (8.0 / LEAF)
                other[:, to] = acc[8:16, leaf_cols(i)] * (8.0 / LEAF)


LEVEL_START = [256 - (256 >> u) for u in range(7)]
UPPER = 224
OWN = 30
SIBLING = 33
OWN_UPPER = 36
T_ROWS = 40
C_ROWS = 8


def node(u, other=False):
    n = lax.shift_right_logical(lax.axis_index("leaf"), u)
    return LEVEL_START[u] + (lax.bitwise_xor(n, 1) if other else n)


def pick_matrices(table, want, rows, count, mats, buf):
    pick = hot(iota((rows, 254), 1) == want)

    def step(g, carry):
        out = dot(pick, table[pl.ds(4 * g, 4)].reshape(256, 254), NT)
        for j in range(4):
            at = pl.multiple_of((4 * g + j) * rows, 8)
            buf[pl.ds(at, rows), :64] = out[:, 64 * j : 64 * j + 64]
        return carry

    lax.fori_loop(0, 16, step, 0, unroll=4)
    for m in range(count):
        mats[64 * m : 64 * m + 64, :] = buf[pl.ds(m, 64, stride=rows), :][:, :64].astype(bf16)


def transfers_wanted():
    row = iota((T_ROWS, 254), 0)
    want = jnp.where(row < 30, row + UPPER, -1)
    for u in range(3):
        want = jnp.where(row == OWN + u, node(u), want)
        want = jnp.where(row == SIBLING + u, node(u, True), want)
        want = jnp.where(row == OWN_UPPER + u, node(u + 3), want)
    return hot(iota((T_ROWS, 254), 1) == want)


def couplings_kernel(uc, seen, mats, buf):
    row = iota((C_ROWS, 254), 0)
    want = jnp.zeros((C_ROWS, 254), i32) - 1
    for u in range(7):
        want = jnp.where(row == u, node(u, u < 3), want)
    pick_matrices(uc, want, C_ROWS, 7, mats, buf)


def middle_kernel(
    recv_in, path_in, mats_in, coup_in, send, recv, path, mats, coup, xs, gain, sems
):
    device = lax.axis_index("leaf")
    copies = fetch(sems, (recv_in, recv), (mats_in, mats), (coup_in, coup), (path_in, path))
    copies[0].wait()
    ext = recv[:, 2048:2176].astype(f32)

    turned = jnp.transpose(ext)
    row, lane = iota((64, 128), 0), iota((64, 128), 1)
    wanted = ((row & 31) + 1).astype(f32)
    fits = lax.shift_right_logical(row, 5) == (lax.shift_right_logical(lane, 2) & 1)
    sums = []
    for g in range(4):
        label = turned[64 + 16 * g : 65 + 16 * g, :]
        picked = dot(hot((label == wanted) & fits), recv[:, 512 * g : 512 * g + 512])
        sums += [picked[:32], picked[32:]]

    xs[0:128, :] = ext[:, :64]
    first, n = 0, 16
    firsts = {3: 0}
    for copy in copies[1:]:
        copy.wait()
    for u in range(3, 6):
        for m in range(n // 2):
            r = 8 * (first + 2 * m)
            e = LEVEL_START[u] - UPPER + 2 * m
            pair = jnp.concatenate([xs[r : r + 8, :], xs[r + 8 : r + 16, :]], axis=1)
            w = own_matrix(mats, e, 2)
            t = 8 * (first + n + m)
            xs[t : t + 8, :] = dot_pair(pair, w)
        first += n
        n //= 2
        firsts[u + 1] = first
    for u in range(7):
        if u < 3:
            partner = path[8 * u : 8 * u + 8, :]
        else:
            sib = lax.bitwise_xor(lax.shift_right_logical(device, u), 1)
            partner = xs[pl.ds(pl.multiple_of((firsts[u] + sib) * 8, 8), 8), :]
        gain[8 * u : 8 * u + 8, :] = dot_pair(partner, own_matrix(coup, u))
    down = gain[48:56, :]
    for u in (5, 4, 3):
        w = own_matrix(mats, OWN_UPPER + u - 3)
        down = dot_pair(down, w, NT) + gain[8 * u : 8 * u + 8, :]
    lines = {}
    for u in (2, 1, 0):
        both = jnp.concatenate(
            [own_matrix(mats, OWN + u), own_matrix(mats, SIBLING + u)], axis=0
        )
        spread = dot_pair(down, both, NT)
        lines[u] = flat(spread[:, 64:] + gain[8 * u : 8 * u + 8, :])
        down = spread[:, :64]
    own_line = flat(down)
    z = device & 7
    last = iota((32, 512), 0) == 31
    for peer in range(8):
        x = lax.bitwise_xor(z, peer)
        line = jnp.where(x == 0, own_line, lines[0])
        line = jnp.where(x >= 2, lines[1], line)
        line = jnp.where(x >= 4, lines[2], line)
        block = jnp.where(last, line, sums[peer])
        send[32 * peer : 32 * peer + 32, :] = block.astype(bf16)


def flat(x):
    return jnp.concatenate([x[v : v + 1] for v in range(8)], axis=1)


def final_kernel(
    recv_in, mine_in, other_in, mats_in, tr, bases, perm_in, out,
    recv, near_mine, near_other, mats, perm, cpl, dwn, dn, tree, sems,
):
    copies = fetch(
        sems,
        (recv_in, recv),
        (mats_in.at[64 * OWN : 64 * OWN + 128], mats),
        (mine_in, near_mine),
        (other_in, near_other),
        (perm_in, perm),
    )
    for copy in copies[:2]:
        copy.wait()
    device = lax.axis_index("leaf")
    core = lax.axis_index("vec")
    z = device & 7
    total = jnp.zeros((32, 512), f32)
    levels = [jnp.zeros((1, 512), f32)] * 3
    for peer in range(8):
        block = recv[32 * peer : 32 * peer + 32, :].astype(f32)
        total = total + block
        x = lax.bitwise_xor(z, peer)
        line = block[31:32]
        for i, use in enumerate((x >= 4, (x >= 2) & (x < 4), x < 2)):
            levels[i] = levels[i] + jnp.where(use, line, 0.0)
    levels = jnp.concatenate(levels + [jnp.zeros((5, 512), f32)], axis=0)
    for v in range(8):
        cpl[pl.ds(v, 32, stride=8), :] = wide(total[:, 64 * v : 64 * v + 64])
        dwn[pl.ds(v, 8, stride=8), :] = wide(levels[:, 64 * v : 64 * v + 64])
    down = dot_pair(dwn[0:8, :64], own_matrix(mats, 1), NT) + dwn[8:16, :64]
    down = dot_pair(down, own_matrix(mats, 0), NT) + dwn[16:24, :64]

    dn[240:248, :] = down + cpl[240:248, :64]
    n = 1
    while n < 16:
        off_parent = 32 - 2 * n
        n *= 2
        off = 32 - 2 * n
        for m in range(n // 2):
            r = 8 * (off_parent + m)
            w = tr[off + 2 * m : off + 2 * m + 2].reshape(128, 64)
            both = dot_pair(dn[r : r + 8, :], w, NT)
            t = 8 * (off + 2 * m)
            dn[t : t + 8, :] = both[:, :64] + cpl[t : t + 8, :64]
            dn[t + 8 : t + 16, :] = both[:, 64:] + cpl[t + 8 : t + 16, :64]
    for leaf in range(16):
        tree[:, LEAF * leaf : LEAF * leaf + LEAF] = dot(
            dn[8 * leaf : 8 * leaf + 8, :].astype(bf16), bases[leaf]
        )

    for copy in copies[2:]:
        copy.wait()

    @pl.when(core == 0)
    def _():
        tree[:, :HALF] += near_mine[...]
        tree[:, HALF:] += near_other[...]

    @pl.when(core == 1)
    def _():
        tree[:, :HALF] += near_other[...]
        tree[:, HALF:] += near_mine[...]

    width = 512
    total = jnp.zeros((256, 256), f32)
    for b in range(COLS // width):
        cols = slice(b * width, (b + 1) * width)
        index = perm[:, cols]
        select = hot_rows(index & 255, width)
        high = jnp.broadcast_to(lax.shift_right_logical(index, 8), (8, width))
        values = tree[:, cols]
        spread = jnp.concatenate(
            [jnp.where(high == q, values, 0.0) for q in range(32)], axis=0
        ).astype(bf16)
        total = total + dot(spread, select, NT)
    for q in range(32):
        out[:, 256 * q : 256 * q + 256] = total[8 * q : 8 * q + 8].astype(bf16)


def shards(
    points, vectors, leaf_order, leaf_bases, transfers, coupling_blocks,
    block_source, block_owner, block_target, up_transfer, up_coupling,
):
    peers = lax.axis_size("leaf")
    axes = ("leaf", "vec")
    vt, pt, send_c = call(
        gather_kernel,
        [((8, COLS), bf16), ((8, COLS), bf16), ((8, LOCAL), bf16)],
        [
            pltpu.VMEM((3, COLS), bf16), pltpu.VMEM((8, COLS), bf16), pltpu.VMEM((1, COLS), i32),
            pltpu.VMEM((256, 256), bf16), pltpu.VMEM((128, 256), f32), pltpu.SemaphoreType.DMA((3,)),
        ],
        (points, vectors, leaf_order), "hhh>vvv",
        2 * 384 * 256 * COLS, 1 << 20,
    )
    pairs_c = []
    pairs_a = [(0, 2 * peers - 1), (2 * peers - 1, 0)]
    for d in range(peers):
        pairs_c += [(2 * d, 2 * d + 1), (2 * d + 1, 2 * d)]
        if d + 1 < peers:
            pairs_a += [(2 * d + 1, 2 * d + 2), (2 * d + 2, 2 * d + 1)]
    rec_c = lax.ppermute(send_c, axes, pairs_c)
    ut = jnp.transpose(up_transfer, (1, 2, 0))
    uc = jnp.transpose(up_coupling, (1, 2, 0))
    cf, path, mats, place = call(
        coeff_kernel,
        [((256, 128), f32), ((32, 64), f32), ((64 * T_ROWS, 64), bf16), ((1, 256), i32)],
        [pltpu.VMEM((64 * T_ROWS, 128), f32)],
        (vt, leaf_bases, transfers, ut, block_owner.reshape(1, -1)), "vvvvv>vvvv",
        2 * 4096 * 256 * 40, 5 << 20,
    )
    send, halo = call(
        product_kernel,
        [((128, 2176), bf16), ((24, HALO), bf16)],
        [pltpu.VMEM((1024, 128), f32), pltpu.VMEM((640, 256), bf16)],
        (
            cf, path, jnp.transpose(coupling_blocks, (1, 2, 0)),
            block_source.reshape(1, -1), place, block_target.reshape(1, -1), vt, pt, rec_c,
        ), "vvvvvvvvv>vv",
        2 * 512 * 256 * 640, 4 << 20,
    )
    halo = lax.ppermute(halo, axes, pairs_a)
    near_groups = [[xy * 8 + z for z in range(8)] for xy in range(peers // 8)]
    far_groups = [[xy * 8 + z for xy in range(peers // 8)] for z in range(8)]
    recv = lax.all_to_all(
        send, "leaf", split_axis=0, concat_axis=0, tiled=True, axis_index_groups=far_groups
    )
    buffers = [
        pltpu.VMEM((8, COLS), bf16), pltpu.VMEM((8, COLS), bf16), pltpu.VMEM((8, LOCAL), bf16),
        pltpu.VMEM((16, 6144), bf16), pltpu.VMEM((6144, 16), bf16), pltpu.VMEM((16, 6144), bf16),
        pltpu.VMEM((8, 6144), f32), pltpu.VMEM((16, HALF), f32), pltpu.SemaphoreType.DMA((6,)),
    ]
    (coup,) = call(
        couplings_kernel,
        [((64 * C_ROWS, 64), bf16)],
        [pltpu.VMEM((64 * C_ROWS, 128), f32)],
        (uc, send), "va>v",
        2 * 4096 * 256 * 8, 3 << 20,
    )
    (begun,) = call(
        near_first_kernel,
        [((16, LEAF * (10 - SPLIT)), f32)],
        buffers + [pltpu.SemaphoreType.DMA((10 - SPLIT,))],
        (vt, pt, rec_c), "aaa>h",
        2 * 37 * 512 * 512 * 256, 1 << 20, vmem=24,
    )
    (send,) = call(
        middle_kernel,
        [((256, 512), bf16)],
        [
            pltpu.VMEM((128, 2176), bf16), pltpu.VMEM((32, 64), f32),
            pltpu.VMEM((64 * T_ROWS, 64), bf16), pltpu.VMEM((64 * C_ROWS, 64), bf16),
            pltpu.VMEM((256, 64), f32), pltpu.VMEM((56, 64), f32), pltpu.SemaphoreType.DMA((4,)),
        ],
        (recv, path, mats, coup), "aaaa>v",
        2 * 256 * 512 * 512, 2 << 20,
    )
    recv = lax.all_to_all(
        send, "leaf", split_axis=0, concat_axis=0, tiled=True, axis_index_groups=near_groups
    )
    near_mine, near_send = call(
        near_rest_kernel,
        [((8, HALF), f32), ((8, HALF), f32)],
        buffers + [pltpu.VMEM((24, HALO), bf16)],
        (vt, pt, rec_c, halo, begun), "aaaah>vv",
        2 * 30 * 512 * 512 * 256, 1 << 20, vmem=24,
    )
    near_other = lax.ppermute(near_send, axes, pairs_c)
    (out,) = call(
        final_kernel,
        [((8, COLS), bf16)],
        [
            pltpu.VMEM((256, 512), bf16), pltpu.VMEM((8, HALF), f32), pltpu.VMEM((8, HALF), f32),
            pltpu.VMEM((128, 64), bf16), pltpu.VMEM((1, COLS), i32),
            pltpu.VMEM((256, 128), f32), pltpu.VMEM((64, 128), f32),
            pltpu.VMEM((248, 64), f32), pltpu.VMEM((8, COLS), f32), pltpu.SemaphoreType.DMA((5,)),
        ],
        (recv, near_mine, near_other, mats, transfers, leaf_bases, leaf_order), "aaaavvh>v",
        2 * 256 * 256 * COLS, 8 << 20,
    )
    return out


def solution(mesh):
    return jax.shard_map(
        shards,
        mesh=mesh,
        in_specs=(
            P(None, "leaf"),
            P("vec", "leaf"),
            P("leaf", None),
            P("leaf", None, None),
            P("leaf", None, None),
            P("leaf", None, None),
            P("leaf"),
            P("leaf", None),
            P("leaf"),
            P(),
            P(),
        ),
        out_specs=P("vec", "leaf"),
        check_vma=False,
    )
```

```python
import jax
import jax.numpy as jnp
import ml_dtypes
from jax import lax
from jax.experimental import pallas as pl
from jax.experimental.pallas import tpu as pltpu
from jax.sharding import PartitionSpec as P

f32 = jnp.float32
bf16 = jnp.bfloat16
i32 = jnp.int32

LEAF = 512
COLS = 8192
HALO = 1024
LOCAL = 5120
HALF = 4096
NT = (((1,), (1,)), ((), ()))
TN = (((0,), (0,)), ((), ()))
SMOOTH_HI = float(ml_dtypes.bfloat16(0.0025))
SMOOTH_LO = float(ml_dtypes.bfloat16(0.0025 - SMOOTH_HI))
VM = pl.BlockSpec(memory_space=pltpu.VMEM)


def dot(a, b, dims=(((1,), (0,)), ((), ()))):
    return lax.dot_general(a, b, dims, preferred_element_type=f32)


def iota(shape, dim):
    return lax.broadcasted_iota(i32, shape, dim)


def hot(mask):
    return jnp.where(mask, 1.0, 0.0).astype(bf16)


def hot_rows(low, width):
    rows = iota((256, width), 0).astype(bf16)
    match = rows == low.astype(bf16)
    return jnp.where(match, jnp.ones((), bf16), jnp.zeros((), bf16))


def halves(x):
    hi = x.astype(bf16)
    lo = (x - hi.astype(f32)).astype(bf16)
    return jnp.concatenate([hi, lo], axis=0)


def wide(x):
    return jnp.concatenate([x, jnp.zeros_like(x)], axis=1)


def dot_pair(x, w, dims=(((1,), (0,)), ((), ()))):
    y = dot(halves(x), w, dims)
    n = x.shape[0]
    return y[:n] + y[n:]


ANY = pl.BlockSpec(memory_space=pl.ANY)
SPEC = {"v": VM, "a": ANY, "h": pl.BlockSpec(memory_space=pltpu.HBM)}


def call(kernel, outs, scratch, args, kinds, flops, nbytes, vmem=16):
    ins, results = kinds.split(">")
    args = [
        pltpu.with_memory_space_constraint(x, pltpu.HBM) if k == "h" else x
        for x, k in zip(args, ins)
    ]
    return pl.pallas_call(
        kernel,
        out_shape=[
            pltpu.HBM(s, d) if k == "h" else jax.ShapeDtypeStruct(s, d)
            for (s, d), k in zip(outs, results)
        ],
        in_specs=[SPEC[k] for k in ins],
        out_specs=[SPEC[k] for k in results],
        scratch_shapes=scratch,
        compiler_params=pltpu.CompilerParams(vmem_limit_bytes=vmem << 20),
        cost_estimate=pl.CostEstimate(flops=flops, bytes_accessed=nbytes, transcendentals=0),
    )(*args)


def fetch(sems, *pairs):
    copies = [
        pltpu.make_async_copy(src, dst, sems.at[i]) for i, (src, dst) in enumerate(pairs)
    ]
    for copy in copies:
        copy.start()
    return copies


def gather_kernel(
    pts_in, vec_in, perm_in, vt, pt, send_c, pts, vec, perm, dv, dp, sems
):
    core = lax.axis_index("vec")
    for copy in fetch(sems, (perm_in, perm), (vec_in, vec), (pts_in, pts)):
        copy.wait()
    for m in range(16):
        a, b = 512 * m, 512 * m + 256
        dv[16 * m : 16 * m + 16, :] = jnp.concatenate(
            [vec[:, a : a + 256], vec[:, b : b + 256]], axis=0
        )
        three = pts[:, a : a + 512].astype(f32)
        four = jnp.concatenate([three, jnp.zeros((1, 512), f32)], axis=0)
        dp[8 * m : 8 * m + 8, :] = jnp.concatenate([four[:, :256], four[:, 256:]], axis=0)
    data_v = dv[...]
    data_p = dp[...].astype(bf16)
    width = 512
    for n in range(COLS // width):
        cols = slice(n * width, (n + 1) * width)
        index = perm[:, cols]
        low = index & 255
        high = jnp.broadcast_to(lax.shift_right_logical(index, 8), (8, width))
        select = hot_rows(low, width)
        got = dot(data_v, select)
        out = got[:8]
        for q in range(1, 32):
            out = jnp.where(high == q, got[8 * q : 8 * q + 8], out)
        vt[:, cols] = out.astype(bf16)
        got = dot(data_p, select)
        pair = high - iota((8, width), 0) // 4
        out = jnp.zeros((8, width), f32)
        for m in range(16):
            out = jnp.where(pair == 2 * m, got[8 * m : 8 * m + 8], out)
        out = out[:4] + out[4:]
        pt[:, cols] = jnp.concatenate([out, jnp.zeros((4, width), f32)], axis=0).astype(bf16)

    @pl.when(core == 0)
    def _():
        send_c[...] = vt[:, COLS - LOCAL :]

    @pl.when(core == 1)
    def _():
        send_c[...] = vt[:, :LOCAL]


def coeff_kernel(vt, bases, tr, ut, bown, cf, path, mats, place, buf):
    cf[248:256, :] = jnp.zeros((8, 128), f32)
    pick = transfers_wanted()

    def pick_steps(steps):
        for g in steps:
            out = dot(pick, ut[4 * g : 4 * g + 4].reshape(256, 254), NT)
            for j in range(4):
                at = (4 * g + j) * T_ROWS
                buf[at : at + T_ROWS, :64] = out[:, 64 * j : 64 * j + 64]

    for leaf in range(16):
        cf[8 * leaf : 8 * leaf + 8, :64] = dot(
            vt[:, LEAF * leaf : LEAF * leaf + LEAF], bases[leaf], NT
        )
    pick_steps(range(0, 4))
    off, n = 0, 16
    for level in range(4):
        for m in range(n // 2):
            r = 8 * (off + 2 * m)
            pair = jnp.concatenate([cf[r : r + 8, :64], cf[r + 8 : r + 16, :64]], axis=1)
            w = tr[off + 2 * m : off + 2 * m + 2].reshape(128, 64)
            t = 8 * (off + n + m)
            cf[t : t + 8, :64] = dot_pair(pair, w)
        off += n
        n //= 2
        pick_steps(range(4 + 3 * level, 7 + 3 * level))
    for m in list(range(OWN, OWN + 3)) + list(range(OWN)) + list(range(OWN + 3, 39)):
        mats[64 * m : 64 * m + 64, :] = buf[pl.ds(m, 64, stride=T_ROWS), :][:, :64].astype(bf16)
    value = cf[240:248, :64]
    for u in range(3):
        path[8 * u : 8 * u + 8, :] = value
        value = dot_pair(value, own_matrix(mats, OWN + u))
    path[24:32, :] = value
    owner = bown[...]
    owner_f = owner.astype(f32)
    column = jnp.transpose(jnp.broadcast_to(owner_f, (128, 256)))
    ranks = []
    for half in range(2):
        row = owner_f[:, 128 * half : 128 * half + 128]
        before = iota((256, 128), 0) < iota((256, 128), 1) + 128 * half
        same = jnp.where((column == row) & before, 1.0, 0.0)
        ranks.append(jnp.sum(same, axis=0, keepdims=True))
    place[...] = owner * 4 + jnp.concatenate(ranks, axis=1).astype(i32)


def own_matrix(mats, row, count=1):
    return mats[64 * row : 64 * (row + count), :]


def product_kernel(
    cf, path, cp, bsrc, place_in, btgt, vt, pt, rec_c, send, halo, pick, prod
):
    core = lax.axis_index("vec")
    ends = ((slice(0, HALO), slice(0, HALO)), (slice(COLS - HALO, COLS), slice(LOCAL - HALO, LOCAL)))
    for which, (cols, other) in enumerate(ends):

        @pl.when(core == which)
        def _():
            halo[0:8, :] = vt[:, cols]
            halo[8:16, :] = rec_c[:, other]
            halo[16:24, :] = pt[:, cols]

    source = hot(iota((32, 256), 0) == bsrc[...])
    for v in range(8):
        mine = cf[pl.ds(v, 32, stride=8), :][:, :64].astype(bf16)
        chosen = dot(mine, source, TN)
        pick[pl.ds(v, 64, stride=8), :] = chosen[:, :128]
        pick[pl.ds(512 + v, 64, stride=8), :] = chosen[:, 128:]
    for half in range(2):
        lanes = slice(128 * half, 128 * half + 128)
        for pb in range(4):
            rows = slice(16 * pb, 16 * pb + 16)

            acc = [jnp.zeros((16, 128), f32)] * 8
            for k in range(64):
                block = cp[k, rows, lanes].astype(f32)
                for v in range(8):
                    row = pick[pl.ds(512 * half + 8 * k + v, 8, stride=0), :]
                    acc[v] = acc[v] + jnp.concatenate([row, row], axis=0) * block
            for v in range(8):
                top = 64 * v + 16 * pb
                prod[top : top + 16, lanes] = acc[v].astype(bf16)
    prod[512:576, :] = jnp.zeros((64, 256), bf16)
    prod[576:640, :] = jnp.broadcast_to((btgt[...] + 1).astype(f32), (64, 256)).astype(bf16)
    place = place_in[...]
    group = lax.shift_right_logical(place, 3) & 3
    slot_row = lax.shift_right_logical(place, 5) * 8 + (place & 7)
    payload = prod[...]
    lane_group = lax.shift_right_logical(iota((128, 128), 1) - 64, 4)
    tail = jnp.zeros((128, 128), f32)
    for g in range(4):
        slots = hot((iota((128, 256), 0) == slot_row) & (group == g))
        out = dot(slots, payload, NT)
        send[:, 512 * g : 512 * g + 512] = out[:, :512].astype(bf16)
        tail = jnp.where(lane_group == g, out[:, 512:], tail)
    tail = tail.reshape(16, 8, 128) + wide(path[24:32, :])[None]
    send[:, 2048:2176] = tail.reshape(128, 128).astype(bf16)


def split3(x):
    a = x.astype(bf16).astype(f32)
    b = (x - a).astype(bf16).astype(f32)
    return a, b, x - a - b


def leaf_cols(leaf):
    return slice(LEAF * leaf, LEAF * leaf + LEAF)


def load_window(vt, pt, rec_c, halo, leaves, vw, pw):
    core = lax.axis_index("vec")
    for which in range(2):

        @pl.when(core == which)
        def _():
            for w in leaves:
                to = leaf_cols(w)
                if w < 2:
                    near_cols = leaf_cols(w if which == 0 else 1 - w)
                    vw[0:8, to] = halo[8:16, near_cols]
                    vw[8:16, to] = halo[0:8, near_cols]
                    pw[:, to] = halo[16:24, near_cols].astype(f32)
                else:
                    local = leaf_cols(w - 2 if which == 0 else 17 - w)
                    vw[0:8, to] = vt[:, local]
                    vw[8:16, to] = rec_c[:, leaf_cols(w - 2 if which == 0 else 11 - w)]
                    pw[:, to] = pt[:, local].astype(f32)


def features(leaves, pw, fs, ft):
    for leaf in leaves:
        cols = leaf_cols(leaf)
        p = pw[0:3, cols]
        norm = p[0:1] * p[0:1] + p[1:2] * p[1:2] + p[2:3] * p[2:3]
        parts = jnp.concatenate(split3(norm), axis=0)
        one = jnp.ones((3, LEAF), f32)
        two = jnp.ones((2, LEAF), f32)
        pad = jnp.zeros((5, LEAF), f32)
        source = jnp.concatenate([p, parts, one, two, pad], axis=0)
        smooth = jnp.where(iota((2, LEAF), 0) == 0, SMOOTH_HI, SMOOTH_LO)
        target = jnp.concatenate([-2.0 * p, one, parts, smooth, pad], axis=0)
        fs[cols, :] = jnp.transpose(source).astype(bf16)
        ft[:, cols] = target.astype(bf16)


def near_target(t, vw, fs, ft, acc):
    tc = leaf_cols(t)
    total = jnp.zeros((16, LEAF), f32)
    for s in range(t - 2, t + 3):
        if 2 <= s < t:
            continue
        sc = leaf_cols(s)
        kernel = lax.rsqrt(dot(fs[sc, :], ft[:, tc])).astype(bf16)
        total = total + dot(vw[:, sc], kernel)
        if t < s < 10:
            acc[:, leaf_cols(s - 2)] += dot(vw[:, tc], kernel, NT)
    acc[:, leaf_cols(t - 2)] += total


SPLIT = 6


def near_first_kernel(
    vt_in, pt_in, c_in, uc_in, begun, coup,
    vt, pt, rec_c, vw, fs, ft, pw, acc, sems, out_sems, buf, uc,
):
    pick = couplings_wanted()

    def pick_steps(steps):
        for g in steps:
            out = dot(pick, uc[4 * g : 4 * g + 4].reshape(256, 254), NT)
            for j in range(4):
                at = (4 * g + j) * C_ROWS
                buf[at : at + C_ROWS, :64] = out[:, 64 * j : 64 * j + 64]

    loads = fetch(sems, (vt_in, vt), (pt_in, pt), (c_in, rec_c), (uc_in, uc))
    for copy in loads[:3]:
        copy.wait()
    load_window(vt, pt, rec_c, None, range(SPLIT, 12), vw, pw)
    features(range(SPLIT, 12), pw, fs, ft)
    acc[...] = jnp.zeros_like(acc)
    loads[3].wait()
    copies = []
    for t in range(SPLIT, 10):
        pick_steps(range(4 * (t - SPLIT), 4 * (t - SPLIT) + 4))
        near_target(t, vw, fs, ft, acc)
        src, dst = acc.at[:, leaf_cols(t - 2)], begun.at[:, leaf_cols(t - SPLIT)]
        copies += [pltpu.make_async_copy(src, dst, out_sems.at[t - SPLIT])]
        copies[-1].start()
    for m in range(7):
        coup[64 * m : 64 * m + 64, :] = buf[pl.ds(m, 64, stride=C_ROWS), :][:, :64].astype(bf16)
    for copy in copies:
        copy.wait()


def near_rest_kernel(
    vt_in, pt_in, c_in, halo_in, begun, mine, other,
    vt, pt, rec_c, vw, fs, ft, pw, acc, sems, halo,
):
    left = LEAF * (SPLIT - 2)
    copies = fetch(
        sems, (vt_in, vt), (pt_in, pt), (c_in, rec_c), (halo_in, halo),
        (begun, acc.at[:, left:]),
    )
    acc[:, :left] = jnp.zeros((16, left), f32)
    for copy in copies[:4]:
        copy.wait()
    core = lax.axis_index("vec")
    end = lax.axis_index("leaf") == (lax.axis_size("leaf") - 1) * core

    @pl.when(end)
    def _():
        halo[...] = jnp.zeros_like(halo)

    load_window(vt, pt, rec_c, halo, range(0, SPLIT + 2), vw, pw)
    features(range(0, SPLIT + 2), pw, fs, ft)
    copies[4].wait()
    for t in range(2, SPLIT):
        near_target(t, vw, fs, ft, acc)
    for which in range(2):

        @pl.when(core == which)
        def _():
            for i in range(8):
                to = leaf_cols(i if which == 0 else 7 - i)
                mine[:, to] = acc[0:8, leaf_cols(i)] * (8.0 / LEAF)
                other[:, to] = acc[8:16, leaf_cols(i)] * (8.0 / LEAF)


LEVEL_START = [256 - (256 >> u) for u in range(7)]
UPPER = 224
OWN = 30
SIBLING = 33
OWN_UPPER = 36
T_ROWS = 40
C_ROWS = 8


def node(u, other=False):
    n = lax.shift_right_logical(lax.axis_index("leaf"), u)
    return LEVEL_START[u] + (lax.bitwise_xor(n, 1) if other else n)


def transfers_wanted():
    row = iota((T_ROWS, 254), 0)
    want = jnp.where(row < 30, row + UPPER, -1)
    for u in range(3):
        want = jnp.where(row == OWN + u, node(u), want)
        want = jnp.where(row == SIBLING + u, node(u, True), want)
        want = jnp.where(row == OWN_UPPER + u, node(u + 3), want)
    return hot(iota((T_ROWS, 254), 1) == want)


def couplings_wanted():
    row = iota((C_ROWS, 254), 0)
    want = jnp.zeros((C_ROWS, 254), i32) - 1
    for u in range(7):
        want = jnp.where(row == u, node(u, u < 3), want)
    return hot(iota((C_ROWS, 254), 1) == want)


def middle_kernel(
    recv_in, path_in, mats_in, coup_in, send, recv, path, mats, coup, xs, gain, sems
):
    device = lax.axis_index("leaf")
    copies = fetch(sems, (recv_in, recv), (mats_in, mats), (coup_in, coup), (path_in, path))
    copies[0].wait()
    ext = recv[:, 2048:2176].astype(f32)

    turned = jnp.transpose(ext)
    row, lane = iota((64, 128), 0), iota((64, 128), 1)
    wanted = ((row & 31) + 1).astype(f32)
    fits = lax.shift_right_logical(row, 5) == (lax.shift_right_logical(lane, 2) & 1)
    sums = []
    for g in range(4):
        label = turned[64 + 16 * g : 65 + 16 * g, :]
        picked = dot(hot((label == wanted) & fits), recv[:, 512 * g : 512 * g + 512])
        sums += [picked[:32], picked[32:]]

    xs[0:128, :] = ext[:, :64]
    first, n = 0, 16
    firsts = {3: 0}
    for copy in copies[1:]:
        copy.wait()
    for u in range(3, 6):
        for m in range(n // 2):
            r = 8 * (first + 2 * m)
            e = LEVEL_START[u] - UPPER + 2 * m
            pair = jnp.concatenate([xs[r : r + 8, :], xs[r + 8 : r + 16, :]], axis=1)
            w = own_matrix(mats, e, 2)
            t = 8 * (first + n + m)
            xs[t : t + 8, :] = dot_pair(pair, w)
        first += n
        n //= 2
        firsts[u + 1] = first
    for u in range(7):
        if u < 3:
            partner = path[8 * u : 8 * u + 8, :]
        else:
            sib = lax.bitwise_xor(lax.shift_right_logical(device, u), 1)
            partner = xs[pl.ds(pl.multiple_of((firsts[u] + sib) * 8, 8), 8), :]
        gain[8 * u : 8 * u + 8, :] = dot_pair(partner, own_matrix(coup, u))
    down = gain[48:56, :]
    for u in (5, 4, 3):
        w = own_matrix(mats, OWN_UPPER + u - 3)
        down = dot_pair(down, w, NT) + gain[8 * u : 8 * u + 8, :]
    lines = {}
    for u in (2, 1, 0):
        both = jnp.concatenate(
            [own_matrix(mats, OWN + u), own_matrix(mats, SIBLING + u)], axis=0
        )
        spread = dot_pair(down, both, NT)
        lines[u] = flat(spread[:, 64:] + gain[8 * u : 8 * u + 8, :])
        down = spread[:, :64]
    own_line = flat(down)
    z = device & 7
    last = iota((32, 512), 0) == 31
    for peer in range(8):
        x = lax.bitwise_xor(z, peer)
        line = jnp.where(x == 0, own_line, lines[0])
        line = jnp.where(x >= 2, lines[1], line)
        line = jnp.where(x >= 4, lines[2], line)
        block = jnp.where(last, line, sums[peer])
        send[32 * peer : 32 * peer + 32, :] = block.astype(bf16)


def flat(x):
    return jnp.concatenate([x[v : v + 1] for v in range(8)], axis=1)


def final_kernel(
    recv_in, mine_in, other_in, mats_in, tr, bases, perm_in, out,
    recv, near_mine, near_other, mats, perm, cpl, dwn, dn, tree, sems,
):
    copies = fetch(
        sems,
        (recv_in, recv),
        (mats_in.at[64 * OWN : 64 * OWN + 128], mats),
        (mine_in, near_mine),
        (other_in, near_other),
        (perm_in, perm),
    )
    for copy in copies[:2]:
        copy.wait()
    device = lax.axis_index("leaf")
    core = lax.axis_index("vec")
    z = device & 7
    total = jnp.zeros((32, 512), f32)
    levels = [jnp.zeros((1, 512), f32)] * 3
    for peer in range(8):
        block = recv[32 * peer : 32 * peer + 32, :].astype(f32)
        total = total + block
        x = lax.bitwise_xor(z, peer)
        line = block[31:32]
        for i, use in enumerate((x >= 4, (x >= 2) & (x < 4), x < 2)):
            levels[i] = levels[i] + jnp.where(use, line, 0.0)
    levels = jnp.concatenate(levels + [jnp.zeros((5, 512), f32)], axis=0)
    for v in range(8):
        cpl[pl.ds(v, 32, stride=8), :] = wide(total[:, 64 * v : 64 * v + 64])
        dwn[pl.ds(v, 8, stride=8), :] = wide(levels[:, 64 * v : 64 * v + 64])
    down = dot_pair(dwn[0:8, :64], own_matrix(mats, 1), NT) + dwn[8:16, :64]
    down = dot_pair(down, own_matrix(mats, 0), NT) + dwn[16:24, :64]

    dn[240:248, :] = down + cpl[240:248, :64]
    n = 1
    while n < 16:
        off_parent = 32 - 2 * n
        n *= 2
        off = 32 - 2 * n
        for m in range(n // 2):
            r = 8 * (off_parent + m)
            w = tr[off + 2 * m : off + 2 * m + 2].reshape(128, 64)
            both = dot_pair(dn[r : r + 8, :], w, NT)
            t = 8 * (off + 2 * m)
            dn[t : t + 8, :] = both[:, :64] + cpl[t : t + 8, :64]
            dn[t + 8 : t + 16, :] = both[:, 64:] + cpl[t + 8 : t + 16, :64]
    for leaf in range(16):
        tree[:, LEAF * leaf : LEAF * leaf + LEAF] = dot(
            dn[8 * leaf : 8 * leaf + 8, :].astype(bf16), bases[leaf]
        )

    for copy in copies[2:]:
        copy.wait()

    @pl.when(core == 0)
    def _():
        tree[:, :HALF] += near_mine[...]
        tree[:, HALF:] += near_other[...]

    @pl.when(core == 1)
    def _():
        tree[:, :HALF] += near_other[...]
        tree[:, HALF:] += near_mine[...]

    width = 512
    total = jnp.zeros((256, 256), f32)
    for b in range(COLS // width):
        cols = slice(b * width, (b + 1) * width)
        index = perm[:, cols]
        select = hot_rows(index & 255, width)
        high = jnp.broadcast_to(lax.shift_right_logical(index, 8), (8, width))
        values = tree[:, cols]
        spread = jnp.concatenate(
            [jnp.where(high == q, values, 0.0) for q in range(32)], axis=0
        ).astype(bf16)
        total = total + dot(spread, select, NT)
    for q in range(32):
        out[:, 256 * q : 256 * q + 256] = total[8 * q : 8 * q + 8].astype(bf16)


def shards(
    points, vectors, leaf_order, leaf_bases, transfers, coupling_blocks,
    block_source, block_owner, block_target, up_transfer, up_coupling,
):
    peers = lax.axis_size("leaf")
    axes = ("leaf", "vec")
    vt, pt, send_c = call(
        gather_kernel,
        [((8, COLS), bf16), ((8, COLS), bf16), ((8, LOCAL), bf16)],
        [
            pltpu.VMEM((3, COLS), bf16), pltpu.VMEM((8, COLS), bf16), pltpu.VMEM((1, COLS), i32),
            pltpu.VMEM((256, 256), bf16), pltpu.VMEM((128, 256), f32), pltpu.SemaphoreType.DMA((3,)),
        ],
        (points, vectors, leaf_order), "hhh>vvv",
        2 * 384 * 256 * COLS, 1 << 20,
    )
    pairs_c = []
    pairs_a = [(0, 2 * peers - 1), (2 * peers - 1, 0)]
    for d in range(peers):
        pairs_c += [(2 * d, 2 * d + 1), (2 * d + 1, 2 * d)]
        if d + 1 < peers:
            pairs_a += [(2 * d + 1, 2 * d + 2), (2 * d + 2, 2 * d + 1)]
    rec_c = lax.ppermute(send_c, axes, pairs_c)
    ut = jnp.transpose(up_transfer, (1, 2, 0))
    uc = jnp.transpose(up_coupling, (1, 2, 0))
    cf, path, mats, place = call(
        coeff_kernel,
        [((256, 128), f32), ((32, 64), f32), ((64 * T_ROWS, 64), bf16), ((1, 256), i32)],
        [pltpu.VMEM((64 * T_ROWS, 128), f32)],
        (vt, leaf_bases, transfers, ut, block_owner.reshape(1, -1)), "vvvvv>vvvv",
        2 * 4096 * 256 * 40, 5 << 20,
    )
    send, halo = call(
        product_kernel,
        [((128, 2176), bf16), ((24, HALO), bf16)],
        [pltpu.VMEM((1024, 128), f32), pltpu.VMEM((640, 256), bf16)],
        (
            cf, path, jnp.transpose(coupling_blocks, (1, 2, 0)),
            block_source.reshape(1, -1), place, block_target.reshape(1, -1), vt, pt, rec_c,
        ), "vvvvvvvvv>vv",
        2 * 512 * 256 * 640, 4 << 20,
    )
    halo = lax.ppermute(halo, axes, pairs_a)
    near_groups = [[xy * 8 + z for z in range(8)] for xy in range(peers // 8)]
    far_groups = [[xy * 8 + z for xy in range(peers // 8)] for z in range(8)]
    recv = lax.all_to_all(
        send, "leaf", split_axis=0, concat_axis=0, tiled=True, axis_index_groups=far_groups
    )
    buffers = [
        pltpu.VMEM((8, COLS), bf16), pltpu.VMEM((8, COLS), bf16), pltpu.VMEM((8, LOCAL), bf16),
        pltpu.VMEM((16, 6144), bf16), pltpu.VMEM((6144, 16), bf16), pltpu.VMEM((16, 6144), bf16),
        pltpu.VMEM((8, 6144), f32), pltpu.VMEM((16, HALF), f32), pltpu.SemaphoreType.DMA((6,)),
    ]
    begun, coup = call(
        near_first_kernel,
        [((16, LEAF * (10 - SPLIT)), f32), ((64 * C_ROWS, 64), bf16)],
        buffers
        + [
            pltpu.SemaphoreType.DMA((10 - SPLIT,)), pltpu.VMEM((64 * C_ROWS, 128), f32),
            pltpu.VMEM((64, 64, 254), bf16),
        ],
        (vt, pt, rec_c, uc), "aaah>hv",
        2 * 33 * 512 * 512 * 256, 3 << 20, vmem=24,
    )
    (send,) = call(
        middle_kernel,
        [((256, 512), bf16)],
        [
            pltpu.VMEM((128, 2176), bf16), pltpu.VMEM((32, 64), f32),
            pltpu.VMEM((64 * T_ROWS, 64), bf16), pltpu.VMEM((64 * C_ROWS, 64), bf16),
            pltpu.VMEM((256, 64), f32), pltpu.VMEM((56, 64), f32), pltpu.SemaphoreType.DMA((4,)),
        ],
        (recv, path, mats, coup), "aaaa>v",
        2 * 256 * 512 * 512, 2 << 20,
    )
    recv = lax.all_to_all(
        send, "leaf", split_axis=0, concat_axis=0, tiled=True, axis_index_groups=near_groups
    )
    near_mine, near_send = call(
        near_rest_kernel,
        [((8, HALF), f32), ((8, HALF), f32)],
        buffers + [pltpu.VMEM((24, HALO), bf16)],
        (vt, pt, rec_c, halo, begun), "aaaah>vv",
        2 * 30 * 512 * 512 * 256, 1 << 20, vmem=24,
    )
    near_other = lax.ppermute(near_send, axes, pairs_c)
    (out,) = call(
        final_kernel,
        [((8, COLS), bf16)],
        [
            pltpu.VMEM((256, 512), bf16), pltpu.VMEM((8, HALF), f32), pltpu.VMEM((8, HALF), f32),
            pltpu.VMEM((128, 64), bf16), pltpu.VMEM((1, COLS), i32),
            pltpu.VMEM((256, 128), f32), pltpu.VMEM((64, 128), f32),
            pltpu.VMEM((248, 64), f32), pltpu.VMEM((8, COLS), f32), pltpu.SemaphoreType.DMA((5,)),
        ],
        (recv, near_mine, near_other, mats, transfers, leaf_bases, leaf_order), "aaaavvh>v",
        2 * 256 * 256 * COLS, 8 << 20,
    )
    return out


def solution(mesh):
    return jax.shard_map(
        shards,
        mesh=mesh,
        in_specs=(
            P(None, "leaf"),
            P("vec", "leaf"),
            P("leaf", None),
            P("leaf", None, None),
            P("leaf", None, None),
            P("leaf", None, None),
            P("leaf"),
            P("leaf", None),
            P("leaf"),
            P(),
            P(),
        ),
        out_specs=P("vec", "leaf"),
        check_vma=False,
    )
```

```python
import jax
import jax.numpy as jnp
import ml_dtypes
from jax import lax
from jax.experimental import pallas as pl
from jax.experimental.pallas import tpu as pltpu
from jax.sharding import PartitionSpec as P

f32 = jnp.float32
bf16 = jnp.bfloat16
i32 = jnp.int32

LEAF = 512
COLS = 8192
HALO = 1024
LOCAL = 5120
HALF = 4096
NT = (((1,), (1,)), ((), ()))
TN = (((0,), (0,)), ((), ()))
SMOOTH_HI = float(ml_dtypes.bfloat16(0.0025))
SMOOTH_LO = float(ml_dtypes.bfloat16(0.0025 - SMOOTH_HI))
VM = pl.BlockSpec(memory_space=pltpu.VMEM)


def dot(a, b, dims=(((1,), (0,)), ((), ()))):
    return lax.dot_general(a, b, dims, preferred_element_type=f32)


def iota(shape, dim):
    return lax.broadcasted_iota(i32, shape, dim)


def hot(mask):
    return jnp.where(mask, 1.0, 0.0).astype(bf16)


def hot_rows(low, width):
    rows = iota((256, width), 0).astype(bf16)
    match = rows == low.astype(bf16)
    return jnp.where(match, jnp.ones((), bf16), jnp.zeros((), bf16))


def halves(x):
    hi = x.astype(bf16)
    lo = (x - hi.astype(f32)).astype(bf16)
    return jnp.concatenate([hi, lo], axis=0)


def wide(x):
    return jnp.concatenate([x, jnp.zeros_like(x)], axis=1)


def dot_pair(x, w, dims=(((1,), (0,)), ((), ()))):
    y = dot(halves(x), w, dims)
    n = x.shape[0]
    return y[:n] + y[n:]


ANY = pl.BlockSpec(memory_space=pl.ANY)
SPEC = {"v": VM, "a": ANY, "h": pl.BlockSpec(memory_space=pltpu.HBM)}


def call(kernel, outs, scratch, args, kinds, flops, nbytes, vmem=16):
    ins, results = kinds.split(">")
    args = [
        pltpu.with_memory_space_constraint(x, pltpu.HBM) if k == "h" else x
        for x, k in zip(args, ins)
    ]
    return pl.pallas_call(
        kernel,
        out_shape=[
            pltpu.HBM(s, d) if k == "h" else jax.ShapeDtypeStruct(s, d)
            for (s, d), k in zip(outs, results)
        ],
        in_specs=[SPEC[k] for k in ins],
        out_specs=[SPEC[k] for k in results],
        scratch_shapes=scratch,
        compiler_params=pltpu.CompilerParams(vmem_limit_bytes=vmem << 20),
        cost_estimate=pl.CostEstimate(flops=flops, bytes_accessed=nbytes, transcendentals=0),
    )(*args)


def fetch(sems, *pairs):
    copies = [
        pltpu.make_async_copy(src, dst, sems.at[i]) for i, (src, dst) in enumerate(pairs)
    ]
    for copy in copies:
        copy.start()
    return copies


def gather_kernel(
    pts_in, vec_in, perm_in, vt, pt, send_c, pts, vec, perm, dv, dp, sems
):
    core = lax.axis_index("vec")
    for copy in fetch(sems, (perm_in, perm), (vec_in, vec), (pts_in, pts)):
        copy.wait()
    for m in range(16):
        a, b = 512 * m, 512 * m + 256
        dv[16 * m : 16 * m + 16, :] = jnp.concatenate(
            [vec[:, a : a + 256], vec[:, b : b + 256]], axis=0
        )
        three = pts[:, a : a + 512].astype(f32)
        four = jnp.concatenate([three, jnp.zeros((1, 512), f32)], axis=0)
        dp[8 * m : 8 * m + 8, :] = jnp.concatenate([four[:, :256], four[:, 256:]], axis=0)
    data_v = dv[...]
    data_p = dp[...].astype(bf16)
    width = 512
    for n in range(COLS // width):
        cols = slice(n * width, (n + 1) * width)
        index = perm[:, cols]
        low = index & 255
        high = jnp.broadcast_to(lax.shift_right_logical(index, 8), (8, width))
        select = hot_rows(low, width)
        got = dot(data_v, select)
        out = got[:8]
        for q in range(1, 32):
            out = jnp.where(high == q, got[8 * q : 8 * q + 8], out)
        vt[:, cols] = out.astype(bf16)
        got = dot(data_p, select)
        pair = high - iota((8, width), 0) // 4
        out = jnp.zeros((8, width), f32)
        for m in range(16):
            out = jnp.where(pair == 2 * m, got[8 * m : 8 * m + 8], out)
        out = out[:4] + out[4:]
        pt[:, cols] = jnp.concatenate([out, jnp.zeros((4, width), f32)], axis=0).astype(bf16)

    @pl.when(core == 0)
    def _():
        send_c[...] = vt[:, COLS - LOCAL :]

    @pl.when(core == 1)
    def _():
        send_c[...] = vt[:, :LOCAL]


def coeff_kernel(vt, bases, tr, ut, bown, cf, path, mats, place, buf):
    cf[248:256, :] = jnp.zeros((8, 128), f32)
    pick = transfers_wanted()

    def pick_steps(steps):
        for g in steps:
            out = dot(pick, ut[4 * g : 4 * g + 4].reshape(256, 254), NT)
            for j in range(4):
                at = (4 * g + j) * T_ROWS
                buf[at : at + T_ROWS, :64] = out[:, 64 * j : 64 * j + 64]

    for leaf in range(16):
        cf[8 * leaf : 8 * leaf + 8, :64] = dot(
            vt[:, LEAF * leaf : LEAF * leaf + LEAF], bases[leaf], NT
        )
    pick_steps(range(0, 4))
    off, n = 0, 16
    for level in range(4):
        for m in range(n // 2):
            r = 8 * (off + 2 * m)
            pair = jnp.concatenate([cf[r : r + 8, :64], cf[r + 8 : r + 16, :64]], axis=1)
            w = tr[off + 2 * m : off + 2 * m + 2].reshape(128, 64)
            t = 8 * (off + n + m)
            cf[t : t + 8, :64] = dot_pair(pair, w)
        off += n
        n //= 2
        pick_steps(range(4 + 3 * level, 7 + 3 * level))
    for m in list(range(OWN, OWN + 3)) + list(range(OWN)) + list(range(OWN + 3, 39)):
        mats[64 * m : 64 * m + 64, :] = buf[pl.ds(m, 64, stride=T_ROWS), :][:, :64].astype(bf16)
    value = cf[240:248, :64]
    for u in range(3):
        path[8 * u : 8 * u + 8, :] = value
        value = dot_pair(value, own_matrix(mats, OWN + u))
    path[24:32, :] = value
    owner = bown[...]
    owner_f = owner.astype(f32)
    column = jnp.transpose(jnp.broadcast_to(owner_f, (128, 256)))
    ranks = []
    for half in range(2):
        row = owner_f[:, 128 * half : 128 * half + 128]
        before = iota((256, 128), 0) < iota((256, 128), 1) + 128 * half
        same = jnp.where((column == row) & before, 1.0, 0.0)
        ranks.append(jnp.sum(same, axis=0, keepdims=True))
    place[...] = owner * 4 + jnp.concatenate(ranks, axis=1).astype(i32)


def own_matrix(mats, row, count=1):
    return mats[64 * row : 64 * (row + count), :]


def product_kernel(
    cf, path, cp, bsrc, place_in, btgt, vt, pt, rec_c, send, halo, pick, prod
):
    core = lax.axis_index("vec")
    ends = ((slice(0, HALO), slice(0, HALO)), (slice(COLS - HALO, COLS), slice(LOCAL - HALO, LOCAL)))
    for which, (cols, other) in enumerate(ends):

        @pl.when(core == which)
        def _():
            halo[0:8, :] = vt[:, cols]
            halo[8:16, :] = rec_c[:, other]
            halo[16:24, :] = pt[:, cols]

    source = hot(iota((32, 256), 0) == bsrc[...])
    for v in range(8):
        mine = cf[pl.ds(v, 32, stride=8), :][:, :64].astype(bf16)
        chosen = dot(mine, source, TN)
        pick[pl.ds(v, 64, stride=8), :] = chosen[:, :128]
        pick[pl.ds(512 + v, 64, stride=8), :] = chosen[:, 128:]
    for half in range(2):
        lanes = slice(128 * half, 128 * half + 128)
        for pb in range(4):
            rows = slice(16 * pb, 16 * pb + 16)

            acc = [jnp.zeros((16, 128), f32)] * 8
            for k in range(64):
                block = cp[k, rows, lanes].astype(f32)
                for v in range(8):
                    row = pick[pl.ds(512 * half + 8 * k + v, 8, stride=0), :]
                    acc[v] = acc[v] + jnp.concatenate([row, row], axis=0) * block
            for v in range(8):
                top = 64 * v + 16 * pb
                prod[top : top + 16, lanes] = acc[v].astype(bf16)
    prod[512:576, :] = jnp.zeros((64, 256), bf16)
    prod[576:640, :] = jnp.broadcast_to((btgt[...] + 1).astype(f32), (64, 256)).astype(bf16)
    place = place_in[...]
    group = lax.shift_right_logical(place, 3) & 3
    slot_row = lax.shift_right_logical(place, 5) * 8 + (place & 7)
    payload = prod[...]
    lane_group = lax.shift_right_logical(iota((128, 128), 1) - 64, 4)
    tail = jnp.zeros((128, 128), f32)
    for g in range(4):
        slots = hot((iota((128, 256), 0) == slot_row) & (group == g))
        out = dot(slots, payload, NT)
        send[:, 512 * g : 512 * g + 512] = out[:, :512].astype(bf16)
        tail = jnp.where(lane_group == g, out[:, 512:], tail)
    tail = tail.reshape(16, 8, 128) + wide(path[24:32, :])[None]
    send[:, 2048:2176] = tail.reshape(128, 128).astype(bf16)


def split3(x):
    a = x.astype(bf16).astype(f32)
    b = (x - a).astype(bf16).astype(f32)
    return a, b, x - a - b


def leaf_cols(leaf):
    return slice(LEAF * leaf, LEAF * leaf + LEAF)


def load_window(vt, pt, rec_c, halo, leaves, vw, pw):
    core = lax.axis_index("vec")
    for which in range(2):

        @pl.when(core == which)
        def _():
            for w in leaves:
                to = leaf_cols(w)
                if w < 2:
                    near_cols = leaf_cols(w if which == 0 else 1 - w)
                    vw[0:8, to] = halo[8:16, near_cols]
                    vw[8:16, to] = halo[0:8, near_cols]
                    pw[:, to] = halo[16:24, near_cols].astype(f32)
                else:
                    local = leaf_cols(w - 2 if which == 0 else 17 - w)
                    vw[0:8, to] = vt[:, local]
                    vw[8:16, to] = rec_c[:, leaf_cols(w - 2 if which == 0 else 11 - w)]
                    pw[:, to] = pt[:, local].astype(f32)


def features(leaves, pw, fs, ft):
    for leaf in leaves:
        cols = leaf_cols(leaf)
        p = pw[0:3, cols]
        norm = p[0:1] * p[0:1] + p[1:2] * p[1:2] + p[2:3] * p[2:3]
        parts = jnp.concatenate(split3(norm), axis=0)
        one = jnp.ones((3, LEAF), f32)
        two = jnp.ones((2, LEAF), f32)
        pad = jnp.zeros((5, LEAF), f32)
        source = jnp.concatenate([p, parts, one, two, pad], axis=0)
        smooth = jnp.where(iota((2, LEAF), 0) == 0, SMOOTH_HI, SMOOTH_LO)
        target = jnp.concatenate([-2.0 * p, one, parts, smooth, pad], axis=0)
        fs[cols, :] = jnp.transpose(source).astype(bf16)
        ft[:, cols] = target.astype(bf16)


def near_target(t, vw, fs, ft, acc):
    tc = leaf_cols(t)
    total = jnp.zeros((16, LEAF), f32)
    for s in range(t - 2, t + 3):
        if 2 <= s < t:
            continue
        sc = leaf_cols(s)
        kernel = lax.rsqrt(dot(fs[sc, :], ft[:, tc])).astype(bf16)
        total = total + dot(vw[:, sc], kernel)
        if t < s < 10:
            acc[:, leaf_cols(s - 2)] += dot(vw[:, tc], kernel, NT)
    acc[:, leaf_cols(t - 2)] += total


SPLIT = 6


def near_first_kernel(
    vt_in, pt_in, c_in, begun, vt, pt, rec_c, vw, fs, ft, pw, acc, sems, out_sems
):
    for copy in fetch(sems, (vt_in, vt), (pt_in, pt), (c_in, rec_c)):
        copy.wait()
    load_window(vt, pt, rec_c, None, range(SPLIT, 12), vw, pw)
    features(range(SPLIT, 12), pw, fs, ft)
    acc[...] = jnp.zeros_like(acc)
    copies = []
    for t in range(SPLIT, 10):
        near_target(t, vw, fs, ft, acc)
        src, dst = acc.at[:, leaf_cols(t - 2)], begun.at[:, leaf_cols(t - SPLIT)]
        copies += [pltpu.make_async_copy(src, dst, out_sems.at[t - SPLIT])]
        copies[-1].start()
    for copy in copies:
        copy.wait()


def near_rest_kernel(
    vt_in, pt_in, c_in, halo_in, begun, mine, other,
    vt, pt, rec_c, vw, fs, ft, pw, acc, sems, halo,
):
    left = LEAF * (SPLIT - 2)
    copies = fetch(
        sems, (vt_in, vt), (pt_in, pt), (c_in, rec_c), (halo_in, halo),
        (begun, acc.at[:, left:]),
    )
    acc[:, :left] = jnp.zeros((16, left), f32)
    for copy in copies[:4]:
        copy.wait()
    core = lax.axis_index("vec")
    end = lax.axis_index("leaf") == (lax.axis_size("leaf") - 1) * core

    @pl.when(end)
    def _():
        halo[...] = jnp.zeros_like(halo)

    load_window(vt, pt, rec_c, halo, range(0, SPLIT + 2), vw, pw)
    features(range(0, SPLIT + 2), pw, fs, ft)
    copies[4].wait()
    for t in range(2, SPLIT):
        near_target(t, vw, fs, ft, acc)
    for which in range(2):

        @pl.when(core == which)
        def _():
            for i in range(8):
                to = leaf_cols(i if which == 0 else 7 - i)
                mine[:, to] = acc[0:8, leaf_cols(i)] * (8.0 / LEAF)
                other[:, to] = acc[8:16, leaf_cols(i)] * (8.0 / LEAF)


LEVEL_START = [256 - (256 >> u) for u in range(7)]
UPPER = 224
OWN = 30
SIBLING = 33
OWN_UPPER = 36
T_ROWS = 40
C_ROWS = 8


def node(u, other=False):
    n = lax.shift_right_logical(lax.axis_index("leaf"), u)
    return LEVEL_START[u] + (lax.bitwise_xor(n, 1) if other else n)


def pick_matrices(table, want, rows, count, mats, buf):
    pick = hot(iota((rows, 254), 1) == want)

    def step(g, carry):
        out = dot(pick, table[pl.ds(4 * g, 4)].reshape(256, 254), NT)
        for j in range(4):
            at = pl.multiple_of((4 * g + j) * rows, 8)
            buf[pl.ds(at, rows), :64] = out[:, 64 * j : 64 * j + 64]
        return carry

    lax.fori_loop(0, 16, step, 0, unroll=4)
    for m in range(count):
        mats[64 * m : 64 * m + 64, :] = buf[pl.ds(m, 64, stride=rows), :][:, :64].astype(bf16)


def transfers_wanted():
    row = iota((T_ROWS, 254), 0)
    want = jnp.where(row < 30, row + UPPER, -1)
    for u in range(3):
        want = jnp.where(row == OWN + u, node(u), want)
        want = jnp.where(row == SIBLING + u, node(u, True), want)
        want = jnp.where(row == OWN_UPPER + u, node(u + 3), want)
    return hot(iota((T_ROWS, 254), 1) == want)


def couplings_kernel(uc, seen, mats, buf):
    row = iota((C_ROWS, 254), 0)
    want = jnp.zeros((C_ROWS, 254), i32) - 1
    for u in range(7):
        want = jnp.where(row == u, node(u, u < 3), want)
    pick_matrices(uc, want, C_ROWS, 7, mats, buf)


def middle_kernel(
    recv_in, path_in, mats_in, coup_in, send, recv, path, mats, coup, xs, gain, sems
):
    device = lax.axis_index("leaf")
    copies = fetch(sems, (recv_in, recv), (mats_in, mats), (coup_in, coup), (path_in, path))
    for copy in copies:
        copy.wait()
    ext = recv[:, 2048:2176].astype(f32)

    turned = jnp.transpose(ext)
    row, lane = iota((64, 128), 0), iota((64, 128), 1)
    wanted = ((row & 31) + 1).astype(f32)
    fits = lax.shift_right_logical(row, 5) == (lax.shift_right_logical(lane, 2) & 1)
    sums = []
    for g in range(4):
        label = turned[64 + 16 * g : 65 + 16 * g, :]
        picked = dot(hot((label == wanted) & fits), recv[:, 512 * g : 512 * g + 512])
        sums += [picked[:32], picked[32:]]

    xs[0:128, :] = ext[:, :64]
    first, n = 0, 16
    firsts = {3: 0}
    for u in range(3, 6):
        for m in range(n // 2):
            r = 8 * (first + 2 * m)
            e = LEVEL_START[u] - UPPER + 2 * m
            pair = jnp.concatenate([xs[r : r + 8, :], xs[r + 8 : r + 16, :]], axis=1)
            w = own_matrix(mats, e, 2)
            t = 8 * (first + n + m)
            xs[t : t + 8, :] = dot_pair(pair, w)
        first += n
        n //= 2
        firsts[u + 1] = first
    for u in range(7):
        if u < 3:
            partner = path[8 * u : 8 * u + 8, :]
        else:
            sib = lax.bitwise_xor(lax.shift_right_logical(device, u), 1)
            partner = xs[pl.ds(pl.multiple_of((firsts[u] + sib) * 8, 8), 8), :]
        gain[8 * u : 8 * u + 8, :] = dot_pair(partner, own_matrix(coup, u))
    down = gain[48:56, :]
    for u in (5, 4, 3):
        w = own_matrix(mats, OWN_UPPER + u - 3)
        down = dot_pair(down, w, NT) + gain[8 * u : 8 * u + 8, :]
    lines = {}
    for u in (2, 1, 0):
        both = jnp.concatenate(
            [own_matrix(mats, OWN + u), own_matrix(mats, SIBLING + u)], axis=0
        )
        spread = dot_pair(down, both, NT)
        lines[u] = flat(spread[:, 64:] + gain[8 * u : 8 * u + 8, :])
        down = spread[:, :64]
    own_line = flat(down)
    z = device & 7
    last = iota((32, 512), 0) == 31
    for peer in range(8):
        x = lax.bitwise_xor(z, peer)
        line = jnp.where(x == 0, own_line, lines[0])
        line = jnp.where(x >= 2, lines[1], line)
        line = jnp.where(x >= 4, lines[2], line)
        block = jnp.where(last, line, sums[peer])
        send[32 * peer : 32 * peer + 32, :] = block.astype(bf16)


def flat(x):
    return jnp.concatenate([x[v : v + 1] for v in range(8)], axis=1)


def final_kernel(
    recv_in, mine_in, other_in, mats_in, tr, bases, perm_in, out,
    recv, near_mine, near_other, mats, perm, cpl, dwn, dn, tree, sems,
):
    copies = fetch(
        sems,
        (recv_in, recv),
        (mats_in.at[64 * OWN : 64 * OWN + 128], mats),
        (mine_in, near_mine),
        (other_in, near_other),
        (perm_in, perm),
    )
    for copy in copies:
        copy.wait()
    device = lax.axis_index("leaf")
    core = lax.axis_index("vec")
    z = device & 7
    total = jnp.zeros((32, 512), f32)
    levels = [jnp.zeros((1, 512), f32)] * 3
    for peer in range(8):
        block = recv[32 * peer : 32 * peer + 32, :].astype(f32)
        total = total + block
        x = lax.bitwise_xor(z, peer)
        line = block[31:32]
        for i, use in enumerate((x >= 4, (x >= 2) & (x < 4), x < 2)):
            levels[i] = levels[i] + jnp.where(use, line, 0.0)
    levels = jnp.concatenate(levels + [jnp.zeros((5, 512), f32)], axis=0)
    for v in range(8):
        cpl[pl.ds(v, 32, stride=8), :] = wide(total[:, 64 * v : 64 * v + 64])
        dwn[pl.ds(v, 8, stride=8), :] = wide(levels[:, 64 * v : 64 * v + 64])
    down = dot_pair(dwn[0:8, :64], own_matrix(mats, 1), NT) + dwn[8:16, :64]
    down = dot_pair(down, own_matrix(mats, 0), NT) + dwn[16:24, :64]

    dn[240:248, :] = down + cpl[240:248, :64]
    n = 1
    while n < 16:
        off_parent = 32 - 2 * n
        n *= 2
        off = 32 - 2 * n
        for m in range(n // 2):
            r = 8 * (off_parent + m)
            w = tr[off + 2 * m : off + 2 * m + 2].reshape(128, 64)
            both = dot_pair(dn[r : r + 8, :], w, NT)
            t = 8 * (off + 2 * m)
            dn[t : t + 8, :] = both[:, :64] + cpl[t : t + 8, :64]
            dn[t + 8 : t + 16, :] = both[:, 64:] + cpl[t + 8 : t + 16, :64]
    for leaf in range(16):
        tree[:, LEAF * leaf : LEAF * leaf + LEAF] = dot(
            dn[8 * leaf : 8 * leaf + 8, :].astype(bf16), bases[leaf]
        )

    @pl.when(core == 0)
    def _():
        tree[:, :HALF] += near_mine[...]
        tree[:, HALF:] += near_other[...]

    @pl.when(core == 1)
    def _():
        tree[:, :HALF] += near_other[...]
        tree[:, HALF:] += near_mine[...]

    width = 512
    total = jnp.zeros((256, 256), f32)
    for b in range(COLS // width):
        cols = slice(b * width, (b + 1) * width)
        index = perm[:, cols]
        select = hot_rows(index & 255, width)
        high = jnp.broadcast_to(lax.shift_right_logical(index, 8), (8, width))
        values = tree[:, cols]
        spread = jnp.concatenate(
            [jnp.where(high == q, values, 0.0) for q in range(32)], axis=0
        ).astype(bf16)
        total = total + dot(spread, select, NT)
    for q in range(32):
        out[:, 256 * q : 256 * q + 256] = total[8 * q : 8 * q + 8].astype(bf16)


def shards(
    points, vectors, leaf_order, leaf_bases, transfers, coupling_blocks,
    block_source, block_owner, block_target, up_transfer, up_coupling,
):
    peers = lax.axis_size("leaf")
    axes = ("leaf", "vec")
    vt, pt, send_c = call(
        gather_kernel,
        [((8, COLS), bf16), ((8, COLS), bf16), ((8, LOCAL), bf16)],
        [
            pltpu.VMEM((3, COLS), bf16), pltpu.VMEM((8, COLS), bf16), pltpu.VMEM((1, COLS), i32),
            pltpu.VMEM((256, 256), bf16), pltpu.VMEM((128, 256), f32), pltpu.SemaphoreType.DMA((3,)),
        ],
        (points, vectors, leaf_order), "hhh>vvv",
        2 * 384 * 256 * COLS, 1 << 20,
    )
    pairs_c = []
    pairs_a = [(0, 2 * peers - 1), (2 * peers - 1, 0)]
    for d in range(peers):
        pairs_c += [(2 * d, 2 * d + 1), (2 * d + 1, 2 * d)]
        if d + 1 < peers:
            pairs_a += [(2 * d + 1, 2 * d + 2), (2 * d + 2, 2 * d + 1)]
    rec_c = lax.ppermute(send_c, axes, pairs_c)
    ut = jnp.transpose(up_transfer, (1, 2, 0))
    uc = jnp.transpose(up_coupling, (1, 2, 0))
    cf, path, mats, place = call(
        coeff_kernel,
        [((256, 128), f32), ((32, 64), f32), ((64 * T_ROWS, 64), bf16), ((1, 256), i32)],
        [pltpu.VMEM((64 * T_ROWS, 128), f32)],
        (vt, leaf_bases, transfers, ut, block_owner.reshape(1, -1)), "vvvvv>vvvv",
        2 * 4096 * 256 * 40, 5 << 20,
    )
    send, halo = call(
        product_kernel,
        [((128, 2176), bf16), ((24, HALO), bf16)],
        [pltpu.VMEM((1024, 128), f32), pltpu.VMEM((640, 256), bf16)],
        (
            cf, path, jnp.transpose(coupling_blocks, (1, 2, 0)),
            block_source.reshape(1, -1), place, block_target.reshape(1, -1), vt, pt, rec_c,
        ), "vvvvvvvvv>vv",
        2 * 512 * 256 * 640, 4 << 20,
    )
    halo = lax.ppermute(halo, axes, pairs_a)
    near_groups = [[xy * 8 + z for z in range(8)] for xy in range(peers // 8)]
    far_groups = [[xy * 8 + z for xy in range(peers // 8)] for z in range(8)]
    recv = lax.all_to_all(
        send, "leaf", split_axis=0, concat_axis=0, tiled=True, axis_index_groups=far_groups
    )
    buffers = [
        pltpu.VMEM((8, COLS), bf16), pltpu.VMEM((8, COLS), bf16), pltpu.VMEM((8, LOCAL), bf16),
        pltpu.VMEM((16, 6144), bf16), pltpu.VMEM((6144, 16), bf16), pltpu.VMEM((16, 6144), bf16),
        pltpu.VMEM((8, 6144), f32), pltpu.VMEM((16, HALF), f32), pltpu.SemaphoreType.DMA((6,)),
    ]
    (coup,) = call(
        couplings_kernel,
        [((64 * C_ROWS, 64), bf16)],
        [pltpu.VMEM((64 * C_ROWS, 128), f32)],
        (uc, send), "va>v",
        2 * 4096 * 256 * 8, 3 << 20,
    )
    (begun,) = call(
        near_first_kernel,
        [((16, LEAF * (10 - SPLIT)), f32)],
        buffers + [pltpu.SemaphoreType.DMA((10 - SPLIT,))],
        (vt, pt, rec_c), "aaa>h",
        2 * 37 * 512 * 512 * 256, 1 << 20, vmem=24,
    )
    (send,) = call(
        middle_kernel,
        [((256, 512), bf16)],
        [
            pltpu.VMEM((128, 2176), bf16), pltpu.VMEM((32, 64), f32),
            pltpu.VMEM((64 * T_ROWS, 64), bf16), pltpu.VMEM((64 * C_ROWS, 64), bf16),
            pltpu.VMEM((256, 64), f32), pltpu.VMEM((56, 64), f32), pltpu.SemaphoreType.DMA((4,)),
        ],
        (recv, path, mats, coup), "aaaa>v",
        2 * 256 * 512 * 512, 2 << 20,
    )
    recv = lax.all_to_all(
        send, "leaf", split_axis=0, concat_axis=0, tiled=True, axis_index_groups=near_groups
    )
    near_mine, near_send = call(
        near_rest_kernel,
        [((8, HALF), f32), ((8, HALF), f32)],
        buffers + [pltpu.VMEM((24, HALO), bf16)],
        (vt, pt, rec_c, halo, begun), "aaaah>vv",
        2 * 30 * 512 * 512 * 256, 1 << 20, vmem=24,
    )
    near_other = lax.ppermute(near_send, axes, pairs_c)
    (out,) = call(
        final_kernel,
        [((8, COLS), bf16)],
        [
            pltpu.VMEM((256, 512), bf16), pltpu.VMEM((8, HALF), f32), pltpu.VMEM((8, HALF), f32),
            pltpu.VMEM((128, 64), bf16), pltpu.VMEM((1, COLS), i32),
            pltpu.VMEM((256, 128), f32), pltpu.VMEM((64, 128), f32),
            pltpu.VMEM((248, 64), f32), pltpu.VMEM((8, COLS), f32), pltpu.SemaphoreType.DMA((5,)),
        ],
        (recv, near_mine, near_other, mats, transfers, leaf_bases, leaf_order), "aaaavvh>v",
        2 * 256 * 256 * COLS, 8 << 20,
    )
    return out


def solution(mesh):
    return jax.shard_map(
        shards,
        mesh=mesh,
        in_specs=(
            P(None, "leaf"),
            P("vec", "leaf"),
            P("leaf", None),
            P("leaf", None, None),
            P("leaf", None, None),
            P("leaf", None, None),
            P("leaf"),
            P("leaf", None),
            P("leaf"),
            P(),
            P(),
        ),
        out_specs=P("vec", "leaf"),
        check_vma=False,
    )
```
